32 devices in a mesh: box: 2 (over core), row: 16 (over z, y, x).
Axes of the slice: x: 2, y: 2, z: 4, core: 2. Of those that a mesh axis runs over, the one named last changes fastest.
Arguments:
- dtn: float32 [4, 6, 384, 2304], P('box', None, 'row'), may hold values from -2 to 8, as said below
- interface_perm: int32 [2, 384], P('box'), may hold values from 0 to 383, each once within a row
Outputs:
- solution_first: float32 [2, 384, 3840], P('box', 'row')
- solution_second: float32 [2, 384, 6144], P('box', 'row')
- merged_map: float32 [2, 8, 384, 6144], P('box', None, 'row')
The draws below stay inside these ranges and needn't reach their ends.
Inputs may be any that keep to these rules, and one draw needn't show every extreme that they name: `dtn`: each box's map, read as a (2304) x (2304) matrix, is symmetric and positive definite.
All inputs are finite; a program needn't handle non-finite values.
Results may differ from the reference program's by a relative error of at most 0.00012.
Values sent between devices are 32-bit elements; how exact they have to be, the bound alone decides.
A program may use at most 192 MiB of HBM per device.

```python
import jax
import jax.numpy as jnp
from jax import lax

F = 384
NBOX = 4
NPAIR = 2


def one_map(key):
    order = 6 * F
    key_noise, key_scale = jax.random.split(key, 2)
    base_noise = jax.random.normal(key_noise, (order, order), jnp.float32)
    row_scale = 1.0 + 0.0 * jax.random.uniform(key_scale, (order,), jnp.float32)
    gram_matrix = jnp.dot(base_noise, base_noise.T, precision=lax.Precision.HIGHEST) / order
    gram_matrix = (gram_matrix + gram_matrix.T) * 0.5
    shifted = gram_matrix + 0.1 * jnp.eye(order, dtype=jnp.float32)
    scaled = row_scale[:, None] * shifted * row_scale[None, :]
    return scaled.reshape(6, F, order)


def draw_dtn(key, part):
    keys = jax.random.split(jax.random.fold_in(key, 11), NBOX)
    return jax.lax.map(one_map, keys)


def setup_inputs(seed: int = 0) -> dict:
    seeds = jax.random.split(jax.random.key(seed), 3)
    return {
        "dtn": draw_dtn(jax.random.fold_in(seeds[2], 71), 0),
        "interface_perm": jax.vmap(lambda own: jax.random.permutation(own, F))(jax.random.split(seeds[1], NPAIR)).reshape((NPAIR, F)).astype(jnp.int32),
    }


def face_index(faces, width):
    return jnp.concatenate([jnp.arange(width, dtype=jnp.int32) + f * width for f in faces])

def pick(matrix, rows, cols):
    return jnp.take(jnp.take(matrix, rows, axis=0), cols, axis=1)

def merge(left, right, left_s, left_o, right_s, right_o):
    couple = pick(left, left_s, left_s) + pick(right, right_s, right_s)
    coupled = jnp.concatenate([pick(left, left_s, left_o), pick(right, right_s, right_o)], axis=1)
    factor = jnp.linalg.cholesky(couple)
    solution = -jax.scipy.linalg.cho_solve((factor, True), coupled)
    n_left = left_o.shape[0]
    n_right = right_o.shape[0]
    top = jnp.concatenate([pick(left, left_o, left_o), jnp.zeros((n_left, n_right), jnp.float32)], axis=1)
    bottom = jnp.concatenate([jnp.zeros((n_right, n_left), jnp.float32), pick(right, right_o, right_o)], axis=1)
    lift = jnp.concatenate([pick(left, left_o, left_s), pick(right, right_o, right_s)], axis=0)
    merged = jnp.concatenate([top, bottom], axis=0) + jnp.dot(lift, solution, precision=lax.Precision.HIGHEST)
    return (solution, merged)

def reference(dtn, interface_perm):
    size = 6 * F
    firsts = []
    merged_one = []
    for p in range(NPAIR):
        first = dtn[2 * p].reshape(size, size)
        second = dtn[2 * p + 1].reshape(size, size)
        order = jnp.concatenate([interface_perm[p].astype(jnp.int32), jnp.arange(F, size, dtype=jnp.int32)])
        second = pick(second, order, order)
        solution, merged = merge(first, second, face_index([1], F), face_index([0, 2, 3, 4, 5], F), face_index([0], F), face_index([1, 2, 3, 4, 5], F))
        firsts.append(solution)
        merged_one.append(merged)
    seconds = []
    maps = []
    for c in range(NPAIR // 2):
        solution, merged = merge(merged_one[2 * c], merged_one[2 * c + 1], face_index([2, 7], F), face_index([0, 1, 3, 4, 5, 6, 8, 9], F), face_index([1, 6], F), face_index([0, 2, 3, 4, 5, 7, 8, 9], F))
        for h in range(2):
            seconds.append(solution[h * F:(h + 1) * F])
            maps.append(merged[h * 8 * F:(h + 1) * 8 * F].reshape(8, F, 16 * F))
    return (jnp.stack(firsts), jnp.stack(seconds), jnp.stack(maps))
```

```python
import functools

import jax
import jax.numpy as jnp
from jax import lax
from jax.experimental import pallas as pl
from jax.experimental.pallas import tpu as pltpu
from jax.sharding import PartitionSpec as P

HIGHEST = lax.Precision.HIGHEST
HIGH = lax.Precision.HIGH
BLOCK = 128
GROUP = 4
MESH = pl.DeviceIdType.MESH


def dot(left, right, precision=HIGHEST):
    return jnp.dot(left, right, precision=precision, preferred_element_type=jnp.float32)


def dot_t(left, right):
    return lax.dot_general(
        left, right, (((0,), (0,)), ((), ())), precision=HIGHEST, preferred_element_type=jnp.float32
    )


def invert_step(blk, lane, g, carry):
    size = blk.shape[0]
    k = g * GROUP
    full = blk[...]
    cols = [
        jnp.take_along_axis(full, jnp.full((size, size), k + i, jnp.int32), axis=1)
        for i in range(GROUP)
    ]
    rows = [blk[pl.ds(k + i, 1), :] for i in range(GROUP)]
    wide = [jnp.broadcast_to(r, (8, size)) for r in rows]
    pivots = [
        [
            jnp.take_along_axis(wide[i], jnp.full((8, size), k + j, jnp.int32), axis=1)
            for j in range(GROUP)
        ]
        for i in range(GROUP)
    ]
    inside = (lane >= k) & (lane < k + GROUP)
    wide = [
        jnp.where(lane == k + i, 1.0, jnp.where(inside, 0.0, wide[i])) for i in range(GROUP)
    ]
    for i in range(GROUP):
        p = 1.0 / pivots[i][i]
        wide[i] = wide[i] * p
        for j in range(i + 1, GROUP):
            pivots[i][j] = pivots[i][j] * p
        for l in range(GROUP):
            if l != i:
                f = pivots[l][i]
                wide[l] = wide[l] - f * wide[i]
                for j in range(i + 1, GROUP):
                    pivots[l][j] = pivots[l][j] - f * pivots[i][j]
    result = jnp.where(inside, 0.0, full)
    for i in range(GROUP):
        result = result - cols[i] * wide[i][0:1]
    blk[...] = result
    for i in range(GROUP):
        blk[pl.ds(k + i, 1), :] = wide[i][0:1]
    return carry


def invert_block(blk):
    size = blk.shape[0]
    lane = lax.broadcasted_iota(jnp.int32, (1, size), 1)
    lax.fori_loop(0, size // GROUP, functools.partial(invert_step, blk, lane), 0)


def invert(mat, blk, col):
    order = mat.shape[0]
    count = order // BLOCK
    eye = (
        lax.broadcasted_iota(jnp.int32, (BLOCK, BLOCK), 0)
        == lax.broadcasted_iota(jnp.int32, (BLOCK, BLOCK), 1)
    ).astype(jnp.float32)

    def outer(j, carry):
        here = pl.ds(pl.multiple_of(j * BLOCK, BLOCK), BLOCK)
        blk[...] = mat[here, here]
        invert_block(blk)
        col[...] = mat[:, here]
        mat[:, here] = jnp.zeros((order, BLOCK), jnp.float32)
        mat[here, here] = eye
        col[here, :] = jnp.zeros((BLOCK, BLOCK), jnp.float32)
        mat[here, :] = dot(blk[...], mat[here, :])

        def inner(i, c):
            there = pl.ds(pl.multiple_of(i * BLOCK, BLOCK), BLOCK)
            mat[there, :] = mat[there, :] - dot(col[there, :], mat[here, :])
            return c

        @pl.loop(0, count)
        def _(i):
            @pl.when(i != j)
            def _():
                inner(i, 0)

        return carry

    lax.fori_loop(0, count, outer, 0)


def first_kernel(perm_ref, small_ref, inv_ref, coupled_ref, own_ref, mat, blk, col):
    f = mat.shape[0]
    count = f // BLOCK

    def block(ref, i):
        return ref[:, i * f : (i + 1) * f]

    def place(rows):
        return (
            perm_ref[rows, :] == lax.broadcasted_iota(jnp.int32, (BLOCK, f), 1)
        ).astype(jnp.float32)

    whole = (perm_ref[...] == lax.broadcasted_iota(jnp.int32, (f, f), 1)).astype(jnp.float32)

    @pl.loop(0, count)
    def _(i):
        here = pl.ds(pl.multiple_of(i * BLOCK, BLOCK), BLOCK)
        moved = dot(place(here), block(small_ref, 1))
        mat[here, :] = small_ref[here, :f] + lax.dot_general(
            moved,
            whole,
            (((1,), (1,)), ((), ())),
            precision=HIGHEST,
            preferred_element_type=jnp.float32,
        )

    invert(mat, blk, col)

    @pl.loop(0, count)
    def _(i):
        here = pl.ds(pl.multiple_of(i * BLOCK, BLOCK), BLOCK)
        inv_ref[here, :f] = mat[here, :]
        inv_ref[here, f:] = dot(mat[here, :], whole)

    @pl.loop(0, count)
    def _(i):
        there = pl.ds(pl.multiple_of(f + i * BLOCK, BLOCK), BLOCK)
        picked = (
            perm_ref[...] == lax.broadcasted_iota(jnp.int32, (f, BLOCK), 1) + i * BLOCK
        ).astype(jnp.float32)
        inv_ref[there, :] = dot_t(picked, inv_ref[:f, :])

    for h in range(2):

        @pl.loop(0, count)
        def _(i):
            here = pl.ds(pl.multiple_of(i * BLOCK, BLOCK), BLOCK)
            rows = pl.ds(pl.multiple_of(h * f + i * BLOCK, BLOCK), BLOCK)
            edge = small_ref[:, pl.ds(pl.multiple_of((2 + h) * f + i * BLOCK, BLOCK), BLOCK)]
            coupled_ref[rows, :] = -dot_t(edge, inv_ref[h * f : (h + 1) * f, :])
            for c in range(2):
                value = dot(coupled_ref[rows, c * f : (c + 1) * f], block(small_ref, 2 + c))
                if c == h:
                    value = value + small_ref[here, (4 + h) * f : (5 + h) * f]
                own_ref[rows, c * f : (c + 1) * f] = value


def second_kernel(own_ref, part_ref, lift_ref, pick_ref, out_ref, mat, blk, col):
    mat[...] = own_ref[...] + part_ref[...]
    invert(mat, blk, col)
    n = lift_ref.shape[0]
    out_ref[:n, :] = dot(lift_ref[...], mat[...])
    out_ref[n:, :] = dot(pick_ref[...], mat[...])


def flip(index, bit):
    return index + bit - 2 * bit * ((index // bit) % 2)


def plan(n, width):
    bits = []
    bit = n // 2
    while bit:
        bits.append(bit)
        bit //= 2
    tiles = width // 128
    first = tiles * 3 // 8
    second = tiles * 3 // 8 + (tiles * 3 % 8 >= 4)
    orders = [bits, bits[:-2] + [1, 2], [1, 2] + bits[:-2]]
    sizes = [first, second, tiles - first - second]
    chunks, at = [], 0
    for order, size in zip(orders, sizes):
        chunks.append((at * 128, size * 128, order))
        at += size
    return bits, chunks


def gather_kernel(n, bits, chunks, x_ref, out_ref, send_sem, recv_sem, own_sem):
    me = lax.axis_index("row")
    barrier = pltpu.get_barrier_semaphore()
    for bit in bits:
        pl.semaphore_signal(
            barrier, inc=1, device_id={"row": flip(me, bit)}, device_id_type=pl.DeviceIdType.MESH
        )
    local = pltpu.make_async_copy(x_ref, out_ref.at[me], own_sem)
    local.start()
    local.wait()
    pl.semaphore_wait(barrier, len(bits))
    pending = [[] for _ in chunks]
    sent = []
    held = [[()] for _ in chunks]
    for t in range(len(bits)):
        for c, (start, size, order) in enumerate(chunks):
            for copy in pending[c]:
                copy.wait_recv()
            pending[c] = []
            bit = order[t]
            for s in held[c]:
                slot = me
                for one in s:
                    slot = flip(slot, one)
                number = (1 << t) - 1 + len(pending[c])
                piece = out_ref.at[slot, :, pl.ds(start, size)]
                copy = pltpu.make_async_remote_copy(
                    src_ref=piece,
                    dst_ref=piece,
                    send_sem=send_sem.at[c, number],
                    recv_sem=recv_sem.at[c, number],
                    device_id={"row": flip(me, bit)},
                    device_id_type=pl.DeviceIdType.MESH,
                )
                copy.start()
                pending[c].append(copy)
                sent.append(copy)
            held[c] = held[c] + [s + (bit,) for s in held[c]]
    for c in range(len(chunks)):
        for copy in pending[c]:
            copy.wait_recv()
    for copy in sent:
        copy.wait_send()


def quick_gather(x):
    n = lax.axis_size("row")
    count, width = x.shape
    bits, chunks = plan(n, width)
    out = pl.pallas_call(
        functools.partial(gather_kernel, n, bits, chunks),
        out_shape=jax.ShapeDtypeStruct((n, count, width), jnp.float32),
        in_specs=[pl.BlockSpec(memory_space=pltpu.VMEM)],
        out_specs=pl.BlockSpec(memory_space=pltpu.VMEM),
        scratch_shapes=[
            pltpu.SemaphoreType.DMA((len(chunks), n - 1)),
            pltpu.SemaphoreType.DMA((len(chunks), n - 1)),
            pltpu.SemaphoreType.DMA,
        ],
        compiler_params=pltpu.CompilerParams(
            collective_id=0, has_side_effects=True, vmem_limit_bytes=16 * 1024 * 1024
        ),
        cost_estimate=pl.CostEstimate(
            flops=10_000_000_000, bytes_accessed=2 * n * count * width * 4, transcendentals=0
        ),
    )(x)
    return out.reshape(n * count, width)


def call(kernel, out, order, *args):
    return pl.pallas_call(
        kernel,
        out_shape=[jax.ShapeDtypeStruct(o, jnp.float32) for o in out],
        in_specs=[pl.BlockSpec(memory_space=pltpu.VMEM)] * len(args),
        out_specs=[pl.BlockSpec(memory_space=pltpu.VMEM)] * len(out),
        scratch_shapes=[
            pltpu.VMEM((order, order), jnp.float32),
            pltpu.VMEM((BLOCK, BLOCK), jnp.float32),
            pltpu.VMEM((order, BLOCK), jnp.float32),
        ],
        compiler_params=pltpu.CompilerParams(vmem_limit_bytes=40 * 1024 * 1024),
        cost_estimate=pl.CostEstimate(
            flops=order * 20_000_000, bytes_accessed=order * order * 8, transcendentals=0
        ),
    )(*args)


def plain_body(dtn, interface_perm):
    a, b = dtn[0], dtn[1]
    count = a.shape[1]
    f = a.shape[2] // 6
    perm = interface_perm[0]
    rank = lax.axis_index("row")
    half = lax.axis_index("box") % 2
    first = half == 0

    def swap(x):
        n = lax.axis_size("box")
        return lax.ppermute(x, "box", [(i, i ^ 1) for i in range(n)])

    def gather(x):
        return lax.all_gather(x, "row", axis=0, tiled=True)

    def cols(x, face):
        return x[..., face * f : (face + 1) * f]

    def side(x):
        return jnp.where(first, cols(x, 3), cols(x, 2))

    def free(x):
        return jnp.where(first, cols(x, 2), cols(x, 3))

    def outer_cols(x, edge):
        return jnp.concatenate([cols(x, edge), free(x), cols(x, 4), cols(x, 5)], axis=-1)

    ay, by = jnp.where(first, a[3], a[2]), jnp.where(first, b[3], b[2])
    a1, b0 = a[1], b[0]
    small = quick_gather(
        jnp.concatenate(
            [cols(a1, 1), cols(b0, 0), side(a1), side(b0), side(ay), side(by)], axis=1
        )
    )
    bulk = gather(
        jnp.concatenate(
            [outer_cols(a1, 0), outer_cols(ay, 0), outer_cols(b0, 1), outer_cols(by, 1)], axis=1
        )
    )
    inv1, coupled, own_ss = call(first_kernel, [(2 * f, 2 * f)] * 3, f, perm[:, None], small)
    a1y, b0y = small[:, 2 * f : 3 * f], small[:, 3 * f : 4 * f]

    def times_side(x):
        return jnp.concatenate([dot(x[:, :f], a1y), dot(x[:, f:], b0y)], axis=1)

    part_ss = swap(own_ss)
    outer_a = jnp.concatenate(
        [a[0], jnp.where(first, a[2], a[3]), a[4], a[5]], axis=0
    )
    outer_b = jnp.concatenate(
        [b[1], jnp.where(first, b[2], b[3]), b[4], b[5]], axis=0
    )
    lift = -jnp.concatenate(
        [dot(cols(outer_a, 1), inv1[:f]), dot(cols(outer_b, 0), inv1[f:])], axis=0
    )
    n = 4 * count
    zero_n = jnp.zeros((n, f), jnp.float32)
    lift_two = times_side(lift) + jnp.concatenate(
        [
            jnp.concatenate([side(outer_a), zero_n], axis=1),
            jnp.concatenate([zero_n, side(outer_b)], axis=1),
        ],
        axis=0,
    )
    start = rank * count
    pick = (
        jnp.arange(2 * f, dtype=jnp.int32)[None, :]
        == half * f + start + jnp.arange(count, dtype=jnp.int32)[:, None]
    ).astype(jnp.float32)
    own_rows = lax.dynamic_slice(inv1, (start, 0), (count, 2 * f))
    z = -call(second_kernel, [(2 * n + count, 2 * f)], 2 * f, own_ss, part_ss, lift_two, pick)[0]
    z_part = swap(z)
    both = jnp.concatenate([z_part, z], axis=0)
    through = dot(both, coupled)
    m = 2 * n + count
    through = jnp.concatenate(
        [through[:m], through[m : m + 2 * n] + lift, through[m + 2 * n :], -own_rows], axis=0
    )
    both = jnp.concatenate([both, jnp.zeros((count, 2 * f), jnp.float32)], axis=0)
    w = 4 * f
    res_a = dot(through[:, :f], bulk[:, :w], HIGH) + dot(both[:, :f], bulk[:, w : 2 * w], HIGH)
    res_b = dot(through[:, f:], bulk[:, 2 * w : 3 * w], HIGH) + dot(both[:, f:], bulk[:, 3 * w :], HIGH)
    results = jnp.concatenate([res_a, res_b], axis=1)
    cross = swap(results[:m])
    own = results[m : 2 * m]
    base = jnp.concatenate(
        [
            jnp.concatenate([outer_cols(outer_a, 0), jnp.zeros((n, w), jnp.float32)], axis=1),
            jnp.concatenate([jnp.zeros((n, w), jnp.float32), outer_cols(outer_b, 1)], axis=1),
        ],
        axis=0,
    )
    own_map = own[: 2 * n] + base
    left = jnp.where(first, own_map, cross[: 2 * n])
    right = jnp.where(first, cross[: 2 * n], own_map)
    merged_map = jnp.concatenate([left, right], axis=1).reshape(1, 8, count, 4 * w)
    own_s, cross_s = own[2 * n :], cross[2 * n :]
    second = jnp.concatenate(
        [jnp.where(first, own_s, cross_s), jnp.where(first, cross_s, own_s)], axis=1
    )
    s1 = results[2 * m :]
    y_a, y_b = -dot(own_rows[:, :f], a1y), -dot(own_rows[:, f:], b0y)

    def ordered(x, y):
        two = jnp.where(first, cols(x, 1), y)
        three = jnp.where(first, y, cols(x, 1))
        return [cols(x, 0), two, three, x[:, 2 * f :]]

    solution_first = jnp.concatenate(ordered(s1[:, :w], y_a) + ordered(s1[:, w:], y_b), axis=1)
    return (solution_first[None], second[None], merged_map)


def split3(x):
    high = x.astype(jnp.bfloat16)
    rest = x - high.astype(jnp.float32)
    mid = rest.astype(jnp.bfloat16)
    low = (rest - mid.astype(jnp.float32)).astype(jnp.bfloat16)
    return high, mid, low


def dims(left, right):
    return (((left,), (right,)), ((), ()))


def bdot(left, right, dn):
    return lax.dot_general(left, right, dn, preferred_element_type=jnp.float32)


def pick_left(onehot, x, contract=1):
    return sum(bdot(onehot, part, dims(contract, 0)) for part in split3(x))


def pick_right(x, onehot, contract=0):
    return sum(bdot(part, onehot, dims(1, contract)) for part in split3(x))


def xdot(left, right, dn):
    return lax.dot_general(left, right, dn, precision=HIGHEST, preferred_element_type=jnp.float32)


def split2(x):
    high = x.astype(jnp.bfloat16)
    low = (x - high.astype(jnp.float32)).astype(jnp.bfloat16)
    return high, low


def dot3(left, right, dn):
    a, b = left
    c, d = right
    return bdot(a, c, dn) + (bdot(a, d, dn) + bdot(b, c, dn))


NN = dims(1, 0)
NT = dims(1, 1)
TN = dims(0, 0)


def invert_small(mat, blk, col, tick):
    order = mat.shape[0]
    count = order // BLOCK
    eye = (
        lax.broadcasted_iota(jnp.int32, (BLOCK, BLOCK), 0)
        == lax.broadcasted_iota(jnp.int32, (BLOCK, BLOCK), 1)
    ).astype(jnp.float32)
    for j in range(count):
        here = pl.ds(j * BLOCK, BLOCK)
        blk[...] = mat[here, here]
        invert_steps(blk, tick)
        col[...] = mat[:, here]
        mat[:, here] = jnp.zeros((order, BLOCK), jnp.float32)
        mat[here, here] = eye
        mat[here, :] = xdot(blk[...], mat[here, :], NN)
        for i in range(count):
            if i != j:
                there = pl.ds(i * BLOCK, BLOCK)
                mat[there, :] = mat[there, :] - xdot(col[there, :], mat[here, :], NN)
        tick()


def invert_steps(blk, tick, parts=2):
    size = blk.shape[0]
    lane = lax.broadcasted_iota(jnp.int32, (1, size), 1)
    total = size // GROUP
    for part in range(parts):
        lax.fori_loop(
            part * total // parts,
            (part + 1) * total // parts,
            functools.partial(invert_step, blk, lane),
            0,
        )
        if part + 1 < parts:
            tick()


class Gather:
    def __init__(self, ref, lead, block, cols, order, me, n, sends, recvs):
        self.ref, self.lead, self.block, self.cols, self.order = ref, lead, block, cols, order
        self.me, self.n, self.sends, self.recvs = me, n, sends, recvs

    def view(self, stage, arrived):
        m = self.n.bit_length() - 1
        index = []
        for b in range(m - 1, -1, -1):
            bit = 1 << b
            own = (self.me // bit) % 2
            if bit in self.order[:stage]:
                index.append(slice(None))
            elif arrived and bit == self.order[stage]:
                index.append(1 - own)
            else:
                index.append(own)
        blocks = pl.ds(self.block[0], self.block[1] - self.block[0])
        cols = pl.ds(self.cols[0], self.cols[1] - self.cols[0])
        return self.ref.at[(*self.lead, blocks, *index, slice(None), cols)]

    def copy(self, stage):
        piece = self.view(stage, False)
        return pltpu.make_async_remote_copy(
            src_ref=piece,
            dst_ref=piece,
            send_sem=self.sends.at[stage],
            recv_sem=self.recvs.at[stage],
            device_id={"row": flip(self.me, self.order[stage])},
            device_id_type=MESH,
        )


def merge_kernel(
    plan, perm_ref, dtn_ref, z_ref, lift_ref, own_ref, y_ref, gx_ref, bulk_ref,
    small, mat1, mat2, mat3, tee, blk, col, edge, ss, part, rhs, hold,
    fill_sem, send0, recv0, send1, recv1, send2, recv2, core_send, core_recv, swap_send, swap_recv,
):
    n, f, count = plan["n"], plan["f"], plan["count"]
    bits = plan["bits"]
    me = lax.axis_index("row")
    pair = lax.axis_index("box")
    half = lax.rem(pair, 2)
    other = pair + 1 - 2 * half
    yface, free = 3 - half, 2 + half
    spot = [(me // bit) % 2 for bit in bits]

    def at(face):
        return pl.ds(face * f, f) if isinstance(face, int) else pl.ds(pl.multiple_of(face * f, BLOCK), f)

    narrow = [(0, 1, 1), (1, 0, 0), (0, 1, yface), (1, 0, yface), (0, yface, yface), (1, yface, yface)]
    outer = [(0, free, 4, 5), (1, free, 4, 5)]
    wide = [(h, 1 - h, c) for h in range(2) for c in outer[h]]
    wide += [(h, yface, c) for h in range(2) for c in outer[h]]
    fills = []
    for b, (h, r, c) in enumerate(narrow):
        fills.append(
            pltpu.make_async_copy(dtn_ref.at[h, r, :, at(c)], small.at[(b, *spot)], fill_sem.at[b])
        )
    for b, (h, r, c) in enumerate(wide):
        fills.append(
            pltpu.make_async_copy(
                dtn_ref.at[h, r, :, at(c)], bulk_ref.at[(0, b, *spot)], fill_sem.at[len(narrow) + b]
            )
        )
    for one in fills:
        one.start()

    barrier = pltpu.get_barrier_semaphore()
    for bit in bits:
        pl.semaphore_signal(barrier, inc=1, device_id={"row": flip(me, bit)}, device_id_type=MESH)
    pl.semaphore_signal(barrier, inc=1, device_id={"box": other}, device_id_type=MESH)
    pl.semaphore_wait(barrier, len(bits) + 1)

    def gathers(ref, lead, chunks, sends, recvs):
        return [
            Gather(ref, lead, block, cols, order, me, n, sends.at[i], recvs.at[i])
            for i, (block, cols, order) in enumerate(chunks)
        ]

    first = gathers(small, (), plan["first"], send0, recv0)
    rest = gathers(small, (), plan["rest"], send1, recv1)
    bulk = gathers(bulk_ref, (0,), plan["bulk"], send2, recv2)
    last = len(bits)

    def cross(i, stage):
        g = bulk[i]
        view = g.view(0, False) if stage < 0 else g.view(stage, True)
        there = Gather(bulk_ref, (1,), g.block, g.cols, g.order, me, n, None, None)
        target = there.view(0, False) if stage < 0 else there.view(stage, True)
        return pltpu.make_async_remote_copy(
            src_ref=view,
            dst_ref=target,
            send_sem=core_send.at[i, stage + 1],
            recv_sem=core_recv.at[i, stage + 1],
            device_id={"box": other},
            device_id_type=MESH,
        )

    def advance(group, i, stage):
        g = group[i]
        if stage > 0:
            g.copy(stage - 1).wait_recv()
        if stage < last:
            g.copy(stage).start()
        if group is bulk:
            cross(i, stage - 1).start()

    events = list(plan["events"])

    def tick():
        if events:
            for name, i, stage in events.pop(0):
                advance({"first": first, "rest": rest, "bulk": bulk}[name], i, stage)

    for one in fills[: len(narrow)]:
        one.wait()
    for stage in range(last + 1):
        for i in range(len(first)):
            advance(first, i, stage)
        if stage == last - 1:
            for i in range(len(rest)):
                advance(rest, i, 0)
    for one in fills[len(narrow) :]:
        one.wait()

    def block(b):
        return small[b].reshape(f, f)

    count_f = f // BLOCK
    whole = (perm_ref[...] == lax.broadcasted_iota(jnp.int32, (f, f), 1)).astype(jnp.bfloat16)
    hold[...] = pick_left(whole, block(1))
    mat1[...] = block(0) + pick_right(hold[...], whole, 1)
    tick()
    invert_small(mat1, blk, col, tick)

    edge[:, :f] = block(2)
    edge[:, f:] = pick_left(whole, block(3))

    def rows_of(i):
        return pl.ds(pl.multiple_of(i * BLOCK, BLOCK), BLOCK)

    @pl.loop(0, count_f)
    def _(i):
        gx_ref[0, 0, rows_of(i), :] = xdot(mat1[rows_of(i), :], edge[...], NN)

    tick()

    def swap(b):
        return pltpu.make_async_remote_copy(
            src_ref=ss.at[b],
            dst_ref=part.at[b],
            send_sem=swap_send.at[b],
            recv_sem=swap_recv.at[b],
            device_id={"box": other},
            device_id_type=MESH,
        )

    for b, (i, j, y) in enumerate([(0, 0, 4), (0, 1, None), (1, 1, 5)]):

        @pl.loop(0, count_f)
        def _(k):
            left = edge[:, pl.ds(pl.multiple_of(i * f + k * BLOCK, BLOCK), BLOCK)]
            value = -xdot(left, gx_ref[0, 0, :, j * f : (j + 1) * f], TN)
            ss[b, rows_of(k), :] = value

        if y is not None:
            ss[b] = ss[b] + block(y)
        if b > 0:
            swap(b - 1).start()
    tick()

    outers = []
    for h in range(2):
        outers.append(
            jnp.concatenate([dtn_ref[h, r, :, pl.ds((1 - h) * f, f)] for r in outer[h]], axis=0)
        )
    swap(2).start()
    m = 4 * count
    joined = jnp.concatenate([outers[0], pick_right(outers[1], whole, 1)], axis=0)
    value = -xdot(joined, mat1[...], NN)
    lift_ref[:, :f] = value
    lift_ref[:, f:] = pick_right(value, whole)
    own_at = pl.ds(pl.multiple_of(me * count, 8), count)
    mine = mat1[own_at, :]
    own_ref[:, :f] = -mine
    own_ref[:, f:] = -pick_right(mine, whole)
    y_ref[...] = -gx_ref[0, 0, own_at, :]
    rhs[: 2 * m, :] = -xdot(joined, gx_ref[0, 0], NN)
    for h in range(2):
        side = jnp.concatenate([dtn_ref[h, r, :, at(yface)] for r in outer[h]], axis=0)
        rhs[h * m : (h + 1) * m, h * f : (h + 1) * f] += side
    rhs[2 * m :, :] = (
        lax.broadcasted_iota(jnp.int32, (count, 2 * f), 1)
        == half * f + me * count + lax.broadcasted_iota(jnp.int32, (count, 2 * f), 0)
    ).astype(jnp.float32)

    @pl.loop(0, count_f)
    def _(i):
        picked = whole_cols(perm_ref, i, f)
        gx_ref[0, 1, rows_of(i), :] = pick_left(picked, gx_ref[0, 0], 0)

    tick()
    swap(0).wait_recv()
    mat2[...] = ss[0] + part[0]
    invert_small(mat2, blk, col, tick)
    gx_copy = pltpu.make_async_remote_copy(
        src_ref=gx_ref.at[0],
        dst_ref=gx_ref.at[1],
        send_sem=swap_send.at[3],
        recv_sem=swap_recv.at[3],
        device_id={"box": other},
        device_id_type=MESH,
    )
    gx_copy.start()
    swap(1).wait_recv()
    hold[...] = ss[1] + part[1]

    @pl.loop(0, count_f)
    def _(i):
        tee[rows_of(i), :] = xdot(mat2[rows_of(i), :], hold[...], NN)

    swap(2).wait_recv()

    @pl.loop(0, count_f)
    def _(i):
        mat3[rows_of(i), :] = (
            ss[2, rows_of(i), :]
            + part[2, rows_of(i), :]
            - xdot(hold[:, rows_of(i)], tee[...], TN)
        )

    tick()
    invert_small(mat3, blk, col, tick)
    left = rhs[:, :f]
    second = xdot(xdot(left, tee[...], NN) - rhs[:, f:], mat3[...], NN)
    z_ref[:, f:] = second
    z_ref[:, :f] = -xdot(left, mat2[...], NN) - xdot(second, tee[...], NT)
    while events:
        tick()
    for b in range(3):
        swap(b).wait_send()
    gx_copy.wait()
    for group in (first, rest, bulk):
        for g in group:
            for stage in range(last):
                g.copy(stage).wait_send()
    for i in range(len(bulk)):
        for stage in range(-1, last):
            cross(i, stage).wait()


def whole_cols(perm_ref, i, f):
    return (
        perm_ref[...] == lax.broadcasted_iota(jnp.int32, (f, BLOCK), 1) + i * BLOCK
    ).astype(jnp.bfloat16)


def product_kernel(
    half_ref, z_ref, lift_ref, own_ref, y_ref, gx_ref, dtn_ref, one_ref, two_ref,
    first_ref, second_ref, map_ref, high, low,
):
    step = pl.program_id(0)
    q, h, c = step // 8, (step // 4) % 2, step % 4
    half = half_ref[0]
    rows, f = z_ref.shape[0], z_ref.shape[1] // 2
    count = own_ref.shape[0]
    m = 4 * count

    @pl.when(step % 8 == 0)
    def _():
        z = split2(z_ref[...])
        for k in range(2):
            value = -dot3(z, split2(gx_ref[0, k]), NT)

            a, b = split2(value)
            high[k, :rows, :], low[k, :rows, :] = a, b

            @pl.when(q == 0)
            def _():
                a, b = split2(value[: 2 * m] + lift_ref[:, k * f : (k + 1) * f])
                high[k, : 2 * m, :], low[k, : 2 * m, :] = a, b

            a, b = split2(own_ref[:, k * f : (k + 1) * f])
            high[k, rows:, :], low[k, rows:, :] = a, b

    @pl.when(step == 0)
    def _():
        for k in range(2):
            at = pl.multiple_of((5 * k + 2 - half) * f, BLOCK)
            first_ref[:, pl.ds(at, f)] = y_ref[:, k * f : (k + 1) * f]

    res = dot3((high[h], low[h]), split2(one_ref[0, 0]), NN)
    zs = split2(z_ref[:, pl.ds(pl.multiple_of(h * f, BLOCK), f)])
    add = dot3(zs, split2(two_ref[0, 0]), NN)
    map_ref[...] = (res[: 2 * m] + add[: 2 * m]).reshape(map_ref.shape)
    second_ref[...] = res[2 * m : rows] + add[2 * m :]

    @pl.when(q == 0)
    def _():
        where = 5 * h + jnp.where(c == 0, 0, jnp.where(c == 1, 1 + half, c + 1))
        first_ref[:, pl.ds(pl.multiple_of(where * f, BLOCK), f)] = res[rows:]
        face = jnp.where(c == 0, h, jnp.where(c == 1, 2 + half, c + 2))
        cols = pl.ds(pl.multiple_of(face * f, BLOCK), f)
        for k, r in enumerate((h, 2 + half, 4, 5)):
            map_ref[4 * h + k] += dtn_ref[h, r, :, cols]


def fast_body(dtn, interface_perm):
    _, faces, count, width = dtn.shape
    f = width // faces
    n = lax.axis_size("row")
    bits = []
    bit = n // 2
    while bit:
        bits.append(bit)
        bit //= 2
    near, far = bits[-2:], bits[:-2]
    orders = [far + near, far + near[::-1], near[::-1] + far]
    tiles = f // BLOCK
    cuts = [(BLOCK * (tiles * i // 3), BLOCK * (tiles * (i + 1) // 3)) for i in range(3)]
    spans = [(0, 6, 0), (6, 12, 1), (12, 16, 2)]
    last = len(bits)
    plan = {
        "n": n,
        "f": f,
        "count": count,
        "bits": bits,
        "first": [((0, 2), cut, order) for cut, order in zip(cuts, orders)],
        "rest": [((2, 6), cut, order) for cut, order in zip(cuts, orders)],
        "bulk": [((a, b), (0, f), orders[k]) for a, b, k in spans],
        "events": [],
    }
    nb = len(plan["bulk"])
    rest = [[("rest", i, s) for i in range(3)] for s in range(1, last + 1)]
    bulk = [[("bulk", i, s) for i in range(nb)] for s in range(last + 1)]
    when = {0: rest[0], 2: rest[1] + bulk[0], 4: rest[2], 6: rest[3] + bulk[1], 11: bulk[2], 16: bulk[3]}
    plan["events"] = [when.get(k, []) for k in range(24)] + bulk[4:]
    split = (2,) * last
    vmem = pl.BlockSpec(memory_space=pltpu.VMEM)
    dma = pltpu.SemaphoreType.DMA
    rows = 9 * count
    f32 = jnp.float32
    z, lift, own, y, gx, bulk_all = pl.pallas_call(
        functools.partial(merge_kernel, plan),
        out_shape=[
            jax.ShapeDtypeStruct(s, f32)
            for s in (
                (rows, 2 * f),
                (8 * count, 2 * f),
                (count, 2 * f),
                (count, 2 * f),
                (2, 2, f, 2 * f),
                (2, 16, *split, count, f),
            )
        ],
        in_specs=[vmem, vmem],
        out_specs=[vmem] * 5 + [pl.BlockSpec(memory_space=pl.ANY)],
        scratch_shapes=[
            pltpu.VMEM((6, *split, count, f), f32),
            pltpu.VMEM((f, f), f32),
            pltpu.VMEM((f, f), f32),
            pltpu.VMEM((f, f), f32),
            pltpu.VMEM((f, f), f32),
            pltpu.VMEM((BLOCK, BLOCK), f32),
            pltpu.VMEM((f, BLOCK), f32),
            pltpu.VMEM((f, 2 * f), f32),
            pltpu.VMEM((3, f, f), f32),
            pltpu.VMEM((3, f, f), f32),
            pltpu.VMEM((rows, 2 * f), f32),
            pltpu.VMEM((f, f), f32),
            dma((22,)),
            dma((3, last)),
            dma((3, last)),
            dma((3, last)),
            dma((3, last)),
            dma((nb, last)),
            dma((nb, last)),
            dma((nb, last + 1)),
            dma((nb, last + 1)),
            dma((4,)),
            dma((4,)),
        ],
        compiler_params=pltpu.CompilerParams(
            collective_id=0, has_side_effects=True, vmem_limit_bytes=48 * 1024 * 1024
        ),
    )(interface_perm[0][:, None], dtn)
    bulk_all = bulk_all.reshape(2, 16, f, f)
    half = (lax.axis_index("box") % 2).astype(jnp.int32)
    lane = 2 * f

    def fixed(shape):
        return pl.BlockSpec(shape, lambda s, r: (0,) * len(shape))

    def column(s, r):
        own_half = r[0]
        return jnp.where(s < 8, own_half, 1 - own_half) * 8 + s % 8

    first, second, merged = pl.pallas_call(
        product_kernel,
        grid_spec=pltpu.PrefetchScalarGridSpec(
            num_scalar_prefetch=1,
            grid=(16,),
            in_specs=[
                fixed((rows, lane)),
                fixed((8 * count, lane)),
                fixed((count, lane)),
                fixed((count, lane)),
                pl.BlockSpec((1, 2, f, lane), lambda s, r: (s // 8, 0, 0, 0)),
                fixed(dtn.shape),
                pl.BlockSpec((1, 1, f, f), lambda s, r: (s // 8, s % 8, 0, 0)),
                pl.BlockSpec((1, 1, f, f), lambda s, r: (s // 8, 8 + s % 8, 0, 0)),
            ],
            out_specs=[
                fixed((count, 10 * f)),
                pl.BlockSpec((count, f), lambda s, r: (0, column(s, r))),
                pl.BlockSpec((8, count, f), lambda s, r: (0, 0, column(s, r))),
            ],
            scratch_shapes=[
                pltpu.VMEM((2, rows + count, f), jnp.bfloat16),
                pltpu.VMEM((2, rows + count, f), jnp.bfloat16),
            ],
        ),
        out_shape=[
            jax.ShapeDtypeStruct((count, 10 * f), f32),
            jax.ShapeDtypeStruct((count, 16 * f), f32),
            jax.ShapeDtypeStruct((8, count, 16 * f), f32),
        ],
        compiler_params=pltpu.CompilerParams(vmem_limit_bytes=40 * 1024 * 1024),
    )(half[None], z, lift, own, y, gx, dtn, bulk_all, bulk_all)
    return (first[None], second[None], merged[None])


def solution(mesh):
    def body(dtn, interface_perm):
        n = mesh.shape["row"]
        count = dtn.shape[2]
        if count % 8 == 0 and n >= 8 and n & (n - 1) == 0:
            return fast_body(dtn, interface_perm)
        return plain_body(dtn, interface_perm)

    return jax.shard_map(
        body,
        mesh=mesh,
        in_specs=(P("box", None, "row", None), P("box", None)),
        out_specs=(P("box", "row", None), P("box", "row", None), P("box", None, "row", None)),
        check_vma=False,
    )
```

```python
import functools

import jax
import jax.numpy as jnp
from jax import lax
from jax.experimental import pallas as pl
from jax.experimental.pallas import tpu as pltpu
from jax.sharding import PartitionSpec as P

HIGHEST = lax.Precision.HIGHEST
HIGH = lax.Precision.HIGH
BLOCK = 128
GROUP = 4
MESH = pl.DeviceIdType.MESH


def dot(left, right, precision=HIGHEST):
    return jnp.dot(left, right, precision=precision, preferred_element_type=jnp.float32)


def dot_t(left, right):
    return lax.dot_general(
        left, right, (((0,), (0,)), ((), ())), precision=HIGHEST, preferred_element_type=jnp.float32
    )


def invert_step(blk, lane, g, carry):
    size = blk.shape[0]
    k = g * GROUP
    full = blk[...]
    cols = [
        jnp.take_along_axis(full, jnp.full((size, size), k + i, jnp.int32), axis=1)
        for i in range(GROUP)
    ]
    rows = [blk[pl.ds(k + i, 1), :] for i in range(GROUP)]
    wide = [jnp.broadcast_to(r, (8, size)) for r in rows]
    pivots = [
        [
            jnp.take_along_axis(wide[i], jnp.full((8, size), k + j, jnp.int32), axis=1)
            for j in range(GROUP)
        ]
        for i in range(GROUP)
    ]
    inside = (lane >= k) & (lane < k + GROUP)
    wide = [
        jnp.where(lane == k + i, 1.0, jnp.where(inside, 0.0, wide[i])) for i in range(GROUP)
    ]
    for i in range(GROUP):
        p = 1.0 / pivots[i][i]
        wide[i] = wide[i] * p
        for j in range(i + 1, GROUP):
            pivots[i][j] = pivots[i][j] * p
        for l in range(GROUP):
            if l != i:
                f = pivots[l][i]
                wide[l] = wide[l] - f * wide[i]
                for j in range(i + 1, GROUP):
                    pivots[l][j] = pivots[l][j] - f * pivots[i][j]
    result = jnp.where(inside, 0.0, full)
    for i in range(GROUP):
        result = result - cols[i] * wide[i][0:1]
    blk[...] = result
    for i in range(GROUP):
        blk[pl.ds(k + i, 1), :] = wide[i][0:1]
    return carry


def invert_block(blk):
    size = blk.shape[0]
    lane = lax.broadcasted_iota(jnp.int32, (1, size), 1)
    lax.fori_loop(0, size // GROUP, functools.partial(invert_step, blk, lane), 0)


def invert(mat, blk, col):
    order = mat.shape[0]
    count = order // BLOCK
    eye = (
        lax.broadcasted_iota(jnp.int32, (BLOCK, BLOCK), 0)
        == lax.broadcasted_iota(jnp.int32, (BLOCK, BLOCK), 1)
    ).astype(jnp.float32)

    def outer(j, carry):
        here = pl.ds(pl.multiple_of(j * BLOCK, BLOCK), BLOCK)
        blk[...] = mat[here, here]
        invert_block(blk)
        col[...] = mat[:, here]
        mat[:, here] = jnp.zeros((order, BLOCK), jnp.float32)
        mat[here, here] = eye
        col[here, :] = jnp.zeros((BLOCK, BLOCK), jnp.float32)
        mat[here, :] = dot(blk[...], mat[here, :])

        def inner(i, c):
            there = pl.ds(pl.multiple_of(i * BLOCK, BLOCK), BLOCK)
            mat[there, :] = mat[there, :] - dot(col[there, :], mat[here, :])
            return c

        @pl.loop(0, count)
        def _(i):
            @pl.when(i != j)
            def _():
                inner(i, 0)

        return carry

    lax.fori_loop(0, count, outer, 0)


def first_kernel(perm_ref, small_ref, inv_ref, coupled_ref, own_ref, mat, blk, col):
    f = mat.shape[0]
    count = f // BLOCK

    def block(ref, i):
        return ref[:, i * f : (i + 1) * f]

    def place(rows):
        return (
            perm_ref[rows, :] == lax.broadcasted_iota(jnp.int32, (BLOCK, f), 1)
        ).astype(jnp.float32)

    whole = (perm_ref[...] == lax.broadcasted_iota(jnp.int32, (f, f), 1)).astype(jnp.float32)

    @pl.loop(0, count)
    def _(i):
        here = pl.ds(pl.multiple_of(i * BLOCK, BLOCK), BLOCK)
        moved = dot(place(here), block(small_ref, 1))
        mat[here, :] = small_ref[here, :f] + lax.dot_general(
            moved,
            whole,
            (((1,), (1,)), ((), ())),
            precision=HIGHEST,
            preferred_element_type=jnp.float32,
        )

    invert(mat, blk, col)

    @pl.loop(0, count)
    def _(i):
        here = pl.ds(pl.multiple_of(i * BLOCK, BLOCK), BLOCK)
        inv_ref[here, :f] = mat[here, :]
        inv_ref[here, f:] = dot(mat[here, :], whole)

    @pl.loop(0, count)
    def _(i):
        there = pl.ds(pl.multiple_of(f + i * BLOCK, BLOCK), BLOCK)
        picked = (
            perm_ref[...] == lax.broadcasted_iota(jnp.int32, (f, BLOCK), 1) + i * BLOCK
        ).astype(jnp.float32)
        inv_ref[there, :] = dot_t(picked, inv_ref[:f, :])

    for h in range(2):

        @pl.loop(0, count)
        def _(i):
            here = pl.ds(pl.multiple_of(i * BLOCK, BLOCK), BLOCK)
            rows = pl.ds(pl.multiple_of(h * f + i * BLOCK, BLOCK), BLOCK)
            edge = small_ref[:, pl.ds(pl.multiple_of((2 + h) * f + i * BLOCK, BLOCK), BLOCK)]
            coupled_ref[rows, :] = -dot_t(edge, inv_ref[h * f : (h + 1) * f, :])
            for c in range(2):
                value = dot(coupled_ref[rows, c * f : (c + 1) * f], block(small_ref, 2 + c))
                if c == h:
                    value = value + small_ref[here, (4 + h) * f : (5 + h) * f]
                own_ref[rows, c * f : (c + 1) * f] = value


def second_kernel(own_ref, part_ref, lift_ref, pick_ref, out_ref, mat, blk, col):
    mat[...] = own_ref[...] + part_ref[...]
    invert(mat, blk, col)
    n = lift_ref.shape[0]
    out_ref[:n, :] = dot(lift_ref[...], mat[...])
    out_ref[n:, :] = dot(pick_ref[...], mat[...])


def flip(index, bit):
    return index + bit - 2 * bit * ((index // bit) % 2)


def plan(n, width):
    bits = []
    bit = n // 2
    while bit:
        bits.append(bit)
        bit //= 2
    tiles = width // 128
    first = tiles * 3 // 8
    second = tiles * 3 // 8 + (tiles * 3 % 8 >= 4)
    orders = [bits, bits[:-2] + [1, 2], [1, 2] + bits[:-2]]
    sizes = [first, second, tiles - first - second]
    chunks, at = [], 0
    for order, size in zip(orders, sizes):
        chunks.append((at * 128, size * 128, order))
        at += size
    return bits, chunks


def gather_kernel(n, bits, chunks, x_ref, out_ref, send_sem, recv_sem, own_sem):
    me = lax.axis_index("row")
    barrier = pltpu.get_barrier_semaphore()
    for bit in bits:
        pl.semaphore_signal(
            barrier, inc=1, device_id={"row": flip(me, bit)}, device_id_type=pl.DeviceIdType.MESH
        )
    local = pltpu.make_async_copy(x_ref, out_ref.at[me], own_sem)
    local.start()
    local.wait()
    pl.semaphore_wait(barrier, len(bits))
    pending = [[] for _ in chunks]
    sent = []
    held = [[()] for _ in chunks]
    for t in range(len(bits)):
        for c, (start, size, order) in enumerate(chunks):
            for copy in pending[c]:
                copy.wait_recv()
            pending[c] = []
            bit = order[t]
            for s in held[c]:
                slot = me
                for one in s:
                    slot = flip(slot, one)
                number = (1 << t) - 1 + len(pending[c])
                piece = out_ref.at[slot, :, pl.ds(start, size)]
                copy = pltpu.make_async_remote_copy(
                    src_ref=piece,
                    dst_ref=piece,
                    send_sem=send_sem.at[c, number],
                    recv_sem=recv_sem.at[c, number],
                    device_id={"row": flip(me, bit)},
                    device_id_type=pl.DeviceIdType.MESH,
                )
                copy.start()
                pending[c].append(copy)
                sent.append(copy)
            held[c] = held[c] + [s + (bit,) for s in held[c]]
    for c in range(len(chunks)):
        for copy in pending[c]:
            copy.wait_recv()
    for copy in sent:
        copy.wait_send()


def quick_gather(x):
    n = lax.axis_size("row")
    count, width = x.shape
    bits, chunks = plan(n, width)
    out = pl.pallas_call(
        functools.partial(gather_kernel, n, bits, chunks),
        out_shape=jax.ShapeDtypeStruct((n, count, width), jnp.float32),
        in_specs=[pl.BlockSpec(memory_space=pltpu.VMEM)],
        out_specs=pl.BlockSpec(memory_space=pltpu.VMEM),
        scratch_shapes=[
            pltpu.SemaphoreType.DMA((len(chunks), n - 1)),
            pltpu.SemaphoreType.DMA((len(chunks), n - 1)),
            pltpu.SemaphoreType.DMA,
        ],
        compiler_params=pltpu.CompilerParams(
            collective_id=0, has_side_effects=True, vmem_limit_bytes=16 * 1024 * 1024
        ),
        cost_estimate=pl.CostEstimate(
            flops=10_000_000_000, bytes_accessed=2 * n * count * width * 4, transcendentals=0
        ),
    )(x)
    return out.reshape(n * count, width)


def call(kernel, out, order, *args):
    return pl.pallas_call(
        kernel,
        out_shape=[jax.ShapeDtypeStruct(o, jnp.float32) for o in out],
        in_specs=[pl.BlockSpec(memory_space=pltpu.VMEM)] * len(args),
        out_specs=[pl.BlockSpec(memory_space=pltpu.VMEM)] * len(out),
        scratch_shapes=[
            pltpu.VMEM((order, order), jnp.float32),
            pltpu.VMEM((BLOCK, BLOCK), jnp.float32),
            pltpu.VMEM((order, BLOCK), jnp.float32),
        ],
        compiler_params=pltpu.CompilerParams(vmem_limit_bytes=40 * 1024 * 1024),
        cost_estimate=pl.CostEstimate(
            flops=order * 20_000_000, bytes_accessed=order * order * 8, transcendentals=0
        ),
    )(*args)


def plain_body(dtn, interface_perm):
    a, b = dtn[0], dtn[1]
    count = a.shape[1]
    f = a.shape[2] // 6
    perm = interface_perm[0]
    rank = lax.axis_index("row")
    half = lax.axis_index("box") % 2
    first = half == 0

    def swap(x):
        n = lax.axis_size("box")
        return lax.ppermute(x, "box", [(i, i ^ 1) for i in range(n)])

    def gather(x):
        return lax.all_gather(x, "row", axis=0, tiled=True)

    def cols(x, face):
        return x[..., face * f : (face + 1) * f]

    def side(x):
        return jnp.where(first, cols(x, 3), cols(x, 2))

    def free(x):
        return jnp.where(first, cols(x, 2), cols(x, 3))

    def outer_cols(x, edge):
        return jnp.concatenate([cols(x, edge), free(x), cols(x, 4), cols(x, 5)], axis=-1)

    ay, by = jnp.where(first, a[3], a[2]), jnp.where(first, b[3], b[2])
    a1, b0 = a[1], b[0]
    small = quick_gather(
        jnp.concatenate(
            [cols(a1, 1), cols(b0, 0), side(a1), side(b0), side(ay), side(by)], axis=1
        )
    )
    bulk = gather(
        jnp.concatenate(
            [outer_cols(a1, 0), outer_cols(ay, 0), outer_cols(b0, 1), outer_cols(by, 1)], axis=1
        )
    )
    inv1, coupled, own_ss = call(first_kernel, [(2 * f, 2 * f)] * 3, f, perm[:, None], small)
    a1y, b0y = small[:, 2 * f : 3 * f], small[:, 3 * f : 4 * f]

    def times_side(x):
        return jnp.concatenate([dot(x[:, :f], a1y), dot(x[:, f:], b0y)], axis=1)

    part_ss = swap(own_ss)
    outer_a = jnp.concatenate(
        [a[0], jnp.where(first, a[2], a[3]), a[4], a[5]], axis=0
    )
    outer_b = jnp.concatenate(
        [b[1], jnp.where(first, b[2], b[3]), b[4], b[5]], axis=0
    )
    lift = -jnp.concatenate(
        [dot(cols(outer_a, 1), inv1[:f]), dot(cols(outer_b, 0), inv1[f:])], axis=0
    )
    n = 4 * count
    zero_n = jnp.zeros((n, f), jnp.float32)
    lift_two = times_side(lift) + jnp.concatenate(
        [
            jnp.concatenate([side(outer_a), zero_n], axis=1),
            jnp.concatenate([zero_n, side(outer_b)], axis=1),
        ],
        axis=0,
    )
    start = rank * count
    pick = (
        jnp.arange(2 * f, dtype=jnp.int32)[None, :]
        == half * f + start + jnp.arange(count, dtype=jnp.int32)[:, None]
    ).astype(jnp.float32)
    own_rows = lax.dynamic_slice(inv1, (start, 0), (count, 2 * f))
    z = -call(second_kernel, [(2 * n + count, 2 * f)], 2 * f, own_ss, part_ss, lift_two, pick)[0]
    z_part = swap(z)
    both = jnp.concatenate([z_part, z], axis=0)
    through = dot(both, coupled)
    m = 2 * n + count
    through = jnp.concatenate(
        [through[:m], through[m : m + 2 * n] + lift, through[m + 2 * n :], -own_rows], axis=0
    )
    both = jnp.concatenate([both, jnp.zeros((count, 2 * f), jnp.float32)], axis=0)
    w = 4 * f
    res_a = dot(through[:, :f], bulk[:, :w], HIGH) + dot(both[:, :f], bulk[:, w : 2 * w], HIGH)
    res_b = dot(through[:, f:], bulk[:, 2 * w : 3 * w], HIGH) + dot(both[:, f:], bulk[:, 3 * w :], HIGH)
    results = jnp.concatenate([res_a, res_b], axis=1)
    cross = swap(results[:m])
    own = results[m : 2 * m]
    base = jnp.concatenate(
        [
            jnp.concatenate([outer_cols(outer_a, 0), jnp.zeros((n, w), jnp.float32)], axis=1),
            jnp.concatenate([jnp.zeros((n, w), jnp.float32), outer_cols(outer_b, 1)], axis=1),
        ],
        axis=0,
    )
    own_map = own[: 2 * n] + base
    left = jnp.where(first, own_map, cross[: 2 * n])
    right = jnp.where(first, cross[: 2 * n], own_map)
    merged_map = jnp.concatenate([left, right], axis=1).reshape(1, 8, count, 4 * w)
    own_s, cross_s = own[2 * n :], cross[2 * n :]
    second = jnp.concatenate(
        [jnp.where(first, own_s, cross_s), jnp.where(first, cross_s, own_s)], axis=1
    )
    s1 = results[2 * m :]
    y_a, y_b = -dot(own_rows[:, :f], a1y), -dot(own_rows[:, f:], b0y)

    def ordered(x, y):
        two = jnp.where(first, cols(x, 1), y)
        three = jnp.where(first, y, cols(x, 1))
        return [cols(x, 0), two, three, x[:, 2 * f :]]

    solution_first = jnp.concatenate(ordered(s1[:, :w], y_a) + ordered(s1[:, w:], y_b), axis=1)
    return (solution_first[None], second[None], merged_map)


def split3(x):
    high = x.astype(jnp.bfloat16)
    rest = x - high.astype(jnp.float32)
    mid = rest.astype(jnp.bfloat16)
    low = (rest - mid.astype(jnp.float32)).astype(jnp.bfloat16)
    return high, mid, low


def dims(left, right):
    return (((left,), (right,)), ((), ()))


def bdot(left, right, dn):
    return lax.dot_general(left, right, dn, preferred_element_type=jnp.float32)


def pick_left(onehot, x, contract=1):
    return sum(bdot(onehot, part, dims(contract, 0)) for part in split3(x))


def pick_right(x, onehot, contract=0):
    return sum(bdot(part, onehot, dims(1, contract)) for part in split3(x))


def xdot(left, right, dn):
    return lax.dot_general(left, right, dn, precision=HIGHEST, preferred_element_type=jnp.float32)


def split2(x):
    high = x.astype(jnp.bfloat16)
    low = (x - high.astype(jnp.float32)).astype(jnp.bfloat16)
    return high, low


def dot3(left, right, dn):
    a, b = left
    c, d = right
    return bdot(a, c, dn) + (bdot(a, d, dn) + bdot(b, c, dn))


NN = dims(1, 0)
NT = dims(1, 1)
TN = dims(0, 0)


FIRST = ['xyba', 'byax', 'baxy', 'byxa', 'abyx', 'bxay']
FIRST_EVENTS = [(0, 0), (1, 0), (4, 0), (2, 0), (3, 0), (0, 1), (5, 0), (1, 1), (4, 1), (2, 1), (3, 1), (5, 1), (0, 2), (4, 2), (2, 2), (1, 2), (3, 2), (5, 2), (4, 3), (0, 3), (2, 3), (1, 3), (3, 3), (5, 3)]
REST = ['bayx', 'bxay', 'aybx', 'bayx', 'abxy', 'baxy']
BULK = [((0, 1), 'axby'), ((1, 2), 'bayx'), ((2, 3), 'xbay'), ((3, 4), 'yabx'), ((4, 6), 'axby'), ((6, 8), 'bayx'), ((8, 10), 'ybxa'), ((10, 12), 'bxay'), ((12, 14), 'byxa'), ((14, 16), 'bayx')]
BULK_START = 3
EVENTS = [(1, 0, 0), (1, 2, 0), (1, 1, 0), (1, 4, 0), (2, 3, 0), (3, 5, 0), (3, 1, 1), (3, 2, 1), (3, 0, 1), (4, 4, 1), (4, 3, 1), (4, 8, 0), (5, 0, 2), (5, 1, 2), (5, 9, 0), (7, 12, 0), (7, 5, 1), (7, 4, 2), (8, 6, 0), (8, 3, 2), (8, 2, 2), (8, 7, 0), (9, 10, 0), (9, 0, 3), (10, 1, 3), (10, 5, 2), (11, 11, 0), (11, 9, 1), (12, 4, 3), (12, 13, 0), (12, 7, 1), (12, 2, 3), (13, 14, 0), (13, 5, 3), (14, 3, 3), (14, 6, 1), (14, 15, 0), (14, 11, 1), (14, 7, 2), (15, 10, 1), (15, 8, 1), (15, 14, 1), (16, 13, 1), (18, 15, 1), (18, 12, 1), (18, 11, 2), (19, 7, 3), (21, 8, 2), (21, 9, 2), (23, 15, 2), (23, 14, 2), (25, 6, 2), (26, 8, 3), (28, 13, 2), (29, 6, 3), (29, 11, 3), (31, 10, 2), (32, 12, 2), (36, 9, 3), (36, 14, 3), (36, 13, 3), (41, 15, 3), (41, 12, 3), (41, 10, 3)]


def invert_small(mat, blk, col, tick):
    order = mat.shape[0]
    count = order // BLOCK
    eye = (
        lax.broadcasted_iota(jnp.int32, (BLOCK, BLOCK), 0)
        == lax.broadcasted_iota(jnp.int32, (BLOCK, BLOCK), 1)
    ).astype(jnp.float32)
    for j in range(count):
        here = pl.ds(j * BLOCK, BLOCK)
        blk[...] = mat[here, here]
        invert_steps(blk, tick)
        col[...] = mat[:, here]
        mat[:, here] = jnp.zeros((order, BLOCK), jnp.float32)
        mat[here, here] = eye
        mat[here, :] = xdot(blk[...], mat[here, :], NN)
        for i in range(count):
            if i != j:
                there = pl.ds(i * BLOCK, BLOCK)
                mat[there, :] = mat[there, :] - xdot(col[there, :], mat[here, :], NN)
        tick()


def invert_steps(blk, tick, parts=4):
    size = blk.shape[0]
    lane = lax.broadcasted_iota(jnp.int32, (1, size), 1)
    total = size // GROUP
    for part in range(parts):
        lax.fori_loop(
            part * total // parts,
            (part + 1) * total // parts,
            functools.partial(invert_step, blk, lane),
            0,
        )
        if part + 1 < parts:
            tick()


class Gather:
    def __init__(self, ref, lead, block, cols, order, me, n, sends, recvs):
        self.ref, self.lead, self.block, self.cols, self.order = ref, lead, block, cols, order
        self.me, self.n, self.sends, self.recvs = me, n, sends, recvs

    def view(self, stage, arrived):
        m = self.n.bit_length() - 1
        index = []
        for b in range(m - 1, -1, -1):
            bit = 1 << b
            own = (self.me // bit) % 2
            if bit in self.order[:stage]:
                index.append(slice(None))
            elif arrived and bit == self.order[stage]:
                index.append(1 - own)
            else:
                index.append(own)
        blocks = pl.ds(self.block[0], self.block[1] - self.block[0])
        cols = pl.ds(self.cols[0], self.cols[1] - self.cols[0])
        return self.ref.at[(*self.lead, blocks, *index, slice(None), cols)]

    def copy(self, stage):
        piece = self.view(stage, False)
        return pltpu.make_async_remote_copy(
            src_ref=piece,
            dst_ref=piece,
            send_sem=self.sends.at[stage],
            recv_sem=self.recvs.at[stage],
            device_id={"row": flip(self.me, self.order[stage])},
            device_id_type=MESH,
        )


def merge_kernel(
    plan, perm_ref, dtn_ref, z_ref, lift_ref, own_ref, y_ref, gx_ref, bulk_ref,
    small, mat1, mat2, mat3, tee, blk, col, edge, ss, part, rhs, hold,
    fill_sem, send0, recv0, send1, recv1, send2, recv2, core_send, core_recv, swap_send, swap_recv,
):
    n, f, count = plan["n"], plan["f"], plan["count"]
    bits = plan["bits"]
    me = lax.axis_index("row")
    pair = lax.axis_index("box")
    half = lax.rem(pair, 2)
    other = pair + 1 - 2 * half
    yface, free = 3 - half, 2 + half
    spot = [(me // bit) % 2 for bit in bits]

    def at(face):
        return pl.ds(face * f, f) if isinstance(face, int) else pl.ds(pl.multiple_of(face * f, BLOCK), f)

    narrow = [(0, 1, 1), (1, 0, 0), (0, 1, yface), (1, 0, yface), (0, yface, yface), (1, yface, yface)]
    outer = [(0, free, 4, 5), (1, free, 4, 5)]
    wide = [(h, r, c) for h in range(2) for c in outer[h] for r in (1 - h, yface)]
    fills = []
    for b, (h, r, c) in enumerate(narrow):
        fills.append(
            pltpu.make_async_copy(dtn_ref.at[h, r, :, at(c)], small.at[(b, *spot)], fill_sem.at[b])
        )
    for b, (h, r, c) in enumerate(wide):
        fills.append(
            pltpu.make_async_copy(
                dtn_ref.at[h, r, :, at(c)], bulk_ref.at[(0, b, *spot)], fill_sem.at[len(narrow) + b]
            )
        )
    for one in fills:
        one.start()

    barrier = pltpu.get_barrier_semaphore()
    for bit in bits:
        pl.semaphore_signal(barrier, inc=1, device_id={"row": flip(me, bit)}, device_id_type=MESH)
    pl.semaphore_signal(barrier, inc=1, device_id={"box": other}, device_id_type=MESH)
    pl.semaphore_wait(barrier, len(bits) + 1)

    def gathers(ref, lead, chunks, sends, recvs):
        return [
            Gather(ref, lead, block, cols, order, me, n, sends.at[i], recvs.at[i])
            for i, (block, cols, order) in enumerate(chunks)
        ]

    first = gathers(small, (), plan["first"], send0, recv0)
    rest = gathers(small, (), plan["rest"], send1, recv1)
    bulk = gathers(bulk_ref, (0,), plan["bulk"], send2, recv2)
    last = len(bits)

    def cross(i, stage):
        g = bulk[i]
        view = g.view(0, False) if stage < 0 else g.view(stage, True)
        there = Gather(bulk_ref, (1,), g.block, g.cols, g.order, me, n, None, None)
        target = there.view(0, False) if stage < 0 else there.view(stage, True)
        return pltpu.make_async_remote_copy(
            src_ref=view,
            dst_ref=target,
            send_sem=core_send.at[i, stage + 1],
            recv_sem=core_recv.at[i, stage + 1],
            device_id={"box": other},
            device_id_type=MESH,
        )

    def advance(group, i, stage):
        g = group[i]
        if stage > 0:
            g.copy(stage - 1).wait_recv()
        if stage < last:
            g.copy(stage).start()
        if group is bulk:
            cross(i, stage - 1).start()

    events = list(plan["events"])
    groups = {"first": first, "rest": rest, "bulk": bulk}

    def tick():
        if events:
            for name, i, stage in events.pop(0):
                advance(groups[name], i, stage)

    for one in fills[: len(narrow)]:
        one.wait()
    for i in range(len(first)):
        advance(first, i, 0)
    for i, stage in plan["first_events"]:
        advance(first, i, stage + 1)
        if (i, stage) == plan["first_events"][-len(first)]:
            for k in range(len(rest)):
                advance(rest, k, 0)
    for one in fills[len(narrow) :]:
        one.wait()

    def block(b):
        return small[b].reshape(f, f)

    count_f = f // BLOCK
    whole = (perm_ref[...] == lax.broadcasted_iota(jnp.int32, (f, f), 1)).astype(jnp.bfloat16)
    hold[...] = pick_left(whole, block(1))
    mat1[...] = block(0) + pick_right(hold[...], whole, 1)
    tick()
    invert_small(mat1, blk, col, tick)

    edge[:, :f] = block(2)
    edge[:, f:] = pick_left(whole, block(3))

    def rows_of(i):
        return pl.ds(pl.multiple_of(i * BLOCK, BLOCK), BLOCK)

    @pl.loop(0, count_f)
    def _(i):
        gx_ref[0, 0, rows_of(i), :] = xdot(mat1[rows_of(i), :], edge[...], NN)

    tick()

    def swap(b):
        return pltpu.make_async_remote_copy(
            src_ref=ss.at[b],
            dst_ref=part.at[b],
            send_sem=swap_send.at[b],
            recv_sem=swap_recv.at[b],
            device_id={"box": other},
            device_id_type=MESH,
        )

    for b, (i, j) in enumerate([(0, 0), (0, 1), (1, 1)]):

        @pl.loop(0, count_f)
        def _(k):
            left = edge[:, pl.ds(pl.multiple_of(i * f + k * BLOCK, BLOCK), BLOCK)]
            value = -xdot(left, gx_ref[0, 0, :, j * f : (j + 1) * f], TN)
            ss[b, rows_of(k), :] = value

    tick()
    ss[0] = ss[0] + block(4)
    swap(1).start()
    ss[2] = ss[2] + block(5)
    swap(0).start()

    outers = []
    for h in range(2):
        outers.append(
            jnp.concatenate([dtn_ref[h, r, :, pl.ds((1 - h) * f, f)] for r in outer[h]], axis=0)
        )
    swap(2).start()
    m = 4 * count
    joined = jnp.concatenate([outers[0], pick_right(outers[1], whole, 1)], axis=0)
    value = -xdot(joined, mat1[...], NN)
    lift_ref[:, :f] = value
    lift_ref[:, f:] = pick_right(value, whole)
    own_at = pl.ds(pl.multiple_of(me * count, 8), count)
    mine = mat1[own_at, :]
    own_ref[:, :f] = -mine
    own_ref[:, f:] = -pick_right(mine, whole)
    y_ref[...] = -gx_ref[0, 0, own_at, :]
    rhs[: 2 * m, :] = -xdot(joined, gx_ref[0, 0], NN)
    for h in range(2):
        side = jnp.concatenate([dtn_ref[h, r, :, at(yface)] for r in outer[h]], axis=0)
        rhs[h * m : (h + 1) * m, h * f : (h + 1) * f] += side
    rhs[2 * m :, :] = (
        lax.broadcasted_iota(jnp.int32, (count, 2 * f), 1)
        == half * f + me * count + lax.broadcasted_iota(jnp.int32, (count, 2 * f), 0)
    ).astype(jnp.float32)

    @pl.loop(0, count_f)
    def _(i):
        picked = whole_cols(perm_ref, i, f)
        gx_ref[0, 1, rows_of(i), :] = pick_left(picked, gx_ref[0, 0], 0)

    tick()
    swap(0).wait_recv()
    mat2[...] = ss[0] + part[0]
    invert_small(mat2, blk, col, tick)
    gx_copy = pltpu.make_async_remote_copy(
        src_ref=gx_ref.at[0],
        dst_ref=gx_ref.at[1],
        send_sem=swap_send.at[3],
        recv_sem=swap_recv.at[3],
        device_id={"box": other},
        device_id_type=MESH,
    )
    gx_copy.start()
    swap(1).wait_recv()
    hold[...] = ss[1] + part[1]

    @pl.loop(0, count_f)
    def _(i):
        tee[rows_of(i), :] = xdot(mat2[rows_of(i), :], hold[...], NN)

    swap(2).wait_recv()

    @pl.loop(0, count_f)
    def _(i):
        mat3[rows_of(i), :] = (
            ss[2, rows_of(i), :]
            + part[2, rows_of(i), :]
            - xdot(hold[:, rows_of(i)], tee[...], TN)
        )

    tick()
    invert_small(mat3, blk, col, tick)
    left = rhs[:, :f]
    second = xdot(xdot(left, tee[...], NN) - rhs[:, f:], mat3[...], NN)
    z_ref[:, f:] = second
    z_ref[:, :f] = -xdot(left, mat2[...], NN) - xdot(second, tee[...], NT)
    while events:
        tick()
    for b in range(3):
        swap(b).wait_send()
    gx_copy.wait()
    for group in (first, rest, bulk):
        for g in group:
            for stage in range(last):
                g.copy(stage).wait_send()
    for i in range(len(bulk)):
        for stage in range(-1, last):
            cross(i, stage).wait()


def whole_cols(perm_ref, i, f):
    return (
        perm_ref[...] == lax.broadcasted_iota(jnp.int32, (f, BLOCK), 1) + i * BLOCK
    ).astype(jnp.bfloat16)


def product_kernel(
    half_ref, z_ref, lift_ref, own_ref, y_ref, gx_ref, dtn_ref, wide_ref,
    first_ref, second_ref, map_ref, high, low,
):
    step = pl.program_id(0)
    q, h, c = step // 4, (step // 2) % 2, 2 * (step % 2)
    half = half_ref[0]
    rows, f = z_ref.shape[0], z_ref.shape[1] // 2
    count = own_ref.shape[0]
    m = 4 * count

    @pl.when(step % 4 == 0)
    def _():
        z = split2(z_ref[...])
        for k in range(2):
            high[k, :rows, f:], low[k, :rows, f:] = [one[:, k * f : (k + 1) * f] for one in z]
            zero = jnp.zeros((count, f), jnp.bfloat16)
            high[k, rows:, f:], low[k, rows:, f:] = zero, zero
            value = -dot3(z, split2(gx_ref[0, k]), NT)
            high[k, :rows, :f], low[k, :rows, :f] = split2(value)

            @pl.when(q == 0)
            def _():
                a, b = split2(value[: 2 * m] + lift_ref[:, k * f : (k + 1) * f])
                high[k, : 2 * m, :f], low[k, : 2 * m, :f] = a, b

            a, b = split2(own_ref[:, k * f : (k + 1) * f])
            high[k, rows:, :f], low[k, rows:, :f] = a, b

    @pl.when(step == 0)
    def _():
        for k in range(2):
            at = pl.multiple_of((5 * k + 2 - half) * f, BLOCK)
            first_ref[:, pl.ds(at, f)] = y_ref[:, k * f : (k + 1) * f]

    def columns(k):
        return wide_ref[0, 2 * k : 2 * k + 2].reshape(2 * f, f)

    right = split2(jnp.concatenate([columns(0), columns(1)], axis=1))
    res = dot3((high[h], low[h]), right, NN)
    map_ref[...] = res[: 2 * m].reshape(map_ref.shape)
    second_ref[...] = res[2 * m : rows]

    @pl.when(q == 0)
    def _():
        for k in range(2):
            place = c + k
            here = slice(k * f, (k + 1) * f)
            where = 5 * h + jnp.where(place == 0, 0, jnp.where(place == 1, 1 + half, place + 1))
            first_ref[:, pl.ds(pl.multiple_of(where * f, BLOCK), f)] = res[rows:, here]
            face = jnp.where(place == 0, h, jnp.where(place == 1, 2 + half, place + 2))
            cols = pl.ds(pl.multiple_of(face * f, BLOCK), f)
            for i, r in enumerate((h, 2 + half, 4, 5)):
                map_ref[4 * h + i, :, here] += dtn_ref[h, r, :, cols]


def fast_body(dtn, interface_perm):
    _, faces, count, width = dtn.shape
    f = width // faces
    n = lax.axis_size("row")
    bits = []
    bit = n // 2
    while bit:
        bits.append(bit)
        bit //= 2
    last = len(bits)
    tiles = f // BLOCK
    cuts = [(BLOCK * (tiles * i // 3), BLOCK * (tiles * (i + 1) // 3)) for i in range(3)]
    named = dict(zip("bayx", bits))

    def order(letters):
        return [named[one] for one in letters]

    six = [((a, a + 1), cut) for a in range(2) for cut in cuts]
    rest_parts = [((a, a + 2), cut) for a in (2, 4) for cut in cuts]
    events = [[] for _ in range(1 + max(k for k, _, _ in EVENTS))]
    events[BULK_START] = [("bulk", i, 0) for i in range(len(BULK))]
    for k, i, stage in EVENTS:
        if i < len(REST):
            events[k].append(("rest", i, stage + 1))
        else:
            events[k].append(("bulk", i - len(REST), stage + 1))
    nb = len(BULK)
    plan = {
        "n": n,
        "f": f,
        "count": count,
        "bits": bits,
        "first": [(*part, order(o)) for part, o in zip(six, FIRST)],
        "first_events": FIRST_EVENTS,
        "rest": [(*part, order(o)) for part, o in zip(rest_parts, REST)],
        "bulk": [(blocks, (0, f), order(o)) for blocks, o in BULK],
        "events": events,
    }
    split = (2,) * last
    vmem = pl.BlockSpec(memory_space=pltpu.VMEM)
    dma = pltpu.SemaphoreType.DMA
    rows = 9 * count
    f32 = jnp.float32
    z, lift, own, y, gx, bulk_all = pl.pallas_call(
        functools.partial(merge_kernel, plan),
        out_shape=[
            jax.ShapeDtypeStruct(s, f32)
            for s in (
                (rows, 2 * f),
                (8 * count, 2 * f),
                (count, 2 * f),
                (count, 2 * f),
                (2, 2, f, 2 * f),
                (2, 16, *split, count, f),
            )
        ],
        in_specs=[vmem, vmem],
        out_specs=[vmem] * 5 + [pl.BlockSpec(memory_space=pl.ANY)],
        scratch_shapes=[
            pltpu.VMEM((6, *split, count, f), f32),
            pltpu.VMEM((f, f), f32),
            pltpu.VMEM((f, f), f32),
            pltpu.VMEM((f, f), f32),
            pltpu.VMEM((f, f), f32),
            pltpu.VMEM((BLOCK, BLOCK), f32),
            pltpu.VMEM((f, BLOCK), f32),
            pltpu.VMEM((f, 2 * f), f32),
            pltpu.VMEM((3, f, f), f32),
            pltpu.VMEM((3, f, f), f32),
            pltpu.VMEM((rows, 2 * f), f32),
            pltpu.VMEM((f, f), f32),
            dma((22,)),
            dma((6, last)),
            dma((6, last)),
            dma((6, last)),
            dma((6, last)),
            dma((nb, last)),
            dma((nb, last)),
            dma((nb, last + 1)),
            dma((nb, last + 1)),
            dma((4,)),
            dma((4,)),
        ],
        compiler_params=pltpu.CompilerParams(
            collective_id=0, has_side_effects=True, vmem_limit_bytes=48 * 1024 * 1024
        ),
    )(interface_perm[0][:, None], dtn)
    bulk_all = bulk_all.reshape(2, 16, f, f)
    half = (lax.axis_index("box") % 2).astype(jnp.int32)
    lane = 2 * f

    def fixed(shape):
        return pl.BlockSpec(shape, lambda s, r: (0,) * len(shape))

    def column(s, r):
        own_half = r[0]
        return jnp.where(s < 4, own_half, 1 - own_half) * 4 + s % 4

    first, second, merged = pl.pallas_call(
        product_kernel,
        grid_spec=pltpu.PrefetchScalarGridSpec(
            num_scalar_prefetch=1,
            grid=(8,),
            in_specs=[
                fixed((rows, lane)),
                fixed((8 * count, lane)),
                fixed((count, lane)),
                fixed((count, lane)),
                pl.BlockSpec((1, 2, f, lane), lambda s, r: (s // 4, 0, 0, 0)),
                fixed(dtn.shape),
                pl.BlockSpec((1, 4, f, f), lambda s, r: (s // 4, s % 4, 0, 0)),
            ],
            out_specs=[
                fixed((count, 10 * f)),
                pl.BlockSpec((count, lane), lambda s, r: (0, column(s, r))),
                pl.BlockSpec((8, count, lane), lambda s, r: (0, 0, column(s, r))),
            ],
            scratch_shapes=[
                pltpu.VMEM((2, rows + count, 2 * f), jnp.bfloat16),
                pltpu.VMEM((2, rows + count, 2 * f), jnp.bfloat16),
            ],
        ),
        out_shape=[
            jax.ShapeDtypeStruct((count, 10 * f), f32),
            jax.ShapeDtypeStruct((count, 16 * f), f32),
            jax.ShapeDtypeStruct((8, count, 16 * f), f32),
        ],
        compiler_params=pltpu.CompilerParams(vmem_limit_bytes=40 * 1024 * 1024),
    )(half[None], z, lift, own, y, gx, dtn, bulk_all)
    return (first[None], second[None], merged[None])


def solution(mesh):
    def body(dtn, interface_perm):
        n = mesh.shape["row"]
        count = dtn.shape[2]
        if count % 8 == 0 and n == 1 << len(FIRST[0]):
            return fast_body(dtn, interface_perm)
        return plain_body(dtn, interface_perm)

    return jax.shard_map(
        body,
        mesh=mesh,
        in_specs=(P("box", None, "row", None), P("box", None)),
        out_specs=(P("box", "row", None), P("box", "row", None), P("box", None, "row", None)),
        check_vma=False,
    )
```

```python
import functools

import jax
import jax.numpy as jnp
from jax import lax
from jax.experimental import pallas as pl
from jax.experimental.pallas import tpu as pltpu
from jax.sharding import PartitionSpec as P

HIGHEST = lax.Precision.HIGHEST
HIGH = lax.Precision.HIGH
BLOCK = 128
GROUP = 4
MESH = pl.DeviceIdType.MESH


def dot(left, right, precision=HIGHEST):
    return jnp.dot(left, right, precision=precision, preferred_element_type=jnp.float32)


def dot_t(left, right):
    return lax.dot_general(
        left, right, (((0,), (0,)), ((), ())), precision=HIGHEST, preferred_element_type=jnp.float32
    )


def invert_step(blk, lane, g, carry):
    size = blk.shape[0]
    k = g * GROUP
    full = blk[...]
    cols = [
        jnp.take_along_axis(full, jnp.full((size, size), k + i, jnp.int32), axis=1)
        for i in range(GROUP)
    ]
    rows = [blk[pl.ds(k + i, 1), :] for i in range(GROUP)]
    wide = [jnp.broadcast_to(r, (8, size)) for r in rows]
    pivots = [
        [
            jnp.take_along_axis(wide[i], jnp.full((8, size), k + j, jnp.int32), axis=1)
            for j in range(GROUP)
        ]
        for i in range(GROUP)
    ]
    inside = (lane >= k) & (lane < k + GROUP)
    wide = [
        jnp.where(lane == k + i, 1.0, jnp.where(inside, 0.0, wide[i])) for i in range(GROUP)
    ]
    for i in range(GROUP):
        p = 1.0 / pivots[i][i]
        wide[i] = wide[i] * p
        for j in range(i + 1, GROUP):
            pivots[i][j] = pivots[i][j] * p
        for l in range(GROUP):
            if l != i:
                f = pivots[l][i]
                wide[l] = wide[l] - f * wide[i]
                for j in range(i + 1, GROUP):
                    pivots[l][j] = pivots[l][j] - f * pivots[i][j]
    result = jnp.where(inside, 0.0, full)
    for i in range(GROUP):
        result = result - cols[i] * wide[i][0:1]
    blk[...] = result
    for i in range(GROUP):
        blk[pl.ds(k + i, 1), :] = wide[i][0:1]
    return carry


def invert_block(blk):
    size = blk.shape[0]
    lane = lax.broadcasted_iota(jnp.int32, (1, size), 1)
    lax.fori_loop(0, size // GROUP, functools.partial(invert_step, blk, lane), 0)


def invert(mat, blk, col):
    order = mat.shape[0]
    count = order // BLOCK
    eye = (
        lax.broadcasted_iota(jnp.int32, (BLOCK, BLOCK), 0)
        == lax.broadcasted_iota(jnp.int32, (BLOCK, BLOCK), 1)
    ).astype(jnp.float32)

    def outer(j, carry):
        here = pl.ds(pl.multiple_of(j * BLOCK, BLOCK), BLOCK)
        blk[...] = mat[here, here]
        invert_block(blk)
        col[...] = mat[:, here]
        mat[:, here] = jnp.zeros((order, BLOCK), jnp.float32)
        mat[here, here] = eye
        col[here, :] = jnp.zeros((BLOCK, BLOCK), jnp.float32)
        mat[here, :] = dot(blk[...], mat[here, :])

        def inner(i, c):
            there = pl.ds(pl.multiple_of(i * BLOCK, BLOCK), BLOCK)
            mat[there, :] = mat[there, :] - dot(col[there, :], mat[here, :])
            return c

        @pl.loop(0, count)
        def _(i):
            @pl.when(i != j)
            def _():
                inner(i, 0)

        return carry

    lax.fori_loop(0, count, outer, 0)


def first_kernel(perm_ref, small_ref, inv_ref, coupled_ref, own_ref, mat, blk, col):
    f = mat.shape[0]
    count = f // BLOCK

    def block(ref, i):
        return ref[:, i * f : (i + 1) * f]

    def place(rows):
        return (
            perm_ref[rows, :] == lax.broadcasted_iota(jnp.int32, (BLOCK, f), 1)
        ).astype(jnp.float32)

    whole = (perm_ref[...] == lax.broadcasted_iota(jnp.int32, (f, f), 1)).astype(jnp.float32)

    @pl.loop(0, count)
    def _(i):
        here = pl.ds(pl.multiple_of(i * BLOCK, BLOCK), BLOCK)
        moved = dot(place(here), block(small_ref, 1))
        mat[here, :] = small_ref[here, :f] + lax.dot_general(
            moved,
            whole,
            (((1,), (1,)), ((), ())),
            precision=HIGHEST,
            preferred_element_type=jnp.float32,
        )

    invert(mat, blk, col)

    @pl.loop(0, count)
    def _(i):
        here = pl.ds(pl.multiple_of(i * BLOCK, BLOCK), BLOCK)
        inv_ref[here, :f] = mat[here, :]
        inv_ref[here, f:] = dot(mat[here, :], whole)

    @pl.loop(0, count)
    def _(i):
        there = pl.ds(pl.multiple_of(f + i * BLOCK, BLOCK), BLOCK)
        picked = (
            perm_ref[...] == lax.broadcasted_iota(jnp.int32, (f, BLOCK), 1) + i * BLOCK
        ).astype(jnp.float32)
        inv_ref[there, :] = dot_t(picked, inv_ref[:f, :])

    for h in range(2):

        @pl.loop(0, count)
        def _(i):
            here = pl.ds(pl.multiple_of(i * BLOCK, BLOCK), BLOCK)
            rows = pl.ds(pl.multiple_of(h * f + i * BLOCK, BLOCK), BLOCK)
            edge = small_ref[:, pl.ds(pl.multiple_of((2 + h) * f + i * BLOCK, BLOCK), BLOCK)]
            coupled_ref[rows, :] = -dot_t(edge, inv_ref[h * f : (h + 1) * f, :])
            for c in range(2):
                value = dot(coupled_ref[rows, c * f : (c + 1) * f], block(small_ref, 2 + c))
                if c == h:
                    value = value + small_ref[here, (4 + h) * f : (5 + h) * f]
                own_ref[rows, c * f : (c + 1) * f] = value


def second_kernel(own_ref, part_ref, lift_ref, pick_ref, out_ref, mat, blk, col):
    mat[...] = own_ref[...] + part_ref[...]
    invert(mat, blk, col)
    n = lift_ref.shape[0]
    out_ref[:n, :] = dot(lift_ref[...], mat[...])
    out_ref[n:, :] = dot(pick_ref[...], mat[...])


def flip(index, bit):
    return index + bit - 2 * bit * ((index // bit) % 2)


def plan(n, width):
    bits = []
    bit = n // 2
    while bit:
        bits.append(bit)
        bit //= 2
    tiles = width // 128
    first = tiles * 3 // 8
    second = tiles * 3 // 8 + (tiles * 3 % 8 >= 4)
    orders = [bits, bits[:-2] + [1, 2], [1, 2] + bits[:-2]]
    sizes = [first, second, tiles - first - second]
    chunks, at = [], 0
    for order, size in zip(orders, sizes):
        chunks.append((at * 128, size * 128, order))
        at += size
    return bits, chunks


def gather_kernel(n, bits, chunks, x_ref, out_ref, send_sem, recv_sem, own_sem):
    me = lax.axis_index("row")
    barrier = pltpu.get_barrier_semaphore()
    for bit in bits:
        pl.semaphore_signal(
            barrier, inc=1, device_id={"row": flip(me, bit)}, device_id_type=pl.DeviceIdType.MESH
        )
    local = pltpu.make_async_copy(x_ref, out_ref.at[me], own_sem)
    local.start()
    local.wait()
    pl.semaphore_wait(barrier, len(bits))
    pending = [[] for _ in chunks]
    sent = []
    held = [[()] for _ in chunks]
    for t in range(len(bits)):
        for c, (start, size, order) in enumerate(chunks):
            for copy in pending[c]:
                copy.wait_recv()
            pending[c] = []
            bit = order[t]
            for s in held[c]:
                slot = me
                for one in s:
                    slot = flip(slot, one)
                number = (1 << t) - 1 + len(pending[c])
                piece = out_ref.at[slot, :, pl.ds(start, size)]
                copy = pltpu.make_async_remote_copy(
                    src_ref=piece,
                    dst_ref=piece,
                    send_sem=send_sem.at[c, number],
                    recv_sem=recv_sem.at[c, number],
                    device_id={"row": flip(me, bit)},
                    device_id_type=pl.DeviceIdType.MESH,
                )
                copy.start()
                pending[c].append(copy)
                sent.append(copy)
            held[c] = held[c] + [s + (bit,) for s in held[c]]
    for c in range(len(chunks)):
        for copy in pending[c]:
            copy.wait_recv()
    for copy in sent:
        copy.wait_send()


def quick_gather(x):
    n = lax.axis_size("row")
    count, width = x.shape
    bits, chunks = plan(n, width)
    out = pl.pallas_call(
        functools.partial(gather_kernel, n, bits, chunks),
        out_shape=jax.ShapeDtypeStruct((n, count, width), jnp.float32),
        in_specs=[pl.BlockSpec(memory_space=pltpu.VMEM)],
        out_specs=pl.BlockSpec(memory_space=pltpu.VMEM),
        scratch_shapes=[
            pltpu.SemaphoreType.DMA((len(chunks), n - 1)),
            pltpu.SemaphoreType.DMA((len(chunks), n - 1)),
            pltpu.SemaphoreType.DMA,
        ],
        compiler_params=pltpu.CompilerParams(
            collective_id=0, has_side_effects=True, vmem_limit_bytes=16 * 1024 * 1024
        ),
        cost_estimate=pl.CostEstimate(
            flops=10_000_000_000, bytes_accessed=2 * n * count * width * 4, transcendentals=0
        ),
    )(x)
    return out.reshape(n * count, width)


def call(kernel, out, order, *args):
    return pl.pallas_call(
        kernel,
        out_shape=[jax.ShapeDtypeStruct(o, jnp.float32) for o in out],
        in_specs=[pl.BlockSpec(memory_space=pltpu.VMEM)] * len(args),
        out_specs=[pl.BlockSpec(memory_space=pltpu.VMEM)] * len(out),
        scratch_shapes=[
            pltpu.VMEM((order, order), jnp.float32),
            pltpu.VMEM((BLOCK, BLOCK), jnp.float32),
            pltpu.VMEM((order, BLOCK), jnp.float32),
        ],
        compiler_params=pltpu.CompilerParams(vmem_limit_bytes=40 * 1024 * 1024),
        cost_estimate=pl.CostEstimate(
            flops=order * 20_000_000, bytes_accessed=order * order * 8, transcendentals=0
        ),
    )(*args)


def plain_body(dtn, interface_perm):
    a, b = dtn[0], dtn[1]
    count = a.shape[1]
    f = a.shape[2] // 6
    perm = interface_perm[0]
    rank = lax.axis_index("row")
    half = lax.axis_index("box") % 2
    first = half == 0

    def swap(x):
        n = lax.axis_size("box")
        return lax.ppermute(x, "box", [(i, i ^ 1) for i in range(n)])

    def gather(x):
        return lax.all_gather(x, "row", axis=0, tiled=True)

    def cols(x, face):
        return x[..., face * f : (face + 1) * f]

    def side(x):
        return jnp.where(first, cols(x, 3), cols(x, 2))

    def free(x):
        return jnp.where(first, cols(x, 2), cols(x, 3))

    def outer_cols(x, edge):
        return jnp.concatenate([cols(x, edge), free(x), cols(x, 4), cols(x, 5)], axis=-1)

    ay, by = jnp.where(first, a[3], a[2]), jnp.where(first, b[3], b[2])
    a1, b0 = a[1], b[0]
    small = quick_gather(
        jnp.concatenate(
            [cols(a1, 1), cols(b0, 0), side(a1), side(b0), side(ay), side(by)], axis=1
        )
    )
    bulk = gather(
        jnp.concatenate(
            [outer_cols(a1, 0), outer_cols(ay, 0), outer_cols(b0, 1), outer_cols(by, 1)], axis=1
        )
    )
    inv1, coupled, own_ss = call(first_kernel, [(2 * f, 2 * f)] * 3, f, perm[:, None], small)
    a1y, b0y = small[:, 2 * f : 3 * f], small[:, 3 * f : 4 * f]

    def times_side(x):
        return jnp.concatenate([dot(x[:, :f], a1y), dot(x[:, f:], b0y)], axis=1)

    part_ss = swap(own_ss)
    outer_a = jnp.concatenate(
        [a[0], jnp.where(first, a[2], a[3]), a[4], a[5]], axis=0
    )
    outer_b = jnp.concatenate(
        [b[1], jnp.where(first, b[2], b[3]), b[4], b[5]], axis=0
    )
    lift = -jnp.concatenate(
        [dot(cols(outer_a, 1), inv1[:f]), dot(cols(outer_b, 0), inv1[f:])], axis=0
    )
    n = 4 * count
    zero_n = jnp.zeros((n, f), jnp.float32)
    lift_two = times_side(lift) + jnp.concatenate(
        [
            jnp.concatenate([side(outer_a), zero_n], axis=1),
            jnp.concatenate([zero_n, side(outer_b)], axis=1),
        ],
        axis=0,
    )
    start = rank * count
    pick = (
        jnp.arange(2 * f, dtype=jnp.int32)[None, :]
        == half * f + start + jnp.arange(count, dtype=jnp.int32)[:, None]
    ).astype(jnp.float32)
    own_rows = lax.dynamic_slice(inv1, (start, 0), (count, 2 * f))
    z = -call(second_kernel, [(2 * n + count, 2 * f)], 2 * f, own_ss, part_ss, lift_two, pick)[0]
    z_part = swap(z)
    both = jnp.concatenate([z_part, z], axis=0)
    through = dot(both, coupled)
    m = 2 * n + count
    through = jnp.concatenate(
        [through[:m], through[m : m + 2 * n] + lift, through[m + 2 * n :], -own_rows], axis=0
    )
    both = jnp.concatenate([both, jnp.zeros((count, 2 * f), jnp.float32)], axis=0)
    w = 4 * f
    res_a = dot(through[:, :f], bulk[:, :w], HIGH) + dot(both[:, :f], bulk[:, w : 2 * w], HIGH)
    res_b = dot(through[:, f:], bulk[:, 2 * w : 3 * w], HIGH) + dot(both[:, f:], bulk[:, 3 * w :], HIGH)
    results = jnp.concatenate([res_a, res_b], axis=1)
    cross = swap(results[:m])
    own = results[m : 2 * m]
    base = jnp.concatenate(
        [
            jnp.concatenate([outer_cols(outer_a, 0), jnp.zeros((n, w), jnp.float32)], axis=1),
            jnp.concatenate([jnp.zeros((n, w), jnp.float32), outer_cols(outer_b, 1)], axis=1),
        ],
        axis=0,
    )
    own_map = own[: 2 * n] + base
    left = jnp.where(first, own_map, cross[: 2 * n])
    right = jnp.where(first, cross[: 2 * n], own_map)
    merged_map = jnp.concatenate([left, right], axis=1).reshape(1, 8, count, 4 * w)
    own_s, cross_s = own[2 * n :], cross[2 * n :]
    second = jnp.concatenate(
        [jnp.where(first, own_s, cross_s), jnp.where(first, cross_s, own_s)], axis=1
    )
    s1 = results[2 * m :]
    y_a, y_b = -dot(own_rows[:, :f], a1y), -dot(own_rows[:, f:], b0y)

    def ordered(x, y):
        two = jnp.where(first, cols(x, 1), y)
        three = jnp.where(first, y, cols(x, 1))
        return [cols(x, 0), two, three, x[:, 2 * f :]]

    solution_first = jnp.concatenate(ordered(s1[:, :w], y_a) + ordered(s1[:, w:], y_b), axis=1)
    return (solution_first[None], second[None], merged_map)


def split3(x):
    high = x.astype(jnp.bfloat16)
    rest = x - high.astype(jnp.float32)
    mid = rest.astype(jnp.bfloat16)
    low = (rest - mid.astype(jnp.float32)).astype(jnp.bfloat16)
    return high, mid, low


def dims(left, right):
    return (((left,), (right,)), ((), ()))


def bdot(left, right, dn):
    return lax.dot_general(left, right, dn, preferred_element_type=jnp.float32)


def pick_left(onehot, x, contract=1):
    return sum(bdot(onehot, part, dims(contract, 0)) for part in split3(x))


def pick_right(x, onehot, contract=0):
    return sum(bdot(part, onehot, dims(1, contract)) for part in split3(x))


def xdot(left, right, dn):
    return lax.dot_general(left, right, dn, precision=HIGHEST, preferred_element_type=jnp.float32)


def split2(x):
    high = x.astype(jnp.bfloat16)
    low = (x - high.astype(jnp.float32)).astype(jnp.bfloat16)
    return high, low


def dot3(left, right, dn):
    a, b = left
    c, d = right
    return bdot(a, c, dn) + (bdot(a, d, dn) + bdot(b, c, dn))


NN = dims(1, 0)
NT = dims(1, 1)
TN = dims(0, 0)


FIRST = ['xyba', 'byax', 'baxy', 'byxa', 'abyx', 'bxay']
FIRST_EVENTS = [(0, 0), (1, 0), (4, 0), (2, 0), (3, 0), (0, 1), (5, 0), (1, 1), (4, 1), (2, 1), (3, 1), (5, 1), (0, 2), (4, 2), (2, 2), (1, 2), (3, 2), (5, 2), (4, 3), (0, 3), (2, 3), (1, 3), (3, 3), (5, 3)]
REST = ['byxa', 'abyx', 'baxy', 'bayx', 'abxy', 'baxy']
BULK = [((0, 1), 'ybxa'), ((1, 2), 'baxy'), ((2, 3), 'bayx'), ((3, 4), 'baxy'), ((4, 6), 'byax'), ((6, 8), 'bxay'), ((8, 10), 'bxya'), ((10, 12), 'abxy'), ((12, 14), 'bayx'), ((14, 16), 'ybxa')]
BULK_START = 3
EVENTS = [(1, 0, 0), (1, 1, 0), (1, 2, 0), (1, 4, 0), (2, 3, 0), (3, 5, 0), (3, 0, 1), (4, 2, 1), (4, 1, 1), (4, 6, 0), (5, 3, 1), (5, 4, 1), (5, 0, 2), (5, 15, 0), (6, 5, 1), (7, 7, 0), (7, 1, 2), (7, 2, 2), (8, 8, 0), (8, 13, 0), (8, 3, 2), (8, 4, 2), (8, 9, 0), (9, 5, 2), (10, 10, 0), (11, 2, 3), (12, 1, 3), (12, 11, 0), (12, 0, 3), (13, 4, 3), (13, 12, 0), (13, 3, 3), (13, 7, 1), (14, 5, 3), (14, 14, 0), (14, 11, 1), (14, 8, 1), (15, 10, 1), (15, 6, 1), (15, 7, 2), (15, 9, 1), (15, 8, 2), (16, 12, 1), (18, 15, 1), (19, 6, 2), (20, 7, 3), (22, 13, 1), (22, 11, 2), (22, 8, 3), (23, 14, 1), (24, 9, 2), (24, 12, 2), (27, 10, 2), (27, 15, 2), (31, 6, 3), (31, 11, 3), (31, 13, 2), (35, 14, 2), (38, 12, 3), (38, 9, 3), (38, 10, 3), (41, 15, 3), (41, 13, 3), (41, 14, 3)]


def inv2(a, b, c):
    ra = 1.0 / a
    t = b * ra
    rs = 1.0 / (c - b * t)
    u = t * rs
    return ra + t * u, -u, rs


def inv4(d):
    a0, a1, a2 = inv2(d[0][0], d[0][1], d[1][1])
    t = [
        [a0 * d[0][2] + a1 * d[1][2], a0 * d[0][3] + a1 * d[1][3]],
        [a1 * d[0][2] + a2 * d[1][2], a1 * d[0][3] + a2 * d[1][3]],
    ]
    s0, s1, s2 = inv2(
        d[2][2] - (d[0][2] * t[0][0] + d[1][2] * t[1][0]),
        d[2][3] - (d[0][2] * t[0][1] + d[1][2] * t[1][1]),
        d[3][3] - (d[0][3] * t[0][1] + d[1][3] * t[1][1]),
    )
    u = [[t[i][0] * s0 + t[i][1] * s1, t[i][0] * s1 + t[i][1] * s2] for i in range(2)]
    e00 = a0 + (u[0][0] * t[0][0] + u[0][1] * t[0][1])
    e01 = a1 + (u[0][0] * t[1][0] + u[0][1] * t[1][1])
    e11 = a2 + (u[1][0] * t[1][0] + u[1][1] * t[1][1])
    return [
        [e00, e01, -u[0][0], -u[0][1]],
        [e01, e11, -u[1][0], -u[1][1]],
        [-u[0][0], -u[1][0], s0, s1],
        [-u[0][1], -u[1][1], s1, s2],
    ]


def spread(x, lane_index):
    return jnp.take_along_axis(x, jnp.full(x.shape, lane_index, jnp.int32), axis=1)


def row(x, i):
    return jnp.broadcast_to(x[i : i + 1], x.shape)


def weigh(weights, values):
    return (weights[0] * values[0] + weights[1] * values[1]) + (weights[2] * values[2] + weights[3] * values[3])


def diag(tile, first, sub):
    e = [spread(tile, first + j) for j in range(4)]
    return [[row(e[j], sub + i) if j >= i else None for j in range(4)] for i in range(4)]


def flat(d):
    return tuple(d[i][j] for i in range(4) for j in range(i, 4))


def unflat(c):
    it = iter(c)
    d = [[None] * 4 for _ in range(4)]
    for i in range(4):
        for j in range(i, 4):
            d[i][j] = next(it)
    return d


def pivot_step(blk, lane, k, sub, d):
    size = blk.shape[0]
    inside = (lane >= k) & (lane < k + 4)
    start = pl.multiple_of(jnp.minimum(k + 4 - (4 - sub) % 8, size - 8), 8)
    skip = (sub + 4) % 8
    g = inv4(d)
    own = blk[pl.ds(pl.multiple_of(k - sub, 8), 8), :]
    near = own if sub == 0 else blk[pl.ds(start, 8), :]
    rows = [jnp.where(lane == k + i, 1.0, jnp.where(inside, 0.0, row(own, sub + i))) for i in range(4)]
    w = [weigh(g[i], rows) for i in range(4)]
    nearc = [spread(near, k + i) for i in range(4)]
    new = jnp.where(inside, 0.0, near) - weigh(nearc, w)
    nd = diag(new, lax.rem(k + 4, size), skip)
    full = blk[...]
    wide = jnp.broadcast_to(inside[0:1], full.shape)
    cols = [jnp.take_along_axis(full, jnp.full(full.shape, k + i, jnp.int32), axis=1) for i in range(4)]
    result = jnp.where(wide, 0.0, full)
    for i in range(4):
        result = result - cols[i] * w[i][0:1]
    blk[...] = result
    for i in range(4):
        blk[pl.ds(k + i, 1), :] = w[i][0:1]
    return nd


def pivots_begin(blk):
    return flat(diag(blk[0:8, :], 0, 0))


def pivots_run(blk, start, stop, carry):
    lane = lax.broadcasted_iota(jnp.int32, (8, blk.shape[1]), 1)
    def body(t, c):
        d = pivot_step(blk, lane, 8 * t, 0, unflat(c))
        d = pivot_step(blk, lane, 8 * t + 4, 4, d)
        return flat(d)
    return lax.fori_loop(start, stop, body, carry)


def invert_small(mat, blk, col, tick):
    order = mat.shape[0]
    count = order // BLOCK
    eye = (
        lax.broadcasted_iota(jnp.int32, (BLOCK, BLOCK), 0)
        == lax.broadcasted_iota(jnp.int32, (BLOCK, BLOCK), 1)
    ).astype(jnp.float32)
    for j in range(count):
        here = pl.ds(j * BLOCK, BLOCK)
        blk[...] = mat[here, here]
        carry = pivots_begin(blk)
        total = BLOCK // 8
        for part in range(4):
            carry = pivots_run(blk, part * total // 4, (part + 1) * total // 4, carry)
            if part < 3:
                tick()
        col[...] = mat[:, here]
        mat[:, here] = jnp.zeros((order, BLOCK), jnp.float32)
        mat[here, here] = eye
        mat[here, :] = xdot(blk[...], mat[here, :], NN)
        for i in range(count):
            if i != j:
                there = pl.ds(i * BLOCK, BLOCK)
                mat[there, :] = mat[there, :] - xdot(col[there, :], mat[here, :], NN)
        tick()


class Gather:
    def __init__(self, ref, lead, block, cols, order, me, n, sends, recvs):
        self.ref, self.lead, self.block, self.cols, self.order = ref, lead, block, cols, order
        self.me, self.n, self.sends, self.recvs = me, n, sends, recvs

    def view(self, stage, arrived):
        m = self.n.bit_length() - 1
        index = []
        for b in range(m - 1, -1, -1):
            bit = 1 << b
            own = (self.me // bit) % 2
            if bit in self.order[:stage]:
                index.append(slice(None))
            elif arrived and bit == self.order[stage]:
                index.append(1 - own)
            else:
                index.append(own)
        blocks = pl.ds(self.block[0], self.block[1] - self.block[0])
        cols = pl.ds(self.cols[0], self.cols[1] - self.cols[0])
        return self.ref.at[(*self.lead, blocks, *index, slice(None), cols)]

    def copy(self, stage):
        piece = self.view(stage, False)
        return pltpu.make_async_remote_copy(
            src_ref=piece,
            dst_ref=piece,
            send_sem=self.sends.at[stage],
            recv_sem=self.recvs.at[stage],
            device_id={"row": flip(self.me, self.order[stage])},
            device_id_type=MESH,
        )


def merge_kernel(
    plan, perm_ref, dtn_ref, z_ref, lift_ref, own_ref, y_ref, gx_ref, bulk_ref,
    small, mat1, mat2, mat3, tee, blk, col, edge, ss, part, rhs, hold,
    fill_sem, send0, recv0, send1, recv1, send2, recv2, core_send, core_recv, swap_send, swap_recv,
):
    n, f, count = plan["n"], plan["f"], plan["count"]
    bits = plan["bits"]
    me = lax.axis_index("row")
    pair = lax.axis_index("box")
    half = lax.rem(pair, 2)
    other = pair + 1 - 2 * half
    yface, free = 3 - half, 2 + half
    spot = [(me // bit) % 2 for bit in bits]

    def at(face):
        return pl.ds(face * f, f) if isinstance(face, int) else pl.ds(pl.multiple_of(face * f, BLOCK), f)

    narrow = [(0, 1, 1), (1, 0, 0), (0, 1, yface), (1, 0, yface), (0, yface, yface), (1, yface, yface)]
    outer = [(0, free, 4, 5), (1, free, 4, 5)]
    wide = [(h, r, c) for h in range(2) for c in outer[h] for r in (1 - h, yface)]
    fills = []
    for b, (h, r, c) in enumerate(narrow):
        fills.append(
            pltpu.make_async_copy(dtn_ref.at[h, r, :, at(c)], small.at[(b, *spot)], fill_sem.at[b])
        )
    for b, (h, r, c) in enumerate(wide):
        fills.append(
            pltpu.make_async_copy(
                dtn_ref.at[h, r, :, at(c)], bulk_ref.at[(0, b, *spot)], fill_sem.at[len(narrow) + b]
            )
        )
    for one in fills:
        one.start()

    barrier = pltpu.get_barrier_semaphore()
    for bit in bits:
        pl.semaphore_signal(barrier, inc=1, device_id={"row": flip(me, bit)}, device_id_type=MESH)
    pl.semaphore_signal(barrier, inc=1, device_id={"box": other}, device_id_type=MESH)
    pl.semaphore_wait(barrier, len(bits) + 1)

    def gathers(ref, lead, chunks, sends, recvs):
        return [
            Gather(ref, lead, block, cols, order, me, n, sends.at[i], recvs.at[i])
            for i, (block, cols, order) in enumerate(chunks)
        ]

    first = gathers(small, (), plan["first"], send0, recv0)
    rest = gathers(small, (), plan["rest"], send1, recv1)
    bulk = gathers(bulk_ref, (0,), plan["bulk"], send2, recv2)
    last = len(bits)

    def cross(i, stage):
        g = bulk[i]
        view = g.view(0, False) if stage < 0 else g.view(stage, True)
        there = Gather(bulk_ref, (1,), g.block, g.cols, g.order, me, n, None, None)
        target = there.view(0, False) if stage < 0 else there.view(stage, True)
        return pltpu.make_async_remote_copy(
            src_ref=view,
            dst_ref=target,
            send_sem=core_send.at[i, stage + 1],
            recv_sem=core_recv.at[i, stage + 1],
            device_id={"box": other},
            device_id_type=MESH,
        )

    def advance(group, i, stage):
        g = group[i]
        if stage > 0:
            g.copy(stage - 1).wait_recv()
        if stage < last:
            g.copy(stage).start()
        if group is bulk:
            cross(i, stage - 1).start()

    events = list(plan["events"])
    groups = {"first": first, "rest": rest, "bulk": bulk}

    def tick():
        if events:
            for name, i, stage in events.pop(0):
                advance(groups[name], i, stage)

    for one in fills[: len(narrow)]:
        one.wait()
    for i in range(len(first)):
        advance(first, i, 0)
    for i, stage in plan["first_events"]:
        advance(first, i, stage + 1)
        if (i, stage) == plan["first_events"][-len(first)]:
            for k in range(len(rest)):
                advance(rest, k, 0)
    for one in fills[len(narrow) :]:
        one.wait()

    def block(b):
        return small[b].reshape(f, f)

    count_f = f // BLOCK
    whole = (perm_ref[...] == lax.broadcasted_iota(jnp.int32, (f, f), 1)).astype(jnp.bfloat16)
    hold[...] = pick_left(whole, block(1))
    mat1[...] = block(0) + pick_right(hold[...], whole, 1)
    tick()
    invert_small(mat1, blk, col, tick)

    edge[:, :f] = block(2)
    edge[:, f:] = pick_left(whole, block(3))

    def rows_of(i):
        return pl.ds(pl.multiple_of(i * BLOCK, BLOCK), BLOCK)

    @pl.loop(0, count_f)
    def _(i):
        gx_ref[0, 0, rows_of(i), :] = xdot(mat1[rows_of(i), :], edge[...], NN)

    tick()

    def swap(b):
        return pltpu.make_async_remote_copy(
            src_ref=ss.at[b],
            dst_ref=part.at[b],
            send_sem=swap_send.at[b],
            recv_sem=swap_recv.at[b],
            device_id={"box": other},
            device_id_type=MESH,
        )

    for b, (i, j) in enumerate([(0, 0), (0, 1), (1, 1)]):

        @pl.loop(0, count_f)
        def _(k):
            left = edge[:, pl.ds(pl.multiple_of(i * f + k * BLOCK, BLOCK), BLOCK)]
            value = -xdot(left, gx_ref[0, 0, :, j * f : (j + 1) * f], TN)
            ss[b, rows_of(k), :] = value

    tick()
    ss[0] = ss[0] + block(4)
    swap(1).start()
    ss[2] = ss[2] + block(5)
    swap(0).start()

    outers = []
    for h in range(2):
        outers.append(
            jnp.concatenate([dtn_ref[h, r, :, pl.ds((1 - h) * f, f)] for r in outer[h]], axis=0)
        )
    swap(2).start()
    m = 4 * count
    joined = jnp.concatenate([outers[0], pick_right(outers[1], whole, 1)], axis=0)
    value = -xdot(joined, mat1[...], NN)
    lift_ref[:, :f] = value
    lift_ref[:, f:] = pick_right(value, whole)
    own_at = pl.ds(pl.multiple_of(me * count, 8), count)
    mine = mat1[own_at, :]
    own_ref[:, :f] = -mine
    own_ref[:, f:] = -pick_right(mine, whole)
    y_ref[...] = -gx_ref[0, 0, own_at, :]
    rhs[: 2 * m, :] = -xdot(joined, gx_ref[0, 0], NN)
    for h in range(2):
        side = jnp.concatenate([dtn_ref[h, r, :, at(yface)] for r in outer[h]], axis=0)
        rhs[h * m : (h + 1) * m, h * f : (h + 1) * f] += side
    rhs[2 * m :, :] = (
        lax.broadcasted_iota(jnp.int32, (count, 2 * f), 1)
        == half * f + me * count + lax.broadcasted_iota(jnp.int32, (count, 2 * f), 0)
    ).astype(jnp.float32)

    @pl.loop(0, count_f)
    def _(i):
        picked = whole_cols(perm_ref, i, f)
        gx_ref[0, 1, rows_of(i), :] = pick_left(picked, gx_ref[0, 0], 0)

    tick()
    swap(0).wait_recv()
    mat2[...] = ss[0] + part[0]
    invert_small(mat2, blk, col, tick)
    gx_copy = pltpu.make_async_remote_copy(
        src_ref=gx_ref.at[0],
        dst_ref=gx_ref.at[1],
        send_sem=swap_send.at[3],
        recv_sem=swap_recv.at[3],
        device_id={"box": other},
        device_id_type=MESH,
    )
    gx_copy.start()
    swap(1).wait_recv()
    hold[...] = ss[1] + part[1]

    @pl.loop(0, count_f)
    def _(i):
        tee[rows_of(i), :] = xdot(mat2[rows_of(i), :], hold[...], NN)

    swap(2).wait_recv()

    @pl.loop(0, count_f)
    def _(i):
        mat3[rows_of(i), :] = (
            ss[2, rows_of(i), :]
            + part[2, rows_of(i), :]
            - xdot(hold[:, rows_of(i)], tee[...], TN)
        )

    tick()
    invert_small(mat3, blk, col, tick)
    left = rhs[:, :f]
    second = xdot(xdot(left, tee[...], NN) - rhs[:, f:], mat3[...], NN)
    z_ref[:, f:] = second
    z_ref[:, :f] = -xdot(left, mat2[...], NN) - xdot(second, tee[...], NT)
    while events:
        tick()
    for b in range(3):
        swap(b).wait_send()
    gx_copy.wait()
    for group in (first, rest, bulk):
        for g in group:
            for stage in range(last):
                g.copy(stage).wait_send()
    for i in range(len(bulk)):
        for stage in range(-1, last):
            cross(i, stage).wait()


def whole_cols(perm_ref, i, f):
    return (
        perm_ref[...] == lax.broadcasted_iota(jnp.int32, (f, BLOCK), 1) + i * BLOCK
    ).astype(jnp.bfloat16)


def product_kernel(
    half_ref, z_ref, lift_ref, own_ref, y_ref, gx_ref, dtn_ref, wide_ref,
    first_ref, second_ref, map_ref, high, low,
):
    step = pl.program_id(0)
    q, h, c = step // 4, (step // 2) % 2, 2 * (step % 2)
    half = half_ref[0]
    rows, f = z_ref.shape[0], z_ref.shape[1] // 2
    count = own_ref.shape[0]
    m = 4 * count

    @pl.when(step % 4 == 0)
    def _():
        z = split2(z_ref[...])
        for k in range(2):
            high[k, :rows, f:], low[k, :rows, f:] = [one[:, k * f : (k + 1) * f] for one in z]
            zero = jnp.zeros((count, f), jnp.bfloat16)
            high[k, rows:, f:], low[k, rows:, f:] = zero, zero
            value = -dot3(z, split2(gx_ref[0, k]), NT)
            high[k, :rows, :f], low[k, :rows, :f] = split2(value)

            @pl.when(q == 0)
            def _():
                a, b = split2(value[: 2 * m] + lift_ref[:, k * f : (k + 1) * f])
                high[k, : 2 * m, :f], low[k, : 2 * m, :f] = a, b

            a, b = split2(own_ref[:, k * f : (k + 1) * f])
            high[k, rows:, :f], low[k, rows:, :f] = a, b

    @pl.when(step == 0)
    def _():
        for k in range(2):
            at = pl.multiple_of((5 * k + 2 - half) * f, BLOCK)
            first_ref[:, pl.ds(at, f)] = y_ref[:, k * f : (k + 1) * f]

    def columns(k):
        return wide_ref[0, 2 * k : 2 * k + 2].reshape(2 * f, f)

    right = split2(jnp.concatenate([columns(0), columns(1)], axis=1))
    res = dot3((high[h], low[h]), right, NN)
    map_ref[...] = res[: 2 * m].reshape(map_ref.shape)
    second_ref[...] = res[2 * m : rows]

    @pl.when(q == 0)
    def _():
        for k in range(2):
            place = c + k
            here = slice(k * f, (k + 1) * f)
            where = 5 * h + jnp.where(place == 0, 0, jnp.where(place == 1, 1 + half, place + 1))
            first_ref[:, pl.ds(pl.multiple_of(where * f, BLOCK), f)] = res[rows:, here]
            face = jnp.where(place == 0, h, jnp.where(place == 1, 2 + half, place + 2))
            cols = pl.ds(pl.multiple_of(face * f, BLOCK), f)
            for i, r in enumerate((h, 2 + half, 4, 5)):
                map_ref[4 * h + i, :, here] += dtn_ref[h, r, :, cols]


def fast_body(dtn, interface_perm):
    _, faces, count, width = dtn.shape
    f = width // faces
    n = lax.axis_size("row")
    bits = []
    bit = n // 2
    while bit:
        bits.append(bit)
        bit //= 2
    last = len(bits)
    tiles = f // BLOCK
    cuts = [(BLOCK * (tiles * i // 3), BLOCK * (tiles * (i + 1) // 3)) for i in range(3)]
    named = dict(zip("bayx", bits))

    def order(letters):
        return [named[one] for one in letters]

    six = [((a, a + 1), cut) for a in range(2) for cut in cuts]
    rest_parts = [((a, a + 2), cut) for a in (2, 4) for cut in cuts]
    events = [[] for _ in range(1 + max(k for k, _, _ in EVENTS))]
    events[BULK_START] = [("bulk", i, 0) for i in range(len(BULK))]
    for k, i, stage in EVENTS:
        if i < len(REST):
            events[k].append(("rest", i, stage + 1))
        else:
            events[k].append(("bulk", i - len(REST), stage + 1))
    nb = len(BULK)
    plan = {
        "n": n,
        "f": f,
        "count": count,
        "bits": bits,
        "first": [(*part, order(o)) for part, o in zip(six, FIRST)],
        "first_events": FIRST_EVENTS,
        "rest": [(*part, order(o)) for part, o in zip(rest_parts, REST)],
        "bulk": [(blocks, (0, f), order(o)) for blocks, o in BULK],
        "events": events,
    }
    split = (2,) * last
    vmem = pl.BlockSpec(memory_space=pltpu.VMEM)
    dma = pltpu.SemaphoreType.DMA
    rows = 9 * count
    f32 = jnp.float32
    z, lift, own, y, gx, bulk_all = pl.pallas_call(
        functools.partial(merge_kernel, plan),
        out_shape=[
            jax.ShapeDtypeStruct(s, f32)
            for s in (
                (rows, 2 * f),
                (8 * count, 2 * f),
                (count, 2 * f),
                (count, 2 * f),
                (2, 2, f, 2 * f),
                (2, 16, *split, count, f),
            )
        ],
        in_specs=[vmem, vmem],
        out_specs=[vmem] * 5 + [pl.BlockSpec(memory_space=pl.ANY)],
        scratch_shapes=[
            pltpu.VMEM((6, *split, count, f), f32),
            pltpu.VMEM((f, f), f32),
            pltpu.VMEM((f, f), f32),
            pltpu.VMEM((f, f), f32),
            pltpu.VMEM((f, f), f32),
            pltpu.VMEM((BLOCK, BLOCK), f32),
            pltpu.VMEM((f, BLOCK), f32),
            pltpu.VMEM((f, 2 * f), f32),
            pltpu.VMEM((3, f, f), f32),
            pltpu.VMEM((3, f, f), f32),
            pltpu.VMEM((rows, 2 * f), f32),
            pltpu.VMEM((f, f), f32),
            dma((22,)),
            dma((6, last)),
            dma((6, last)),
            dma((6, last)),
            dma((6, last)),
            dma((nb, last)),
            dma((nb, last)),
            dma((nb, last + 1)),
            dma((nb, last + 1)),
            dma((4,)),
            dma((4,)),
        ],
        compiler_params=pltpu.CompilerParams(
            collective_id=0, has_side_effects=True, vmem_limit_bytes=48 * 1024 * 1024
        ),
    )(interface_perm[0][:, None], dtn)
    bulk_all = bulk_all.reshape(2, 16, f, f)
    half = (lax.axis_index("box") % 2).astype(jnp.int32)
    lane = 2 * f

    def fixed(shape):
        return pl.BlockSpec(shape, lambda s, r: (0,) * len(shape))

    def column(s, r):
        own_half = r[0]
        return jnp.where(s < 4, own_half, 1 - own_half) * 4 + s % 4

    first, second, merged = pl.pallas_call(
        product_kernel,
        grid_spec=pltpu.PrefetchScalarGridSpec(
            num_scalar_prefetch=1,
            grid=(8,),
            in_specs=[
                fixed((rows, lane)),
                fixed((8 * count, lane)),
                fixed((count, lane)),
                fixed((count, lane)),
                pl.BlockSpec((1, 2, f, lane), lambda s, r: (s // 4, 0, 0, 0)),
                fixed(dtn.shape),
                pl.BlockSpec((1, 4, f, f), lambda s, r: (s // 4, s % 4, 0, 0)),
            ],
            out_specs=[
                fixed((count, 10 * f)),
                pl.BlockSpec((count, lane), lambda s, r: (0, column(s, r))),
                pl.BlockSpec((8, count, lane), lambda s, r: (0, 0, column(s, r))),
            ],
            scratch_shapes=[
                pltpu.VMEM((2, rows + count, 2 * f), jnp.bfloat16),
                pltpu.VMEM((2, rows + count, 2 * f), jnp.bfloat16),
            ],
        ),
        out_shape=[
            jax.ShapeDtypeStruct((count, 10 * f), f32),
            jax.ShapeDtypeStruct((count, 16 * f), f32),
            jax.ShapeDtypeStruct((8, count, 16 * f), f32),
        ],
        compiler_params=pltpu.CompilerParams(vmem_limit_bytes=40 * 1024 * 1024),
    )(half[None], z, lift, own, y, gx, dtn, bulk_all)
    return (first[None], second[None], merged[None])


def solution(mesh):
    def body(dtn, interface_perm):
        n = mesh.shape["row"]
        count = dtn.shape[2]
        if count % 8 == 0 and n == 1 << len(FIRST[0]):
            return fast_body(dtn, interface_perm)
        return plain_body(dtn, interface_perm)

    return jax.shard_map(
        body,
        mesh=mesh,
        in_specs=(P("box", None, "row", None), P("box", None)),
        out_specs=(P("box", "row", None), P("box", "row", None), P("box", None, "row", None)),
        check_vma=False,
    )
```

```python
import functools

import jax
import jax.numpy as jnp
from jax import lax
from jax.experimental import pallas as pl
from jax.experimental.pallas import tpu as pltpu
from jax.sharding import PartitionSpec as P

HIGHEST = lax.Precision.HIGHEST
HIGH = lax.Precision.HIGH
BLOCK = 128
GROUP = 4
MESH = pl.DeviceIdType.MESH


def dot(left, right, precision=HIGHEST):
    return jnp.dot(left, right, precision=precision, preferred_element_type=jnp.float32)


def dot_t(left, right):
    return lax.dot_general(
        left, right, (((0,), (0,)), ((), ())), precision=HIGHEST, preferred_element_type=jnp.float32
    )


def invert_step(blk, lane, g, carry):
    size = blk.shape[0]
    k = g * GROUP
    full = blk[...]
    cols = [
        jnp.take_along_axis(full, jnp.full((size, size), k + i, jnp.int32), axis=1)
        for i in range(GROUP)
    ]
    rows = [blk[pl.ds(k + i, 1), :] for i in range(GROUP)]
    wide = [jnp.broadcast_to(r, (8, size)) for r in rows]
    pivots = [
        [
            jnp.take_along_axis(wide[i], jnp.full((8, size), k + j, jnp.int32), axis=1)
            for j in range(GROUP)
        ]
        for i in range(GROUP)
    ]
    inside = (lane >= k) & (lane < k + GROUP)
    wide = [
        jnp.where(lane == k + i, 1.0, jnp.where(inside, 0.0, wide[i])) for i in range(GROUP)
    ]
    for i in range(GROUP):
        p = 1.0 / pivots[i][i]
        wide[i] = wide[i] * p
        for j in range(i + 1, GROUP):
            pivots[i][j] = pivots[i][j] * p
        for l in range(GROUP):
            if l != i:
                f = pivots[l][i]
                wide[l] = wide[l] - f * wide[i]
                for j in range(i + 1, GROUP):
                    pivots[l][j] = pivots[l][j] - f * pivots[i][j]
    result = jnp.where(inside, 0.0, full)
    for i in range(GROUP):
        result = result - cols[i] * wide[i][0:1]
    blk[...] = result
    for i in range(GROUP):
        blk[pl.ds(k + i, 1), :] = wide[i][0:1]
    return carry


def invert_block(blk):
    size = blk.shape[0]
    lane = lax.broadcasted_iota(jnp.int32, (1, size), 1)
    lax.fori_loop(0, size // GROUP, functools.partial(invert_step, blk, lane), 0)


def invert(mat, blk, col):
    order = mat.shape[0]
    count = order // BLOCK
    eye = (
        lax.broadcasted_iota(jnp.int32, (BLOCK, BLOCK), 0)
        == lax.broadcasted_iota(jnp.int32, (BLOCK, BLOCK), 1)
    ).astype(jnp.float32)

    def outer(j, carry):
        here = pl.ds(pl.multiple_of(j * BLOCK, BLOCK), BLOCK)
        blk[...] = mat[here, here]
        invert_block(blk)
        col[...] = mat[:, here]
        mat[:, here] = jnp.zeros((order, BLOCK), jnp.float32)
        mat[here, here] = eye
        col[here, :] = jnp.zeros((BLOCK, BLOCK), jnp.float32)
        mat[here, :] = dot(blk[...], mat[here, :])

        def inner(i, c):
            there = pl.ds(pl.multiple_of(i * BLOCK, BLOCK), BLOCK)
            mat[there, :] = mat[there, :] - dot(col[there, :], mat[here, :])
            return c

        @pl.loop(0, count)
        def _(i):
            @pl.when(i != j)
            def _():
                inner(i, 0)

        return carry

    lax.fori_loop(0, count, outer, 0)


def first_kernel(perm_ref, small_ref, inv_ref, coupled_ref, own_ref, mat, blk, col):
    f = mat.shape[0]
    count = f // BLOCK

    def block(ref, i):
        return ref[:, i * f : (i + 1) * f]

    def place(rows):
        return (
            perm_ref[rows, :] == lax.broadcasted_iota(jnp.int32, (BLOCK, f), 1)
        ).astype(jnp.float32)

    whole = (perm_ref[...] == lax.broadcasted_iota(jnp.int32, (f, f), 1)).astype(jnp.float32)

    @pl.loop(0, count)
    def _(i):
        here = pl.ds(pl.multiple_of(i * BLOCK, BLOCK), BLOCK)
        moved = dot(place(here), block(small_ref, 1))
        mat[here, :] = small_ref[here, :f] + lax.dot_general(
            moved,
            whole,
            (((1,), (1,)), ((), ())),
            precision=HIGHEST,
            preferred_element_type=jnp.float32,
        )

    invert(mat, blk, col)

    @pl.loop(0, count)
    def _(i):
        here = pl.ds(pl.multiple_of(i * BLOCK, BLOCK), BLOCK)
        inv_ref[here, :f] = mat[here, :]
        inv_ref[here, f:] = dot(mat[here, :], whole)

    @pl.loop(0, count)
    def _(i):
        there = pl.ds(pl.multiple_of(f + i * BLOCK, BLOCK), BLOCK)
        picked = (
            perm_ref[...] == lax.broadcasted_iota(jnp.int32, (f, BLOCK), 1) + i * BLOCK
        ).astype(jnp.float32)
        inv_ref[there, :] = dot_t(picked, inv_ref[:f, :])

    for h in range(2):

        @pl.loop(0, count)
        def _(i):
            here = pl.ds(pl.multiple_of(i * BLOCK, BLOCK), BLOCK)
            rows = pl.ds(pl.multiple_of(h * f + i * BLOCK, BLOCK), BLOCK)
            edge = small_ref[:, pl.ds(pl.multiple_of((2 + h) * f + i * BLOCK, BLOCK), BLOCK)]
            coupled_ref[rows, :] = -dot_t(edge, inv_ref[h * f : (h + 1) * f, :])
            for c in range(2):
                value = dot(coupled_ref[rows, c * f : (c + 1) * f], block(small_ref, 2 + c))
                if c == h:
                    value = value + small_ref[here, (4 + h) * f : (5 + h) * f]
                own_ref[rows, c * f : (c + 1) * f] = value


def second_kernel(own_ref, part_ref, lift_ref, pick_ref, out_ref, mat, blk, col):
    mat[...] = own_ref[...] + part_ref[...]
    invert(mat, blk, col)
    n = lift_ref.shape[0]
    out_ref[:n, :] = dot(lift_ref[...], mat[...])
    out_ref[n:, :] = dot(pick_ref[...], mat[...])


def flip(index, bit):
    return index + bit - 2 * bit * ((index // bit) % 2)


def plan(n, width):
    bits = []
    bit = n // 2
    while bit:
        bits.append(bit)
        bit //= 2
    tiles = width // 128
    first = tiles * 3 // 8
    second = tiles * 3 // 8 + (tiles * 3 % 8 >= 4)
    orders = [bits, bits[:-2] + [1, 2], [1, 2] + bits[:-2]]
    sizes = [first, second, tiles - first - second]
    chunks, at = [], 0
    for order, size in zip(orders, sizes):
        chunks.append((at * 128, size * 128, order))
        at += size
    return bits, chunks


def gather_kernel(n, bits, chunks, x_ref, out_ref, send_sem, recv_sem, own_sem):
    me = lax.axis_index("row")
    barrier = pltpu.get_barrier_semaphore()
    for bit in bits:
        pl.semaphore_signal(
            barrier, inc=1, device_id={"row": flip(me, bit)}, device_id_type=pl.DeviceIdType.MESH
        )
    local = pltpu.make_async_copy(x_ref, out_ref.at[me], own_sem)
    local.start()
    local.wait()
    pl.semaphore_wait(barrier, len(bits))
    pending = [[] for _ in chunks]
    sent = []
    held = [[()] for _ in chunks]
    for t in range(len(bits)):
        for c, (start, size, order) in enumerate(chunks):
            for copy in pending[c]:
                copy.wait_recv()
            pending[c] = []
            bit = order[t]
            for s in held[c]:
                slot = me
                for one in s:
                    slot = flip(slot, one)
                number = (1 << t) - 1 + len(pending[c])
                piece = out_ref.at[slot, :, pl.ds(start, size)]
                copy = pltpu.make_async_remote_copy(
                    src_ref=piece,
                    dst_ref=piece,
                    send_sem=send_sem.at[c, number],
                    recv_sem=recv_sem.at[c, number],
                    device_id={"row": flip(me, bit)},
                    device_id_type=pl.DeviceIdType.MESH,
                )
                copy.start()
                pending[c].append(copy)
                sent.append(copy)
            held[c] = held[c] + [s + (bit,) for s in held[c]]
    for c in range(len(chunks)):
        for copy in pending[c]:
            copy.wait_recv()
    for copy in sent:
        copy.wait_send()


def quick_gather(x):
    n = lax.axis_size("row")
    count, width = x.shape
    bits, chunks = plan(n, width)
    out = pl.pallas_call(
        functools.partial(gather_kernel, n, bits, chunks),
        out_shape=jax.ShapeDtypeStruct((n, count, width), jnp.float32),
        in_specs=[pl.BlockSpec(memory_space=pltpu.VMEM)],
        out_specs=pl.BlockSpec(memory_space=pltpu.VMEM),
        scratch_shapes=[
            pltpu.SemaphoreType.DMA((len(chunks), n - 1)),
            pltpu.SemaphoreType.DMA((len(chunks), n - 1)),
            pltpu.SemaphoreType.DMA,
        ],
        compiler_params=pltpu.CompilerParams(
            collective_id=0, has_side_effects=True, vmem_limit_bytes=16 * 1024 * 1024
        ),
        cost_estimate=pl.CostEstimate(
            flops=10_000_000_000, bytes_accessed=2 * n * count * width * 4, transcendentals=0
        ),
    )(x)
    return out.reshape(n * count, width)


def call(kernel, out, order, *args):
    return pl.pallas_call(
        kernel,
        out_shape=[jax.ShapeDtypeStruct(o, jnp.float32) for o in out],
        in_specs=[pl.BlockSpec(memory_space=pltpu.VMEM)] * len(args),
        out_specs=[pl.BlockSpec(memory_space=pltpu.VMEM)] * len(out),
        scratch_shapes=[
            pltpu.VMEM((order, order), jnp.float32),
            pltpu.VMEM((BLOCK, BLOCK), jnp.float32),
            pltpu.VMEM((order, BLOCK), jnp.float32),
        ],
        compiler_params=pltpu.CompilerParams(vmem_limit_bytes=40 * 1024 * 1024),
        cost_estimate=pl.CostEstimate(
            flops=order * 20_000_000, bytes_accessed=order * order * 8, transcendentals=0
        ),
    )(*args)


def plain_body(dtn, interface_perm):
    a, b = dtn[0], dtn[1]
    count = a.shape[1]
    f = a.shape[2] // 6
    perm = interface_perm[0]
    rank = lax.axis_index("row")
    half = lax.axis_index("box") % 2
    first = half == 0

    def swap(x):
        n = lax.axis_size("box")
        return lax.ppermute(x, "box", [(i, i ^ 1) for i in range(n)])

    def gather(x):
        return lax.all_gather(x, "row", axis=0, tiled=True)

    def cols(x, face):
        return x[..., face * f : (face + 1) * f]

    def side(x):
        return jnp.where(first, cols(x, 3), cols(x, 2))

    def free(x):
        return jnp.where(first, cols(x, 2), cols(x, 3))

    def outer_cols(x, edge):
        return jnp.concatenate([cols(x, edge), free(x), cols(x, 4), cols(x, 5)], axis=-1)

    ay, by = jnp.where(first, a[3], a[2]), jnp.where(first, b[3], b[2])
    a1, b0 = a[1], b[0]
    small = quick_gather(
        jnp.concatenate(
            [cols(a1, 1), cols(b0, 0), side(a1), side(b0), side(ay), side(by)], axis=1
        )
    )
    bulk = gather(
        jnp.concatenate(
            [outer_cols(a1, 0), outer_cols(ay, 0), outer_cols(b0, 1), outer_cols(by, 1)], axis=1
        )
    )
    inv1, coupled, own_ss = call(first_kernel, [(2 * f, 2 * f)] * 3, f, perm[:, None], small)
    a1y, b0y = small[:, 2 * f : 3 * f], small[:, 3 * f : 4 * f]

    def times_side(x):
        return jnp.concatenate([dot(x[:, :f], a1y), dot(x[:, f:], b0y)], axis=1)

    part_ss = swap(own_ss)
    outer_a = jnp.concatenate(
        [a[0], jnp.where(first, a[2], a[3]), a[4], a[5]], axis=0
    )
    outer_b = jnp.concatenate(
        [b[1], jnp.where(first, b[2], b[3]), b[4], b[5]], axis=0
    )
    lift = -jnp.concatenate(
        [dot(cols(outer_a, 1), inv1[:f]), dot(cols(outer_b, 0), inv1[f:])], axis=0
    )
    n = 4 * count
    zero_n = jnp.zeros((n, f), jnp.float32)
    lift_two = times_side(lift) + jnp.concatenate(
        [
            jnp.concatenate([side(outer_a), zero_n], axis=1),
            jnp.concatenate([zero_n, side(outer_b)], axis=1),
        ],
        axis=0,
    )
    start = rank * count
    pick = (
        jnp.arange(2 * f, dtype=jnp.int32)[None, :]
        == half * f + start + jnp.arange(count, dtype=jnp.int32)[:, None]
    ).astype(jnp.float32)
    own_rows = lax.dynamic_slice(inv1, (start, 0), (count, 2 * f))
    z = -call(second_kernel, [(2 * n + count, 2 * f)], 2 * f, own_ss, part_ss, lift_two, pick)[0]
    z_part = swap(z)
    both = jnp.concatenate([z_part, z], axis=0)
    through = dot(both, coupled)
    m = 2 * n + count
    through = jnp.concatenate(
        [through[:m], through[m : m + 2 * n] + lift, through[m + 2 * n :], -own_rows], axis=0
    )
    both = jnp.concatenate([both, jnp.zeros((count, 2 * f), jnp.float32)], axis=0)
    w = 4 * f
    res_a = dot(through[:, :f], bulk[:, :w], HIGH) + dot(both[:, :f], bulk[:, w : 2 * w], HIGH)
    res_b = dot(through[:, f:], bulk[:, 2 * w : 3 * w], HIGH) + dot(both[:, f:], bulk[:, 3 * w :], HIGH)
    results = jnp.concatenate([res_a, res_b], axis=1)
    cross = swap(results[:m])
    own = results[m : 2 * m]
    base = jnp.concatenate(
        [
            jnp.concatenate([outer_cols(outer_a, 0), jnp.zeros((n, w), jnp.float32)], axis=1),
            jnp.concatenate([jnp.zeros((n, w), jnp.float32), outer_cols(outer_b, 1)], axis=1),
        ],
        axis=0,
    )
    own_map = own[: 2 * n] + base
    left = jnp.where(first, own_map, cross[: 2 * n])
    right = jnp.where(first, cross[: 2 * n], own_map)
    merged_map = jnp.concatenate([left, right], axis=1).reshape(1, 8, count, 4 * w)
    own_s, cross_s = own[2 * n :], cross[2 * n :]
    second = jnp.concatenate(
        [jnp.where(first, own_s, cross_s), jnp.where(first, cross_s, own_s)], axis=1
    )
    s1 = results[2 * m :]
    y_a, y_b = -dot(own_rows[:, :f], a1y), -dot(own_rows[:, f:], b0y)

    def ordered(x, y):
        two = jnp.where(first, cols(x, 1), y)
        three = jnp.where(first, y, cols(x, 1))
        return [cols(x, 0), two, three, x[:, 2 * f :]]

    solution_first = jnp.concatenate(ordered(s1[:, :w], y_a) + ordered(s1[:, w:], y_b), axis=1)
    return (solution_first[None], second[None], merged_map)


def split3(x):
    high = x.astype(jnp.bfloat16)
    rest = x - high.astype(jnp.float32)
    mid = rest.astype(jnp.bfloat16)
    low = (rest - mid.astype(jnp.float32)).astype(jnp.bfloat16)
    return high, mid, low


def dims(left, right):
    return (((left,), (right,)), ((), ()))


def bdot(left, right, dn):
    return lax.dot_general(left, right, dn, preferred_element_type=jnp.float32)


def pick_left(onehot, x, contract=1):
    return sum(bdot(onehot, part, dims(contract, 0)) for part in split3(x))


def pick_right(x, onehot, contract=0):
    return sum(bdot(part, onehot, dims(1, contract)) for part in split3(x))


def xdot(left, right, dn):
    return lax.dot_general(left, right, dn, precision=HIGHEST, preferred_element_type=jnp.float32)


def split2(x):
    high = x.astype(jnp.bfloat16)
    low = (x - high.astype(jnp.float32)).astype(jnp.bfloat16)
    return high, low


def dot3(left, right, dn):
    a, b = left
    c, d = right
    return bdot(a, c, dn) + (bdot(a, d, dn) + bdot(b, c, dn))


NN = dims(1, 0)
NT = dims(1, 1)
TN = dims(0, 0)


FIRST = ['xyba', 'byax', 'baxy', 'byxa', 'abyx', 'bxay']
FIRST_EVENTS = [(0, 0), (1, 0), (4, 0), (2, 0), (3, 0), (0, 1), (5, 0), (1, 1), (4, 1), (2, 1), (3, 1), (5, 1), (0, 2), (4, 2), (2, 2), (1, 2), (3, 2), (5, 2), (4, 3), (0, 3), (2, 3), (1, 3), (3, 3), (5, 3)]
REST = ['byxa', 'abyx', 'baxy', 'bayx', 'abxy', 'baxy']
BULK = [((0, 1), 'ybxa'), ((1, 2), 'baxy'), ((2, 3), 'bayx'), ((3, 4), 'baxy'), ((4, 6), 'byax'), ((6, 8), 'bxay'), ((8, 10), 'bxya'), ((10, 12), 'abxy'), ((12, 14), 'bayx'), ((14, 16), 'ybxa')]
BULK_START = 3
EVENTS = [(1, 0, 0), (1, 1, 0), (1, 2, 0), (1, 4, 0), (2, 3, 0), (3, 5, 0), (3, 0, 1), (4, 2, 1), (4, 1, 1), (4, 6, 0), (5, 3, 1), (5, 4, 1), (5, 0, 2), (5, 15, 0), (6, 5, 1), (7, 7, 0), (7, 1, 2), (7, 2, 2), (8, 8, 0), (8, 13, 0), (8, 3, 2), (8, 4, 2), (8, 9, 0), (9, 5, 2), (10, 10, 0), (11, 2, 3), (12, 1, 3), (12, 11, 0), (12, 0, 3), (13, 4, 3), (13, 12, 0), (13, 3, 3), (13, 7, 1), (14, 5, 3), (14, 14, 0), (14, 11, 1), (14, 8, 1), (15, 10, 1), (15, 6, 1), (15, 7, 2), (15, 9, 1), (15, 8, 2), (16, 12, 1), (18, 15, 1), (19, 6, 2), (20, 7, 3), (22, 13, 1), (22, 11, 2), (22, 8, 3), (23, 14, 1), (24, 9, 2), (24, 12, 2), (27, 10, 2), (27, 15, 2), (31, 6, 3), (31, 11, 3), (31, 13, 2), (35, 14, 2), (38, 12, 3), (38, 9, 3), (38, 10, 3), (41, 15, 3), (41, 13, 3), (41, 14, 3)]


def inv2(a, b, c):
    ra = 1.0 / a
    t = b * ra
    rs = 1.0 / (c - b * t)
    u = t * rs
    return ra + t * u, -u, rs


def inv4(d):
    a0, a1, a2 = inv2(d[0][0], d[0][1], d[1][1])
    t = [
        [a0 * d[0][2] + a1 * d[1][2], a0 * d[0][3] + a1 * d[1][3]],
        [a1 * d[0][2] + a2 * d[1][2], a1 * d[0][3] + a2 * d[1][3]],
    ]
    s0, s1, s2 = inv2(
        d[2][2] - (d[0][2] * t[0][0] + d[1][2] * t[1][0]),
        d[2][3] - (d[0][2] * t[0][1] + d[1][2] * t[1][1]),
        d[3][3] - (d[0][3] * t[0][1] + d[1][3] * t[1][1]),
    )
    u = [[t[i][0] * s0 + t[i][1] * s1, t[i][0] * s1 + t[i][1] * s2] for i in range(2)]
    e00 = a0 + (u[0][0] * t[0][0] + u[0][1] * t[0][1])
    e01 = a1 + (u[0][0] * t[1][0] + u[0][1] * t[1][1])
    e11 = a2 + (u[1][0] * t[1][0] + u[1][1] * t[1][1])
    return [
        [e00, e01, -u[0][0], -u[0][1]],
        [e01, e11, -u[1][0], -u[1][1]],
        [-u[0][0], -u[1][0], s0, s1],
        [-u[0][1], -u[1][1], s1, s2],
    ]


def spread(x, lane_index):
    return jnp.take_along_axis(x, jnp.full(x.shape, lane_index, jnp.int32), axis=1)


def row(x, i):
    return jnp.broadcast_to(x[i : i + 1], x.shape)


def weigh(weights, values):
    return (weights[0] * values[0] + weights[1] * values[1]) + (weights[2] * values[2] + weights[3] * values[3])


def diag(tile, first, sub):
    e = [spread(tile, first + j) for j in range(4)]
    return [[row(e[j], sub + i) if j >= i else None for j in range(4)] for i in range(4)]


def flat(d):
    return tuple(d[i][j] for i in range(4) for j in range(i, 4))


def unflat(c):
    it = iter(c)
    d = [[None] * 4 for _ in range(4)]
    for i in range(4):
        for j in range(i, 4):
            d[i][j] = next(it)
    return d


def pivot_step(blk, lane, k, sub, d):
    size = blk.shape[0]
    inside = (lane >= k) & (lane < k + 4)
    start = pl.multiple_of(jnp.minimum(k + 4 - (4 - sub) % 8, size - 8), 8)
    skip = (sub + 4) % 8
    g = inv4(d)
    own = blk[pl.ds(pl.multiple_of(k - sub, 8), 8), :]
    near = own if sub == 0 else blk[pl.ds(start, 8), :]
    rows = [jnp.where(lane == k + i, 1.0, jnp.where(inside, 0.0, row(own, sub + i))) for i in range(4)]
    w = [weigh(g[i], rows) for i in range(4)]
    nearc = [spread(near, k + i) for i in range(4)]
    new = jnp.where(inside, 0.0, near) - weigh(nearc, w)
    nd = diag(new, lax.rem(k + 4, size), skip)
    full = blk[...]
    wide = jnp.broadcast_to(inside[0:1], full.shape)
    cols = [jnp.take_along_axis(full, jnp.full(full.shape, k + i, jnp.int32), axis=1) for i in range(4)]
    result = jnp.where(wide, 0.0, full)
    for i in range(4):
        result = result - cols[i] * w[i][0:1]
    blk[...] = result
    for i in range(4):
        blk[pl.ds(k + i, 1), :] = w[i][0:1]
    return nd


def pivots_begin(blk):
    return flat(diag(blk[0:8, :], 0, 0))


def pivots_run(blk, start, stop, carry):
    lane = lax.broadcasted_iota(jnp.int32, (8, blk.shape[1]), 1)
    def body(t, c):
        d = pivot_step(blk, lane, 8 * t, 0, unflat(c))
        d = pivot_step(blk, lane, 8 * t + 4, 4, d)
        return flat(d)
    return lax.fori_loop(start, stop, body, carry)


def invert_small(mat, blk, col, tick):
    order = mat.shape[0]
    count = order // BLOCK
    eye = (
        lax.broadcasted_iota(jnp.int32, (BLOCK, BLOCK), 0)
        == lax.broadcasted_iota(jnp.int32, (BLOCK, BLOCK), 1)
    ).astype(jnp.float32)
    for j in range(count):
        here = pl.ds(j * BLOCK, BLOCK)
        blk[...] = mat[here, here]
        carry = pivots_begin(blk)
        total = BLOCK // 8
        for part in range(4):
            carry = pivots_run(blk, part * total // 4, (part + 1) * total // 4, carry)
            if part < 3:
                tick()
        col[...] = mat[:, here]
        mat[:, here] = jnp.zeros((order, BLOCK), jnp.float32)
        mat[here, here] = eye
        mat[here, :] = xdot(blk[...], mat[here, :], NN)
        for i in range(count):
            if i != j:
                there = pl.ds(i * BLOCK, BLOCK)
                mat[there, :] = mat[there, :] - xdot(col[there, :], mat[here, :], NN)
        tick()


class Gather:
    def __init__(self, ref, lead, block, cols, order, me, n, sends, recvs):
        self.ref, self.lead, self.block, self.cols, self.order = ref, lead, block, cols, order
        self.me, self.n, self.sends, self.recvs = me, n, sends, recvs

    def view(self, stage, arrived):
        m = self.n.bit_length() - 1
        index = []
        for b in range(m - 1, -1, -1):
            bit = 1 << b
            own = (self.me // bit) % 2
            if bit in self.order[:stage]:
                index.append(slice(None))
            elif arrived and bit == self.order[stage]:
                index.append(1 - own)
            else:
                index.append(own)
        blocks = pl.ds(self.block[0], self.block[1] - self.block[0])
        cols = pl.ds(self.cols[0], self.cols[1] - self.cols[0])
        return self.ref.at[(*self.lead, blocks, *index, slice(None), cols)]

    def copy(self, stage):
        piece = self.view(stage, False)
        return pltpu.make_async_remote_copy(
            src_ref=piece,
            dst_ref=piece,
            send_sem=self.sends.at[stage],
            recv_sem=self.recvs.at[stage],
            device_id={"row": flip(self.me, self.order[stage])},
            device_id_type=MESH,
        )


def merge_kernel(
    plan, perm_ref, dtn_any, z_ref, lift_ref, own_ref, y_ref, gx_ref, bulk_ref,
    small, mat1, mat2, mat3, tee, blk, col, edge, ss, part, rhs, hold, dtn_ref,
    fill_sem, send0, recv0, send1, recv1, send2, recv2, core_send, core_recv, swap_send, swap_recv,
):
    n, f, count = plan["n"], plan["f"], plan["count"]
    bits = plan["bits"]
    me = lax.axis_index("row")
    pair = lax.axis_index("box")
    half = lax.rem(pair, 2)
    other = pair + 1 - 2 * half
    yface, free = 3 - half, 2 + half
    spot = [(me // bit) % 2 for bit in bits]

    def at(face):
        return pl.ds(face * f, f) if isinstance(face, int) else pl.ds(pl.multiple_of(face * f, BLOCK), f)

    narrow = [(0, 1, 1), (1, 0, 0), (0, 1, yface), (1, 0, yface), (0, yface, yface), (1, yface, yface)]
    outer = [(0, free, 4, 5), (1, free, 4, 5)]
    wide = [(h, r, c) for h in range(2) for c in outer[h] for r in (1 - h, yface)]
    fills = []
    for b, (h, r, c) in enumerate(narrow):
        fills.append(
            pltpu.make_async_copy(dtn_any.at[h, r, :, at(c)], small.at[(b, *spot)], fill_sem.at[b])
        )
    for b, (h, r, c) in enumerate(wide):
        fills.append(
            pltpu.make_async_copy(
                dtn_ref.at[h, r, :, at(c)], bulk_ref.at[(0, b, *spot)], fill_sem.at[len(narrow) + b]
            )
        )
    load = pltpu.make_async_copy(dtn_any, dtn_ref, fill_sem.at[len(narrow) + len(wide)])
    for one in fills[: len(narrow)]:
        one.start()
    load.start()

    barrier = pltpu.get_barrier_semaphore()
    for bit in bits:
        pl.semaphore_signal(barrier, inc=1, device_id={"row": flip(me, bit)}, device_id_type=MESH)
    pl.semaphore_signal(barrier, inc=1, device_id={"box": other}, device_id_type=MESH)
    pl.semaphore_wait(barrier, len(bits) + 1)

    def gathers(ref, lead, chunks, sends, recvs):
        return [
            Gather(ref, lead, block, cols, order, me, n, sends.at[i], recvs.at[i])
            for i, (block, cols, order) in enumerate(chunks)
        ]

    first = gathers(small, (), plan["first"], send0, recv0)
    rest = gathers(small, (), plan["rest"], send1, recv1)
    bulk = gathers(bulk_ref, (0,), plan["bulk"], send2, recv2)
    last = len(bits)

    def cross(i, stage):
        g = bulk[i]
        view = g.view(0, False) if stage < 0 else g.view(stage, True)
        there = Gather(bulk_ref, (1,), g.block, g.cols, g.order, me, n, None, None)
        target = there.view(0, False) if stage < 0 else there.view(stage, True)
        return pltpu.make_async_remote_copy(
            src_ref=view,
            dst_ref=target,
            send_sem=core_send.at[i, stage + 1],
            recv_sem=core_recv.at[i, stage + 1],
            device_id={"box": other},
            device_id_type=MESH,
        )

    def advance(group, i, stage):
        g = group[i]
        if stage > 0:
            g.copy(stage - 1).wait_recv()
        if stage < last:
            g.copy(stage).start()
        if group is bulk:
            cross(i, stage - 1).start()

    events = list(plan["events"])
    groups = {"first": first, "rest": rest, "bulk": bulk}

    def tick():
        if events:
            for name, i, stage in events.pop(0):
                advance(groups[name], i, stage)

    for one in fills[: len(narrow)]:
        one.wait()
    for i in range(len(first)):
        advance(first, i, 0)
    for i, stage in plan["first_events"]:
        advance(first, i, stage + 1)
        if (i, stage) == plan["first_events"][-len(first)]:
            for k in range(len(rest)):
                advance(rest, k, 0)
    load.wait()
    for one in fills[len(narrow) :]:
        one.start()
    for one in fills[len(narrow) :]:
        one.wait()

    def block(b):
        return small[b].reshape(f, f)

    count_f = f // BLOCK
    whole = (perm_ref[...] == lax.broadcasted_iota(jnp.int32, (f, f), 0)).astype(jnp.bfloat16)
    hold[...] = pick_left(whole, block(1), 0)
    mat1[...] = block(0) + pick_right(hold[...], whole)
    tick()
    invert_small(mat1, blk, col, tick)

    edge[:, :f] = block(2)
    edge[:, f:] = pick_left(whole, block(3), 0)

    def rows_of(i):
        return pl.ds(pl.multiple_of(i * BLOCK, BLOCK), BLOCK)

    @pl.loop(0, count_f)
    def _(i):
        gx_ref[0, 0, rows_of(i), :] = xdot(mat1[rows_of(i), :], edge[...], NN)

    tick()

    def swap(b):
        return pltpu.make_async_remote_copy(
            src_ref=ss.at[b],
            dst_ref=part.at[b],
            send_sem=swap_send.at[b],
            recv_sem=swap_recv.at[b],
            device_id={"box": other},
            device_id_type=MESH,
        )

    for b, (i, j) in enumerate([(0, 0), (0, 1), (1, 1)]):

        @pl.loop(0, count_f)
        def _(k):
            left = edge[:, pl.ds(pl.multiple_of(i * f + k * BLOCK, BLOCK), BLOCK)]
            value = -xdot(left, gx_ref[0, 0, :, j * f : (j + 1) * f], TN)
            ss[b, rows_of(k), :] = value

    tick()
    ss[0] = ss[0] + block(4)
    swap(1).start()
    ss[2] = ss[2] + block(5)
    swap(0).start()

    outers = []
    for h in range(2):
        outers.append(
            jnp.concatenate([dtn_ref[h, r, :, pl.ds((1 - h) * f, f)] for r in outer[h]], axis=0)
        )
    swap(2).start()
    m = 4 * count
    joined = jnp.concatenate([outers[0], pick_right(outers[1], whole)], axis=0)
    value = -xdot(joined, mat1[...], NN)
    lift_ref[:, :f] = value
    lift_ref[:, f:] = pick_right(value, whole, 1)
    own_at = pl.ds(pl.multiple_of(me * count, 8), count)
    mine = mat1[own_at, :]
    own_ref[:, :f] = -mine
    own_ref[:, f:] = -pick_right(mine, whole, 1)
    y_ref[...] = -gx_ref[0, 0, own_at, :]
    rhs[: 2 * m, :] = -xdot(joined, gx_ref[0, 0], NN)
    for h in range(2):
        side = jnp.concatenate([dtn_ref[h, r, :, at(yface)] for r in outer[h]], axis=0)
        rhs[h * m : (h + 1) * m, h * f : (h + 1) * f] += side
    rhs[2 * m :, :] = (
        lax.broadcasted_iota(jnp.int32, (count, 2 * f), 1)
        == half * f + me * count + lax.broadcasted_iota(jnp.int32, (count, 2 * f), 0)
    ).astype(jnp.float32)

    @pl.loop(0, count_f)
    def _(i):
        picked = (
            perm_ref[...] == lax.broadcasted_iota(jnp.int32, (BLOCK, f), 0) + i * BLOCK
        ).astype(jnp.bfloat16)
        gx_ref[0, 1, rows_of(i), :] = pick_left(picked, gx_ref[0, 0])

    tick()
    swap(0).wait_recv()
    mat2[...] = ss[0] + part[0]
    invert_small(mat2, blk, col, tick)
    gx_copy = pltpu.make_async_remote_copy(
        src_ref=gx_ref.at[0],
        dst_ref=gx_ref.at[1],
        send_sem=swap_send.at[3],
        recv_sem=swap_recv.at[3],
        device_id={"box": other},
        device_id_type=MESH,
    )
    gx_copy.start()
    swap(1).wait_recv()
    hold[...] = ss[1] + part[1]

    @pl.loop(0, count_f)
    def _(i):
        tee[rows_of(i), :] = xdot(mat2[rows_of(i), :], hold[...], NN)

    swap(2).wait_recv()

    @pl.loop(0, count_f)
    def _(i):
        mat3[rows_of(i), :] = (
            ss[2, rows_of(i), :]
            + part[2, rows_of(i), :]
            - xdot(hold[:, rows_of(i)], tee[...], TN)
        )

    tick()
    invert_small(mat3, blk, col, tick)
    left = rhs[:, :f]
    second = xdot(xdot(left, tee[...], NN) - rhs[:, f:], mat3[...], NN)
    z_ref[:, f:] = second
    z_ref[:, :f] = -xdot(left, mat2[...], NN) - xdot(second, tee[...], NT)
    while events:
        tick()
    for b in range(3):
        swap(b).wait_send()
    gx_copy.wait()
    for group in (first, rest, bulk):
        for g in group:
            for stage in range(last):
                g.copy(stage).wait_send()
    for i in range(len(bulk)):
        for stage in range(-1, last):
            cross(i, stage).wait()


def product_kernel(
    half_ref, z_ref, lift_ref, own_ref, y_ref, gx_ref, dtn_ref, wide_ref,
    first_ref, second_ref, map_ref, high, low,
):
    step = pl.program_id(0)
    q, h, c = step // 4, (step // 2) % 2, 2 * (step % 2)
    half = half_ref[0]
    rows, f = z_ref.shape[0], z_ref.shape[1] // 2
    count = own_ref.shape[0]
    m = 4 * count

    @pl.when(step % 4 == 0)
    def _():
        z = split2(z_ref[...])
        for k in range(2):
            high[k, :rows, f:], low[k, :rows, f:] = [one[:, k * f : (k + 1) * f] for one in z]
            zero = jnp.zeros((count, f), jnp.bfloat16)
            high[k, rows:, f:], low[k, rows:, f:] = zero, zero
            value = -dot3(z, split2(gx_ref[0, k]), NT)
            high[k, :rows, :f], low[k, :rows, :f] = split2(value)

            @pl.when(q == 0)
            def _():
                a, b = split2(value[: 2 * m] + lift_ref[:, k * f : (k + 1) * f])
                high[k, : 2 * m, :f], low[k, : 2 * m, :f] = a, b

            a, b = split2(own_ref[:, k * f : (k + 1) * f])
            high[k, rows:, :f], low[k, rows:, :f] = a, b

    @pl.when(step == 0)
    def _():
        for k in range(2):
            at = pl.multiple_of((5 * k + 2 - half) * f, BLOCK)
            first_ref[:, pl.ds(at, f)] = y_ref[:, k * f : (k + 1) * f]

    def columns(k):
        return wide_ref[0, 2 * k : 2 * k + 2].reshape(2 * f, f)

    right = split2(jnp.concatenate([columns(0), columns(1)], axis=1))
    res = dot3((high[h], low[h]), right, NN)
    map_ref[...] = res[: 2 * m].reshape(map_ref.shape)
    second_ref[...] = res[2 * m : rows]

    @pl.when(q == 0)
    def _():
        for k in range(2):
            place = c + k
            here = slice(k * f, (k + 1) * f)
            where = 5 * h + jnp.where(place == 0, 0, jnp.where(place == 1, 1 + half, place + 1))
            first_ref[:, pl.ds(pl.multiple_of(where * f, BLOCK), f)] = res[rows:, here]
            face = jnp.where(place == 0, h, jnp.where(place == 1, 2 + half, place + 2))
            cols = pl.ds(pl.multiple_of(face * f, BLOCK), f)
            for i, r in enumerate((h, 2 + half, 4, 5)):
                map_ref[4 * h + i, :, here] += dtn_ref[h, r, :, cols]


def fast_body(dtn, interface_perm):
    _, faces, count, width = dtn.shape
    f = width // faces
    n = lax.axis_size("row")
    bits = []
    bit = n // 2
    while bit:
        bits.append(bit)
        bit //= 2
    last = len(bits)
    tiles = f // BLOCK
    cuts = [(BLOCK * (tiles * i // 3), BLOCK * (tiles * (i + 1) // 3)) for i in range(3)]
    named = dict(zip("bayx", bits))

    def order(letters):
        return [named[one] for one in letters]

    six = [((a, a + 1), cut) for a in range(2) for cut in cuts]
    rest_parts = [((a, a + 2), cut) for a in (2, 4) for cut in cuts]
    events = [[] for _ in range(1 + max(k for k, _, _ in EVENTS))]
    events[BULK_START] = [("bulk", i, 0) for i in range(len(BULK))]
    for k, i, stage in EVENTS:
        if i < len(REST):
            events[k].append(("rest", i, stage + 1))
        else:
            events[k].append(("bulk", i - len(REST), stage + 1))
    nb = len(BULK)
    plan = {
        "n": n,
        "f": f,
        "count": count,
        "bits": bits,
        "first": [(*part, order(o)) for part, o in zip(six, FIRST)],
        "first_events": FIRST_EVENTS,
        "rest": [(*part, order(o)) for part, o in zip(rest_parts, REST)],
        "bulk": [(blocks, (0, f), order(o)) for blocks, o in BULK],
        "events": events,
    }
    split = (2,) * last
    vmem = pl.BlockSpec(memory_space=pltpu.VMEM)
    dma = pltpu.SemaphoreType.DMA
    rows = 9 * count
    f32 = jnp.float32
    z, lift, own, y, gx, bulk_all = pl.pallas_call(
        functools.partial(merge_kernel, plan),
        out_shape=[
            jax.ShapeDtypeStruct(s, f32)
            for s in (
                (rows, 2 * f),
                (8 * count, 2 * f),
                (count, 2 * f),
                (count, 2 * f),
                (2, 2, f, 2 * f),
                (2, 16, *split, count, f),
            )
        ],
        in_specs=[vmem, pl.BlockSpec(memory_space=pl.ANY)],
        out_specs=[vmem] * 5 + [pl.BlockSpec(memory_space=pl.ANY)],
        scratch_shapes=[
            pltpu.VMEM((6, *split, count, f), f32),
            pltpu.VMEM((f, f), f32),
            pltpu.VMEM((f, f), f32),
            pltpu.VMEM((f, f), f32),
            pltpu.VMEM((f, f), f32),
            pltpu.VMEM((BLOCK, BLOCK), f32),
            pltpu.VMEM((f, BLOCK), f32),
            pltpu.VMEM((f, 2 * f), f32),
            pltpu.VMEM((3, f, f), f32),
            pltpu.VMEM((3, f, f), f32),
            pltpu.VMEM((rows, 2 * f), f32),
            pltpu.VMEM((f, f), f32),
            pltpu.VMEM(dtn.shape, f32),
            dma((23,)),
            dma((6, last)),
            dma((6, last)),
            dma((6, last)),
            dma((6, last)),
            dma((nb, last)),
            dma((nb, last)),
            dma((nb, last + 1)),
            dma((nb, last + 1)),
            dma((4,)),
            dma((4,)),
        ],
        compiler_params=pltpu.CompilerParams(
            collective_id=0, has_side_effects=True, vmem_limit_bytes=67_043_328
        ),
    )(interface_perm, dtn)
    bulk_all = bulk_all.reshape(2, 16, f, f)
    half = (lax.axis_index("box") % 2).astype(jnp.int32)
    lane = 2 * f

    def fixed(shape):
        return pl.BlockSpec(shape, lambda s, r: (0,) * len(shape))

    def column(s, r):
        own_half = r[0]
        return jnp.where(s < 4, own_half, 1 - own_half) * 4 + s % 4

    first, second, merged = pl.pallas_call(
        product_kernel,
        grid_spec=pltpu.PrefetchScalarGridSpec(
            num_scalar_prefetch=1,
            grid=(8,),
            in_specs=[
                fixed((rows, lane)),
                fixed((8 * count, lane)),
                fixed((count, lane)),
                fixed((count, lane)),
                pl.BlockSpec((1, 2, f, lane), lambda s, r: (s // 4, 0, 0, 0)),
                fixed(dtn.shape),
                pl.BlockSpec((1, 4, f, f), lambda s, r: (s // 4, s % 4, 0, 0)),
            ],
            out_specs=[
                fixed((count, 10 * f)),
                pl.BlockSpec((count, lane), lambda s, r: (0, column(s, r))),
                pl.BlockSpec((8, count, lane), lambda s, r: (0, 0, column(s, r))),
            ],
            scratch_shapes=[
                pltpu.VMEM((2, rows + count, 2 * f), jnp.bfloat16),
                pltpu.VMEM((2, rows + count, 2 * f), jnp.bfloat16),
            ],
        ),
        out_shape=[
            jax.ShapeDtypeStruct((count, 10 * f), f32),
            jax.ShapeDtypeStruct((count, 16 * f), f32),
            jax.ShapeDtypeStruct((8, count, 16 * f), f32),
        ],
        compiler_params=pltpu.CompilerParams(vmem_limit_bytes=67_043_328),
    )(half[None], z, lift, own, y, gx, dtn, bulk_all)
    return (first[None], second[None], merged[None])


def solution(mesh):
    def body(dtn, interface_perm):
        n = mesh.shape["row"]
        count = dtn.shape[2]
        if count % 8 == 0 and n == 1 << len(FIRST[0]):
            return fast_body(dtn, interface_perm)
        return plain_body(dtn, interface_perm)

    return jax.shard_map(
        body,
        mesh=mesh,
        in_specs=(P("box", None, "row", None), P("box", None)),
        out_specs=(P("box", "row", None), P("box", "row", None), P("box", None, "row", None)),
        check_vma=False,
    )
```

```python
import functools

import jax
import jax.numpy as jnp
from jax import lax
from jax.experimental import pallas as pl
from jax.experimental.pallas import tpu as pltpu
from jax.sharding import PartitionSpec as P

HIGHEST = lax.Precision.HIGHEST
HIGH = lax.Precision.HIGH
BLOCK = 128
GROUP = 4
MESH = pl.DeviceIdType.MESH


def dot(left, right, precision=HIGHEST):
    return jnp.dot(left, right, precision=precision, preferred_element_type=jnp.float32)


def dot_t(left, right):
    return lax.dot_general(
        left, right, (((0,), (0,)), ((), ())), precision=HIGHEST, preferred_element_type=jnp.float32
    )


def invert_step(blk, lane, g, carry):
    size = blk.shape[0]
    k = g * GROUP
    full = blk[...]
    cols = [
        jnp.take_along_axis(full, jnp.full((size, size), k + i, jnp.int32), axis=1)
        for i in range(GROUP)
    ]
    rows = [blk[pl.ds(k + i, 1), :] for i in range(GROUP)]
    wide = [jnp.broadcast_to(r, (8, size)) for r in rows]
    pivots = [
        [
            jnp.take_along_axis(wide[i], jnp.full((8, size), k + j, jnp.int32), axis=1)
            for j in range(GROUP)
        ]
        for i in range(GROUP)
    ]
    inside = (lane >= k) & (lane < k + GROUP)
    wide = [
        jnp.where(lane == k + i, 1.0, jnp.where(inside, 0.0, wide[i])) for i in range(GROUP)
    ]
    for i in range(GROUP):
        p = 1.0 / pivots[i][i]
        wide[i] = wide[i] * p
        for j in range(i + 1, GROUP):
            pivots[i][j] = pivots[i][j] * p
        for l in range(GROUP):
            if l != i:
                f = pivots[l][i]
                wide[l] = wide[l] - f * wide[i]
                for j in range(i + 1, GROUP):
                    pivots[l][j] = pivots[l][j] - f * pivots[i][j]
    result = jnp.where(inside, 0.0, full)
    for i in range(GROUP):
        result = result - cols[i] * wide[i][0:1]
    blk[...] = result
    for i in range(GROUP):
        blk[pl.ds(k + i, 1), :] = wide[i][0:1]
    return carry


def invert_block(blk):
    size = blk.shape[0]
    lane = lax.broadcasted_iota(jnp.int32, (1, size), 1)
    lax.fori_loop(0, size // GROUP, functools.partial(invert_step, blk, lane), 0)


def invert(mat, blk, col):
    order = mat.shape[0]
    count = order // BLOCK
    eye = (
        lax.broadcasted_iota(jnp.int32, (BLOCK, BLOCK), 0)
        == lax.broadcasted_iota(jnp.int32, (BLOCK, BLOCK), 1)
    ).astype(jnp.float32)

    def outer(j, carry):
        here = pl.ds(pl.multiple_of(j * BLOCK, BLOCK), BLOCK)
        blk[...] = mat[here, here]
        invert_block(blk)
        col[...] = mat[:, here]
        mat[:, here] = jnp.zeros((order, BLOCK), jnp.float32)
        mat[here, here] = eye
        col[here, :] = jnp.zeros((BLOCK, BLOCK), jnp.float32)
        mat[here, :] = dot(blk[...], mat[here, :])

        def inner(i, c):
            there = pl.ds(pl.multiple_of(i * BLOCK, BLOCK), BLOCK)
            mat[there, :] = mat[there, :] - dot(col[there, :], mat[here, :])
            return c

        @pl.loop(0, count)
        def _(i):
            @pl.when(i != j)
            def _():
                inner(i, 0)

        return carry

    lax.fori_loop(0, count, outer, 0)


def first_kernel(perm_ref, small_ref, inv_ref, coupled_ref, own_ref, mat, blk, col):
    f = mat.shape[0]
    count = f // BLOCK

    def block(ref, i):
        return ref[:, i * f : (i + 1) * f]

    def place(rows):
        return (
            perm_ref[rows, :] == lax.broadcasted_iota(jnp.int32, (BLOCK, f), 1)
        ).astype(jnp.float32)

    whole = (perm_ref[...] == lax.broadcasted_iota(jnp.int32, (f, f), 1)).astype(jnp.float32)

    @pl.loop(0, count)
    def _(i):
        here = pl.ds(pl.multiple_of(i * BLOCK, BLOCK), BLOCK)
        moved = dot(place(here), block(small_ref, 1))
        mat[here, :] = small_ref[here, :f] + lax.dot_general(
            moved,
            whole,
            (((1,), (1,)), ((), ())),
            precision=HIGHEST,
            preferred_element_type=jnp.float32,
        )

    invert(mat, blk, col)

    @pl.loop(0, count)
    def _(i):
        here = pl.ds(pl.multiple_of(i * BLOCK, BLOCK), BLOCK)
        inv_ref[here, :f] = mat[here, :]
        inv_ref[here, f:] = dot(mat[here, :], whole)

    @pl.loop(0, count)
    def _(i):
        there = pl.ds(pl.multiple_of(f + i * BLOCK, BLOCK), BLOCK)
        picked = (
            perm_ref[...] == lax.broadcasted_iota(jnp.int32, (f, BLOCK), 1) + i * BLOCK
        ).astype(jnp.float32)
        inv_ref[there, :] = dot_t(picked, inv_ref[:f, :])

    for h in range(2):

        @pl.loop(0, count)
        def _(i):
            here = pl.ds(pl.multiple_of(i * BLOCK, BLOCK), BLOCK)
            rows = pl.ds(pl.multiple_of(h * f + i * BLOCK, BLOCK), BLOCK)
            edge = small_ref[:, pl.ds(pl.multiple_of((2 + h) * f + i * BLOCK, BLOCK), BLOCK)]
            coupled_ref[rows, :] = -dot_t(edge, inv_ref[h * f : (h + 1) * f, :])
            for c in range(2):
                value = dot(coupled_ref[rows, c * f : (c + 1) * f], block(small_ref, 2 + c))
                if c == h:
                    value = value + small_ref[here, (4 + h) * f : (5 + h) * f]
                own_ref[rows, c * f : (c + 1) * f] = value


def second_kernel(own_ref, part_ref, lift_ref, pick_ref, out_ref, mat, blk, col):
    mat[...] = own_ref[...] + part_ref[...]
    invert(mat, blk, col)
    n = lift_ref.shape[0]
    out_ref[:n, :] = dot(lift_ref[...], mat[...])
    out_ref[n:, :] = dot(pick_ref[...], mat[...])


def flip(index, bit):
    return index + bit - 2 * bit * ((index // bit) % 2)


def plan(n, width):
    bits = []
    bit = n // 2
    while bit:
        bits.append(bit)
        bit //= 2
    tiles = width // 128
    first = tiles * 3 // 8
    second = tiles * 3 // 8 + (tiles * 3 % 8 >= 4)
    orders = [bits, bits[:-2] + [1, 2], [1, 2] + bits[:-2]]
    sizes = [first, second, tiles - first - second]
    chunks, at = [], 0
    for order, size in zip(orders, sizes):
        chunks.append((at * 128, size * 128, order))
        at += size
    return bits, chunks


def gather_kernel(n, bits, chunks, x_ref, out_ref, send_sem, recv_sem, own_sem):
    me = lax.axis_index("row")
    barrier = pltpu.get_barrier_semaphore()
    for bit in bits:
        pl.semaphore_signal(
            barrier, inc=1, device_id={"row": flip(me, bit)}, device_id_type=pl.DeviceIdType.MESH
        )
    local = pltpu.make_async_copy(x_ref, out_ref.at[me], own_sem)
    local.start()
    local.wait()
    pl.semaphore_wait(barrier, len(bits))
    pending = [[] for _ in chunks]
    sent = []
    held = [[()] for _ in chunks]
    for t in range(len(bits)):
        for c, (start, size, order) in enumerate(chunks):
            for copy in pending[c]:
                copy.wait_recv()
            pending[c] = []
            bit = order[t]
            for s in held[c]:
                slot = me
                for one in s:
                    slot = flip(slot, one)
                number = (1 << t) - 1 + len(pending[c])
                piece = out_ref.at[slot, :, pl.ds(start, size)]
                copy = pltpu.make_async_remote_copy(
                    src_ref=piece,
                    dst_ref=piece,
                    send_sem=send_sem.at[c, number],
                    recv_sem=recv_sem.at[c, number],
                    device_id={"row": flip(me, bit)},
                    device_id_type=pl.DeviceIdType.MESH,
                )
                copy.start()
                pending[c].append(copy)
                sent.append(copy)
            held[c] = held[c] + [s + (bit,) for s in held[c]]
    for c in range(len(chunks)):
        for copy in pending[c]:
            copy.wait_recv()
    for copy in sent:
        copy.wait_send()


def quick_gather(x):
    n = lax.axis_size("row")
    count, width = x.shape
    bits, chunks = plan(n, width)
    out = pl.pallas_call(
        functools.partial(gather_kernel, n, bits, chunks),
        out_shape=jax.ShapeDtypeStruct((n, count, width), jnp.float32),
        in_specs=[pl.BlockSpec(memory_space=pltpu.VMEM)],
        out_specs=pl.BlockSpec(memory_space=pltpu.VMEM),
        scratch_shapes=[
            pltpu.SemaphoreType.DMA((len(chunks), n - 1)),
            pltpu.SemaphoreType.DMA((len(chunks), n - 1)),
            pltpu.SemaphoreType.DMA,
        ],
        compiler_params=pltpu.CompilerParams(
            collective_id=0, has_side_effects=True, vmem_limit_bytes=16 * 1024 * 1024
        ),
        cost_estimate=pl.CostEstimate(
            flops=10_000_000_000, bytes_accessed=2 * n * count * width * 4, transcendentals=0
        ),
    )(x)
    return out.reshape(n * count, width)


def call(kernel, out, order, *args):
    return pl.pallas_call(
        kernel,
        out_shape=[jax.ShapeDtypeStruct(o, jnp.float32) for o in out],
        in_specs=[pl.BlockSpec(memory_space=pltpu.VMEM)] * len(args),
        out_specs=[pl.BlockSpec(memory_space=pltpu.VMEM)] * len(out),
        scratch_shapes=[
            pltpu.VMEM((order, order), jnp.float32),
            pltpu.VMEM((BLOCK, BLOCK), jnp.float32),
            pltpu.VMEM((order, BLOCK), jnp.float32),
        ],
        compiler_params=pltpu.CompilerParams(vmem_limit_bytes=40 * 1024 * 1024),
        cost_estimate=pl.CostEstimate(
            flops=order * 20_000_000, bytes_accessed=order * order * 8, transcendentals=0
        ),
    )(*args)


def plain_body(dtn, interface_perm):
    a, b = dtn[0], dtn[1]
    count = a.shape[1]
    f = a.shape[2] // 6
    perm = interface_perm[0]
    rank = lax.axis_index("row")
    half = lax.axis_index("box") % 2
    first = half == 0

    def swap(x):
        n = lax.axis_size("box")
        return lax.ppermute(x, "box", [(i, i ^ 1) for i in range(n)])

    def gather(x):
        return lax.all_gather(x, "row", axis=0, tiled=True)

    def cols(x, face):
        return x[..., face * f : (face + 1) * f]

    def side(x):
        return jnp.where(first, cols(x, 3), cols(x, 2))

    def free(x):
        return jnp.where(first, cols(x, 2), cols(x, 3))

    def outer_cols(x, edge):
        return jnp.concatenate([cols(x, edge), free(x), cols(x, 4), cols(x, 5)], axis=-1)

    ay, by = jnp.where(first, a[3], a[2]), jnp.where(first, b[3], b[2])
    a1, b0 = a[1], b[0]
    small = quick_gather(
        jnp.concatenate(
            [cols(a1, 1), cols(b0, 0), side(a1), side(b0), side(ay), side(by)], axis=1
        )
    )
    bulk = gather(
        jnp.concatenate(
            [outer_cols(a1, 0), outer_cols(ay, 0), outer_cols(b0, 1), outer_cols(by, 1)], axis=1
        )
    )
    inv1, coupled, own_ss = call(first_kernel, [(2 * f, 2 * f)] * 3, f, perm[:, None], small)
    a1y, b0y = small[:, 2 * f : 3 * f], small[:, 3 * f : 4 * f]

    def times_side(x):
        return jnp.concatenate([dot(x[:, :f], a1y), dot(x[:, f:], b0y)], axis=1)

    part_ss = swap(own_ss)
    outer_a = jnp.concatenate(
        [a[0], jnp.where(first, a[2], a[3]), a[4], a[5]], axis=0
    )
    outer_b = jnp.concatenate(
        [b[1], jnp.where(first, b[2], b[3]), b[4], b[5]], axis=0
    )
    lift = -jnp.concatenate(
        [dot(cols(outer_a, 1), inv1[:f]), dot(cols(outer_b, 0), inv1[f:])], axis=0
    )
    n = 4 * count
    zero_n = jnp.zeros((n, f), jnp.float32)
    lift_two = times_side(lift) + jnp.concatenate(
        [
            jnp.concatenate([side(outer_a), zero_n], axis=1),
            jnp.concatenate([zero_n, side(outer_b)], axis=1),
        ],
        axis=0,
    )
    start = rank * count
    pick = (
        jnp.arange(2 * f, dtype=jnp.int32)[None, :]
        == half * f + start + jnp.arange(count, dtype=jnp.int32)[:, None]
    ).astype(jnp.float32)
    own_rows = lax.dynamic_slice(inv1, (start, 0), (count, 2 * f))
    z = -call(second_kernel, [(2 * n + count, 2 * f)], 2 * f, own_ss, part_ss, lift_two, pick)[0]
    z_part = swap(z)
    both = jnp.concatenate([z_part, z], axis=0)
    through = dot(both, coupled)
    m = 2 * n + count
    through = jnp.concatenate(
        [through[:m], through[m : m + 2 * n] + lift, through[m + 2 * n :], -own_rows], axis=0
    )
    both = jnp.concatenate([both, jnp.zeros((count, 2 * f), jnp.float32)], axis=0)
    w = 4 * f
    res_a = dot(through[:, :f], bulk[:, :w], HIGH) + dot(both[:, :f], bulk[:, w : 2 * w], HIGH)
    res_b = dot(through[:, f:], bulk[:, 2 * w : 3 * w], HIGH) + dot(both[:, f:], bulk[:, 3 * w :], HIGH)
    results = jnp.concatenate([res_a, res_b], axis=1)
    cross = swap(results[:m])
    own = results[m : 2 * m]
    base = jnp.concatenate(
        [
            jnp.concatenate([outer_cols(outer_a, 0), jnp.zeros((n, w), jnp.float32)], axis=1),
            jnp.concatenate([jnp.zeros((n, w), jnp.float32), outer_cols(outer_b, 1)], axis=1),
        ],
        axis=0,
    )
    own_map = own[: 2 * n] + base
    left = jnp.where(first, own_map, cross[: 2 * n])
    right = jnp.where(first, cross[: 2 * n], own_map)
    merged_map = jnp.concatenate([left, right], axis=1).reshape(1, 8, count, 4 * w)
    own_s, cross_s = own[2 * n :], cross[2 * n :]
    second = jnp.concatenate(
        [jnp.where(first, own_s, cross_s), jnp.where(first, cross_s, own_s)], axis=1
    )
    s1 = results[2 * m :]
    y_a, y_b = -dot(own_rows[:, :f], a1y), -dot(own_rows[:, f:], b0y)

    def ordered(x, y):
        two = jnp.where(first, cols(x, 1), y)
        three = jnp.where(first, y, cols(x, 1))
        return [cols(x, 0), two, three, x[:, 2 * f :]]

    solution_first = jnp.concatenate(ordered(s1[:, :w], y_a) + ordered(s1[:, w:], y_b), axis=1)
    return (solution_first[None], second[None], merged_map)


def split3(x):
    high = x.astype(jnp.bfloat16)
    rest = x - high.astype(jnp.float32)
    mid = rest.astype(jnp.bfloat16)
    low = (rest - mid.astype(jnp.float32)).astype(jnp.bfloat16)
    return high, mid, low


def dims(left, right):
    return (((left,), (right,)), ((), ()))


def bdot(left, right, dn):
    return lax.dot_general(left, right, dn, preferred_element_type=jnp.float32)


def pick_left(onehot, x, contract=1):
    return sum(bdot(onehot, part, dims(contract, 0)) for part in split3(x))


def pick_right(x, onehot, contract=0):
    return sum(bdot(part, onehot, dims(1, contract)) for part in split3(x))


def xdot(left, right, dn):
    return lax.dot_general(left, right, dn, precision=HIGHEST, preferred_element_type=jnp.float32)


def split2(x):
    high = x.astype(jnp.bfloat16)
    low = (x - high.astype(jnp.float32)).astype(jnp.bfloat16)
    return high, low


def dot3(left, right, dn):
    a, b = left
    c, d = right
    return bdot(a, c, dn) + (bdot(a, d, dn) + bdot(b, c, dn))


NN = dims(1, 0)
NT = dims(1, 1)
TN = dims(0, 0)


FIRST = ['xyba', 'byax', 'baxy', 'byxa', 'abyx', 'bxay']
FIRST_EVENTS = [(0, 0), (1, 0), (4, 0), (2, 0), (3, 0), (0, 1), (5, 0), (1, 1), (4, 1), (2, 1), (3, 1), (5, 1), (0, 2), (4, 2), (2, 2), (1, 2), (3, 2), (5, 2), (4, 3), (0, 3), (2, 3), (1, 3), (3, 3), (5, 3)]
REST = ['byxa', 'abyx', 'baxy', 'bayx', 'abxy', 'baxy']
BULK = [((0, 1), 'ybxa'), ((1, 2), 'baxy'), ((2, 3), 'bayx'), ((3, 4), 'baxy'), ((4, 6), 'byax'), ((6, 8), 'bxay'), ((8, 10), 'bxya'), ((10, 12), 'abxy'), ((12, 14), 'bayx'), ((14, 16), 'ybxa')]
BULK_START = 3
EVENTS = [(1, 0, 0), (1, 1, 0), (1, 2, 0), (1, 4, 0), (2, 3, 0), (3, 5, 0), (3, 0, 1), (4, 2, 1), (4, 1, 1), (4, 6, 0), (5, 3, 1), (5, 4, 1), (5, 0, 2), (5, 15, 0), (6, 5, 1), (7, 7, 0), (7, 1, 2), (7, 2, 2), (8, 8, 0), (8, 13, 0), (8, 3, 2), (8, 4, 2), (8, 9, 0), (9, 5, 2), (10, 10, 0), (11, 2, 3), (12, 1, 3), (12, 11, 0), (12, 0, 3), (13, 4, 3), (13, 12, 0), (13, 3, 3), (13, 7, 1), (14, 5, 3), (14, 14, 0), (14, 11, 1), (14, 8, 1), (15, 10, 1), (15, 6, 1), (15, 7, 2), (15, 9, 1), (15, 8, 2), (16, 12, 1), (18, 15, 1), (19, 6, 2), (20, 7, 3), (22, 13, 1), (22, 11, 2), (22, 8, 3), (23, 14, 1), (24, 9, 2), (24, 12, 2), (27, 10, 2), (27, 15, 2), (31, 6, 3), (31, 11, 3), (31, 13, 2), (35, 14, 2), (38, 12, 3), (38, 9, 3), (38, 10, 3), (41, 15, 3), (41, 13, 3), (41, 14, 3)]


def inv2(a, b, c):
    ra = 1.0 / a
    t = b * ra
    rs = 1.0 / (c - b * t)
    u = t * rs
    return ra + t * u, -u, rs


def inv4(d):
    a0, a1, a2 = inv2(d[0][0], d[0][1], d[1][1])
    t = [
        [a0 * d[0][2] + a1 * d[1][2], a0 * d[0][3] + a1 * d[1][3]],
        [a1 * d[0][2] + a2 * d[1][2], a1 * d[0][3] + a2 * d[1][3]],
    ]
    s0, s1, s2 = inv2(
        d[2][2] - (d[0][2] * t[0][0] + d[1][2] * t[1][0]),
        d[2][3] - (d[0][2] * t[0][1] + d[1][2] * t[1][1]),
        d[3][3] - (d[0][3] * t[0][1] + d[1][3] * t[1][1]),
    )
    u = [[t[i][0] * s0 + t[i][1] * s1, t[i][0] * s1 + t[i][1] * s2] for i in range(2)]
    e00 = a0 + (u[0][0] * t[0][0] + u[0][1] * t[0][1])
    e01 = a1 + (u[0][0] * t[1][0] + u[0][1] * t[1][1])
    e11 = a2 + (u[1][0] * t[1][0] + u[1][1] * t[1][1])
    return [
        [e00, e01, -u[0][0], -u[0][1]],
        [e01, e11, -u[1][0], -u[1][1]],
        [-u[0][0], -u[1][0], s0, s1],
        [-u[0][1], -u[1][1], s1, s2],
    ]


def spread(x, lane_index):
    return jnp.take_along_axis(x, jnp.full(x.shape, lane_index, jnp.int32), axis=1)


def row(x, i):
    return jnp.broadcast_to(x[i : i + 1], x.shape)


def weigh(weights, values):
    return (weights[0] * values[0] + weights[1] * values[1]) + (weights[2] * values[2] + weights[3] * values[3])


def diag(tile, first, sub):
    e = [spread(tile, first + j) for j in range(4)]
    return [[row(e[j], sub + i) if j >= i else None for j in range(4)] for i in range(4)]


def flat(d):
    return tuple(d[i][j] for i in range(4) for j in range(i, 4))


def unflat(c):
    it = iter(c)
    d = [[None] * 4 for _ in range(4)]
    for i in range(4):
        for j in range(i, 4):
            d[i][j] = next(it)
    return d


def pivot_step(blk, lane, k, sub, d):
    size = blk.shape[0]
    inside = (lane >= k) & (lane < k + 4)
    start = pl.multiple_of(jnp.minimum(k + 4 - (4 - sub) % 8, size - 8), 8)
    skip = (sub + 4) % 8
    g = inv4(d)
    own = blk[pl.ds(pl.multiple_of(k - sub, 8), 8), :]
    near = own if sub == 0 else blk[pl.ds(start, 8), :]
    rows = [jnp.where(lane == k + i, 1.0, jnp.where(inside, 0.0, row(own, sub + i))) for i in range(4)]
    w = [weigh(g[i], rows) for i in range(4)]
    nearc = [spread(near, k + i) for i in range(4)]
    new = jnp.where(inside, 0.0, near) - weigh(nearc, w)
    nd = diag(new, lax.rem(k + 4, size), skip)
    full = blk[...]
    wide = jnp.broadcast_to(inside[0:1], full.shape)
    cols = [jnp.take_along_axis(full, jnp.full(full.shape, k + i, jnp.int32), axis=1) for i in range(4)]
    result = jnp.where(wide, 0.0, full)
    for i in range(4):
        result = result - cols[i] * w[i][0:1]
    blk[...] = result
    for i in range(4):
        blk[pl.ds(k + i, 1), :] = w[i][0:1]
    return nd


def pivots_begin(blk):
    return flat(diag(blk[0:8, :], 0, 0))


def pivots_run(blk, start, stop, carry):
    lane = lax.broadcasted_iota(jnp.int32, (8, blk.shape[1]), 1)
    def body(t, c):
        d = pivot_step(blk, lane, 8 * t, 0, unflat(c))
        d = pivot_step(blk, lane, 8 * t + 4, 4, d)
        return flat(d)
    return lax.fori_loop(start, stop, body, carry)


def invert_small(mat, blk, col, tick):
    order = mat.shape[0]
    count = order // BLOCK
    eye = (
        lax.broadcasted_iota(jnp.int32, (BLOCK, BLOCK), 0)
        == lax.broadcasted_iota(jnp.int32, (BLOCK, BLOCK), 1)
    ).astype(jnp.float32)
    for j in range(count):
        here = pl.ds(j * BLOCK, BLOCK)
        blk[...] = mat[here, here]
        carry = pivots_begin(blk)
        total = BLOCK // 8
        for part in range(4):
            carry = pivots_run(blk, part * total // 4, (part + 1) * total // 4, carry)
            if part < 3:
                tick()
        col[...] = mat[:, here]
        mat[:, here] = jnp.zeros((order, BLOCK), jnp.float32)
        mat[here, here] = eye
        mat[here, :] = xdot(blk[...], mat[here, :], NN)
        for i in range(count):
            if i != j:
                there = pl.ds(i * BLOCK, BLOCK)
                mat[there, :] = mat[there, :] - xdot(col[there, :], mat[here, :], NN)
        tick()


class Gather:
    def __init__(self, ref, lead, block, cols, order, me, n, sends, recvs):
        self.ref, self.lead, self.block, self.cols, self.order = ref, lead, block, cols, order
        self.me, self.n, self.sends, self.recvs = me, n, sends, recvs

    def view(self, stage, arrived):
        m = self.n.bit_length() - 1
        index = []
        for b in range(m - 1, -1, -1):
            bit = 1 << b
            own = (self.me // bit) % 2
            if bit in self.order[:stage]:
                index.append(slice(None))
            elif arrived and bit == self.order[stage]:
                index.append(1 - own)
            else:
                index.append(own)
        blocks = pl.ds(self.block[0], self.block[1] - self.block[0])
        cols = pl.ds(self.cols[0], self.cols[1] - self.cols[0])
        return self.ref.at[(*self.lead, blocks, *index, slice(None), cols)]

    def copy(self, stage):
        piece = self.view(stage, False)
        return pltpu.make_async_remote_copy(
            src_ref=piece,
            dst_ref=piece,
            send_sem=self.sends.at[stage],
            recv_sem=self.recvs.at[stage],
            device_id={"row": flip(self.me, self.order[stage])},
            device_id_type=MESH,
        )


def merge_kernel(
    plan, perm_ref, dtn_any, high_ref, low_ref, y_ref, gx_ref, bulk_ref,
    small, mat1, mat2, mat3, tee, blk, col, edge, ss, part, rhs, hold, dtn_ref, z_ref, lift_ref, own_ref,
    fill_sem, send0, recv0, send1, recv1, send2, recv2, core_send, core_recv, swap_send, swap_recv,
):
    n, f, count = plan["n"], plan["f"], plan["count"]
    bits = plan["bits"]
    me = lax.axis_index("row")
    pair = lax.axis_index("box")
    half = lax.rem(pair, 2)
    other = pair + 1 - 2 * half
    yface, free = 3 - half, 2 + half
    spot = [(me // bit) % 2 for bit in bits]

    def at(face):
        return pl.ds(face * f, f) if isinstance(face, int) else pl.ds(pl.multiple_of(face * f, BLOCK), f)

    narrow = [(0, 1, 1), (1, 0, 0), (0, 1, yface), (1, 0, yface), (0, yface, yface), (1, yface, yface)]
    outer = [(0, free, 4, 5), (1, free, 4, 5)]
    wide = [(h, r, c) for h in range(2) for c in outer[h] for r in (1 - h, yface)]
    fills = []
    for b, (h, r, c) in enumerate(narrow):
        fills.append(
            pltpu.make_async_copy(dtn_any.at[h, r, :, at(c)], small.at[(b, *spot)], fill_sem.at[b])
        )
    for b, (h, r, c) in enumerate(wide):
        fills.append(
            pltpu.make_async_copy(
                dtn_ref.at[h, r, :, at(c)], bulk_ref.at[(0, b, *spot)], fill_sem.at[len(narrow) + b]
            )
        )
    load = pltpu.make_async_copy(dtn_any, dtn_ref, fill_sem.at[len(narrow) + len(wide)])
    for one in fills[: len(narrow)]:
        one.start()
    load.start()

    barrier = pltpu.get_barrier_semaphore()
    for bit in bits:
        pl.semaphore_signal(barrier, inc=1, device_id={"row": flip(me, bit)}, device_id_type=MESH)
    pl.semaphore_signal(barrier, inc=1, device_id={"box": other}, device_id_type=MESH)
    pl.semaphore_wait(barrier, len(bits) + 1)

    def gathers(ref, lead, chunks, sends, recvs):
        return [
            Gather(ref, lead, block, cols, order, me, n, sends.at[i], recvs.at[i])
            for i, (block, cols, order) in enumerate(chunks)
        ]

    first = gathers(small, (), plan["first"], send0, recv0)
    rest = gathers(small, (), plan["rest"], send1, recv1)
    bulk = gathers(bulk_ref, (0,), plan["bulk"], send2, recv2)
    last = len(bits)

    def cross(i, stage):
        g = bulk[i]
        view = g.view(0, False) if stage < 0 else g.view(stage, True)
        there = Gather(bulk_ref, (1,), g.block, g.cols, g.order, me, n, None, None)
        target = there.view(0, False) if stage < 0 else there.view(stage, True)
        return pltpu.make_async_remote_copy(
            src_ref=view,
            dst_ref=target,
            send_sem=core_send.at[i, stage + 1],
            recv_sem=core_recv.at[i, stage + 1],
            device_id={"box": other},
            device_id_type=MESH,
        )

    def advance(group, i, stage):
        g = group[i]
        if stage > 0:
            g.copy(stage - 1).wait_recv()
        if stage < last:
            g.copy(stage).start()
        if group is bulk:
            cross(i, stage - 1).start()

    events = list(plan["events"])
    groups = {"first": first, "rest": rest, "bulk": bulk}

    def tick():
        if events:
            for name, i, stage in events.pop(0):
                advance(groups[name], i, stage)

    for one in fills[: len(narrow)]:
        one.wait()
    for i in range(len(first)):
        advance(first, i, 0)
    for i, stage in plan["first_events"]:
        advance(first, i, stage + 1)
        if (i, stage) == plan["first_events"][-len(first)]:
            for k in range(len(rest)):
                advance(rest, k, 0)
    load.wait()
    for one in fills[len(narrow) :]:
        one.start()
    for one in fills[len(narrow) :]:
        one.wait()

    def block(b):
        return small[b].reshape(f, f)

    count_f = f // BLOCK
    whole = (perm_ref[...] == lax.broadcasted_iota(jnp.int32, (f, f), 0)).astype(jnp.bfloat16)
    hold[...] = pick_left(whole, block(1), 0)
    mat1[...] = block(0) + pick_right(hold[...], whole)
    tick()
    invert_small(mat1, blk, col, tick)

    edge[:, :f] = block(2)
    edge[:, f:] = pick_left(whole, block(3), 0)

    def rows_of(i):
        return pl.ds(pl.multiple_of(i * BLOCK, BLOCK), BLOCK)

    @pl.loop(0, count_f)
    def _(i):
        gx_ref[0, 0, rows_of(i), :] = xdot(mat1[rows_of(i), :], edge[...], NN)

    tick()

    def swap(b):
        return pltpu.make_async_remote_copy(
            src_ref=ss.at[b],
            dst_ref=part.at[b],
            send_sem=swap_send.at[b],
            recv_sem=swap_recv.at[b],
            device_id={"box": other},
            device_id_type=MESH,
        )

    for b, (i, j) in enumerate([(0, 0), (0, 1), (1, 1)]):

        @pl.loop(0, count_f)
        def _(k):
            left = edge[:, pl.ds(pl.multiple_of(i * f + k * BLOCK, BLOCK), BLOCK)]
            value = -xdot(left, gx_ref[0, 0, :, j * f : (j + 1) * f], TN)
            ss[b, rows_of(k), :] = value

    tick()
    ss[0] = ss[0] + block(4)
    swap(1).start()
    ss[2] = ss[2] + block(5)
    swap(0).start()

    outers = []
    for h in range(2):
        outers.append(
            jnp.concatenate([dtn_ref[h, r, :, pl.ds((1 - h) * f, f)] for r in outer[h]], axis=0)
        )
    swap(2).start()
    m = 4 * count
    joined = jnp.concatenate([outers[0], pick_right(outers[1], whole)], axis=0)
    value = -xdot(joined, mat1[...], NN)
    lift_ref[:, :f] = value
    lift_ref[:, f:] = pick_right(value, whole, 1)
    own_at = pl.ds(pl.multiple_of(me * count, 8), count)
    mine = mat1[own_at, :]
    own_ref[:, :f] = -mine
    own_ref[:, f:] = -pick_right(mine, whole, 1)
    y_ref[...] = -gx_ref[0, 0, own_at, :]
    rhs[: 2 * m, :] = -xdot(joined, gx_ref[0, 0], NN)
    for h in range(2):
        side = jnp.concatenate([dtn_ref[h, r, :, at(yface)] for r in outer[h]], axis=0)
        rhs[h * m : (h + 1) * m, h * f : (h + 1) * f] += side
    rhs[2 * m :, :] = (
        lax.broadcasted_iota(jnp.int32, (count, 2 * f), 1)
        == half * f + me * count + lax.broadcasted_iota(jnp.int32, (count, 2 * f), 0)
    ).astype(jnp.float32)

    @pl.loop(0, count_f)
    def _(i):
        picked = (
            perm_ref[...] == lax.broadcasted_iota(jnp.int32, (BLOCK, f), 0) + i * BLOCK
        ).astype(jnp.bfloat16)
        gx_ref[0, 1, rows_of(i), :] = pick_left(picked, gx_ref[0, 0])

    tick()
    swap(0).wait_recv()
    mat2[...] = ss[0] + part[0]
    invert_small(mat2, blk, col, tick)
    gx_copy = pltpu.make_async_remote_copy(
        src_ref=gx_ref.at[0],
        dst_ref=gx_ref.at[1],
        send_sem=swap_send.at[3],
        recv_sem=swap_recv.at[3],
        device_id={"box": other},
        device_id_type=MESH,
    )
    gx_copy.start()
    swap(1).wait_recv()
    hold[...] = ss[1] + part[1]

    @pl.loop(0, count_f)
    def _(i):
        tee[rows_of(i), :] = xdot(mat2[rows_of(i), :], hold[...], NN)

    swap(2).wait_recv()

    @pl.loop(0, count_f)
    def _(i):
        mat3[rows_of(i), :] = (
            ss[2, rows_of(i), :]
            + part[2, rows_of(i), :]
            - xdot(hold[:, rows_of(i)], tee[...], TN)
        )

    tick()
    invert_small(mat3, blk, col, tick)
    left = rhs[:, :f]
    second = xdot(xdot(left, tee[...], NN) - rhs[:, f:], mat3[...], NN)
    z_ref[:, f:] = second
    z_ref[:, :f] = -xdot(left, mat2[...], NN) - xdot(second, tee[...], NT)
    left_over = [event for some in events for event in some]
    early = [event for event in left_over if event[2] < last]
    late = [event for event in left_over if event[2] == last]
    cut = len(late) // 2

    def finish(some):
        for name, i, stage in some:
            advance(groups[name], i, stage)

    def left_factors(q):
        zs = split2(z_ref[...])
        for k in range(2):
            here = slice(k * f, (k + 1) * f)
            value = -dot3(zs, split2(gx_ref[q, k]), NT)
            if q == 0:
                value = jnp.concatenate([value[: 2 * m] + lift_ref[:, here], value[2 * m :]], axis=0)
            high_ref[q, k, :, :f], low_ref[q, k, :, :f] = split2(
                jnp.concatenate([value, own_ref[:, here]], axis=0)
            )
            high_ref[q, k, :, f:], low_ref[q, k, :, f:] = split2(
                jnp.concatenate([z_ref[:, here], jnp.zeros((count, f), jnp.float32)], axis=0)
            )

    finish(early)
    left_factors(0)
    finish(late[:cut])
    gx_copy.wait_recv()
    left_factors(1)
    finish(late[cut:])
    for b in range(3):
        swap(b).wait_send()
    gx_copy.wait_send()
    for group in (first, rest, bulk):
        for g in group:
            for stage in range(last):
                g.copy(stage).wait_send()
    for i in range(len(bulk)):
        for stage in range(-1, last):
            cross(i, stage).wait()


def product_kernel(
    half_ref, high_ref, low_ref, y_ref, dtn_ref, wide_ref, first_ref, second_ref, map_ref,
):
    step = pl.program_id(0)
    q, h, c = step // 4, (step // 2) % 2, 2 * (step % 2)
    half = half_ref[0]
    count, f = y_ref.shape[0], y_ref.shape[1] // 2
    m = 4 * count
    rows = 9 * count

    @pl.when(step == 0)
    def _():
        for k in range(2):
            at = pl.multiple_of((5 * k + 2 - half) * f, BLOCK)
            first_ref[:, pl.ds(at, f)] = y_ref[:, k * f : (k + 1) * f]

    def columns(k):
        return wide_ref[0, 2 * k : 2 * k + 2].reshape(2 * f, f)

    right = split2(jnp.concatenate([columns(0), columns(1)], axis=1))
    res = dot3((high_ref[0, h], low_ref[0, h]), right, NN)
    map_ref[...] = res[: 2 * m].reshape(map_ref.shape)
    second_ref[...] = res[2 * m : rows]

    @pl.when(q == 0)
    def _():
        for k in range(2):
            place = c + k
            here = slice(k * f, (k + 1) * f)
            where = 5 * h + jnp.where(place == 0, 0, jnp.where(place == 1, 1 + half, place + 1))
            first_ref[:, pl.ds(pl.multiple_of(where * f, BLOCK), f)] = res[rows:, here]
            face = jnp.where(place == 0, h, jnp.where(place == 1, 2 + half, place + 2))
            cols = pl.ds(pl.multiple_of(face * f, BLOCK), f)
            for i, r in enumerate((h, 2 + half, 4, 5)):
                map_ref[4 * h + i, :, here] += dtn_ref[h, r, :, cols]


def fast_body(dtn, interface_perm):
    _, faces, count, width = dtn.shape
    f = width // faces
    n = lax.axis_size("row")
    bits = []
    bit = n // 2
    while bit:
        bits.append(bit)
        bit //= 2
    last = len(bits)
    tiles = f // BLOCK
    cuts = [(BLOCK * (tiles * i // 3), BLOCK * (tiles * (i + 1) // 3)) for i in range(3)]
    named = dict(zip("bayx", bits))

    def order(letters):
        return [named[one] for one in letters]

    six = [((a, a + 1), cut) for a in range(2) for cut in cuts]
    rest_parts = [((a, a + 2), cut) for a in (2, 4) for cut in cuts]
    events = [[] for _ in range(1 + max(k for k, _, _ in EVENTS))]
    events[BULK_START] = [("bulk", i, 0) for i in range(len(BULK))]
    for k, i, stage in EVENTS:
        if i < len(REST):
            events[k].append(("rest", i, stage + 1))
        else:
            events[k].append(("bulk", i - len(REST), stage + 1))
    nb = len(BULK)
    plan = {
        "n": n,
        "f": f,
        "count": count,
        "bits": bits,
        "first": [(*part, order(o)) for part, o in zip(six, FIRST)],
        "first_events": FIRST_EVENTS,
        "rest": [(*part, order(o)) for part, o in zip(rest_parts, REST)],
        "bulk": [(blocks, (0, f), order(o)) for blocks, o in BULK],
        "events": events,
    }
    split = (2,) * last
    vmem = pl.BlockSpec(memory_space=pltpu.VMEM)
    dma = pltpu.SemaphoreType.DMA
    rows = 9 * count
    f32 = jnp.float32
    high, low, y, _, bulk_all = pl.pallas_call(
        functools.partial(merge_kernel, plan),
        out_shape=[
            jax.ShapeDtypeStruct(s, kind)
            for s, kind in (
                ((2, 2, rows + count, 2 * f), jnp.bfloat16),
                ((2, 2, rows + count, 2 * f), jnp.bfloat16),
                ((count, 2 * f), f32),
                ((2, 2, f, 2 * f), f32),
                ((2, 16, *split, count, f), f32),
            )
        ],
        in_specs=[vmem, pl.BlockSpec(memory_space=pl.ANY)],
        out_specs=[vmem] * 4 + [pl.BlockSpec(memory_space=pl.ANY)],
        scratch_shapes=[
            pltpu.VMEM((6, *split, count, f), f32),
            pltpu.VMEM((f, f), f32),
            pltpu.VMEM((f, f), f32),
            pltpu.VMEM((f, f), f32),
            pltpu.VMEM((f, f), f32),
            pltpu.VMEM((BLOCK, BLOCK), f32),
            pltpu.VMEM((f, BLOCK), f32),
            pltpu.VMEM((f, 2 * f), f32),
            pltpu.VMEM((3, f, f), f32),
            pltpu.VMEM((3, f, f), f32),
            pltpu.VMEM((rows, 2 * f), f32),
            pltpu.VMEM((f, f), f32),
            pltpu.VMEM(dtn.shape, f32),
            pltpu.VMEM((rows, 2 * f), f32),
            pltpu.VMEM((8 * count, 2 * f), f32),
            pltpu.VMEM((count, 2 * f), f32),
            dma((23,)),
            dma((6, last)),
            dma((6, last)),
            dma((6, last)),
            dma((6, last)),
            dma((nb, last)),
            dma((nb, last)),
            dma((nb, last + 1)),
            dma((nb, last + 1)),
            dma((4,)),
            dma((4,)),
        ],
        compiler_params=pltpu.CompilerParams(
            collective_id=0, has_side_effects=True, vmem_limit_bytes=67_043_328
        ),
    )(interface_perm, dtn)
    bulk_all = bulk_all.reshape(2, 16, f, f)
    half = (lax.axis_index("box") % 2).astype(jnp.int32)
    lane = 2 * f

    def fixed(shape):
        return pl.BlockSpec(shape, lambda s, r: (0,) * len(shape))

    def column(s, r):
        own_half = r[0]
        return jnp.where(s < 4, own_half, 1 - own_half) * 4 + s % 4

    first, second, merged = pl.pallas_call(
        product_kernel,
        grid_spec=pltpu.PrefetchScalarGridSpec(
            num_scalar_prefetch=1,
            grid=(8,),
            in_specs=[
                pl.BlockSpec((1, 2, rows + count, lane), lambda s, r: (s // 4, 0, 0, 0)),
                pl.BlockSpec((1, 2, rows + count, lane), lambda s, r: (s // 4, 0, 0, 0)),
                fixed((count, lane)),
                fixed(dtn.shape),
                pl.BlockSpec((1, 4, f, f), lambda s, r: (s // 4, s % 4, 0, 0)),
            ],
            out_specs=[
                fixed((count, 10 * f)),
                pl.BlockSpec((count, lane), lambda s, r: (0, column(s, r))),
                pl.BlockSpec((8, count, lane), lambda s, r: (0, 0, column(s, r))),
            ],
        ),
        out_shape=[
            jax.ShapeDtypeStruct((count, 10 * f), f32),
            jax.ShapeDtypeStruct((count, 16 * f), f32),
            jax.ShapeDtypeStruct((8, count, 16 * f), f32),
        ],
        compiler_params=pltpu.CompilerParams(vmem_limit_bytes=67_043_328),
    )(half[None], high, low, y, dtn, bulk_all)
    return (first[None], second[None], merged[None])


def solution(mesh):
    def body(dtn, interface_perm):
        n = mesh.shape["row"]
        count = dtn.shape[2]
        if count % 8 == 0 and n == 1 << len(FIRST[0]):
            return fast_body(dtn, interface_perm)
        return plain_body(dtn, interface_perm)

    return jax.shard_map(
        body,
        mesh=mesh,
        in_specs=(P("box", None, "row", None), P("box", None)),
        out_specs=(P("box", "row", None), P("box", "row", None), P("box", None, "row", None)),
        check_vma=False,
    )
```
